32 devices in a mesh: dp: 8 (over z, x), seq: 4 (over y, core).
Axes of the slice: x: 2, y: 2, z: 4, core: 2. Of those that a mesh axis runs over, the one named last changes fastest.
Arguments:
- tokens: bfloat16 [16, 512, 1024], P('dp', 'seq'), may hold values from -6 to 6
- cotangent: bfloat16 [16, 512, 1024], P('dp', 'seq'), may hold values from -6 to 6
- item_count: int32 [8], P('dp'), may hold values from 1 to 2, as said below
- valid_len: int32 [16], P('dp'), may hold values from 256 to 512, as said below
- w_qkv: bfloat16 [1024, 3072], P(('dp', 'seq')), may hold values from -0.25 to 0.25
- q_bias: bfloat16 [1024], P(('dp', 'seq')), may hold values from -1.796875 to 1.796875
- v_bias: bfloat16 [1024], P(('dp', 'seq')), may hold values from -1.796875 to 1.796875
- w_out: bfloat16 [1024, 1024], P(('dp', 'seq')), may hold values from -0.75 to 0.75
- out_bias: bfloat16 [1024], P(('dp', 'seq')), may hold values from -1.796875 to 1.796875
- w_up: bfloat16 [1024, 4096], P(('dp', 'seq')), may hold values from -0.1875 to 0.1875
- up_bias: bfloat16 [4096], P(('dp', 'seq')), may hold values from -1.796875 to 1.796875
- w_down: bfloat16 [4096, 1024], P(('dp', 'seq')), may hold values from -0.125 to 0.125
- down_bias: bfloat16 [1024], P(('dp', 'seq')), may hold values from -1.796875 to 1.796875
- gain_one: bfloat16 [1024], P(('dp', 'seq')), may hold values from 0.25 to 1.75
- shift_one: bfloat16 [1024], P(('dp', 'seq')), may hold values from -1.796875 to 1.796875
- gain_two: bfloat16 [1024], P(('dp', 'seq')), may hold values from 0.25 to 1.75
- shift_two: bfloat16 [1024], P(('dp', 'seq')), may hold values from -1.796875 to 1.796875
Outputs:
- block_out: float32 [16, 512, 1024], P('dp', 'seq')
- grad_tokens: float32 [16, 512, 1024], P('dp', 'seq')
- grad_w_qkv: float32 [1024, 3072], P(('dp', 'seq'))
- grad_q_bias: float32 [1024], P(('dp', 'seq'))
- grad_v_bias: float32 [1024], P(('dp', 'seq'))
- grad_w_out: float32 [1024, 1024], P(('dp', 'seq'))
- grad_out_bias: float32 [1024], P(('dp', 'seq'))
- grad_w_up: float32 [1024, 4096], P(('dp', 'seq'))
- grad_up_bias: float32 [4096], P(('dp', 'seq'))
- grad_w_down: float32 [4096, 1024], P(('dp', 'seq'))
- grad_down_bias: float32 [1024], P(('dp', 'seq'))
- grad_gain_one: float32 [1024], P(('dp', 'seq'))
- grad_shift_one: float32 [1024], P(('dp', 'seq'))
- grad_gain_two: float32 [1024], P(('dp', 'seq'))
- grad_shift_two: float32 [1024], P(('dp', 'seq'))
The draws below stay inside these ranges and needn't reach their ends.
Inputs may be any that keep to these rules, and one draw needn't show every extreme that they name: `item_count`: each data group holds 1 or 2 items in its first slots; some group is full. `valid_len`: valid patches of each item slot, counted from its first patch; some live item has all 512.
All inputs are finite; a program needn't handle non-finite values.
Results may differ from the reference program's by a relative error of at most 0.014.
Values may be sent and summed in bfloat16 or wider, within the bound.
No kernel may reach another device: no remote copies, remote signals or barrier semaphores. Data moves between devices by JAX's collectives and lax.ppermute only.
A program may use at most 192 MiB of HBM per device.

```python
import jax
import jax.numpy as jnp
from jax import lax

D = 1024
FF = 4096
HEADS = 16
HEAD_DIM = 64
SLOTS = 2
LENGTH = 512
ITEMS = 16
N_DP = 8


def draw_item_count(key, part):
    counts = jax.random.randint(jax.random.fold_in(key, 11), (N_DP,), SLOTS - 1, SLOTS + 1)
    chosen = jax.random.randint(jax.random.fold_in(key, 12), (), 0, N_DP)
    return jnp.where(jnp.arange(N_DP) == chosen, SLOTS, counts).astype(jnp.int32)


def draw_valid_len(key, part):
    lengths = jax.random.randint(jax.random.fold_in(key, 13), (ITEMS,), LENGTH // 2, LENGTH + 1)
    chosen = jax.random.randint(jax.random.fold_in(key, 12), (), 0, N_DP) * SLOTS
    places = jnp.arange(ITEMS)
    lengths = jnp.where(places == chosen, LENGTH, lengths)
    lengths = jnp.where(places == chosen + 1, LENGTH // 2, lengths)
    return lengths.astype(jnp.int32)


def shard_levels(own_key, extent, pieces, low, largest):
    def one(position, blocks):
        draws = jax.random.uniform(jax.random.fold_in(jax.random.fold_in(own_key, 6), position), (blocks,), jnp.float32, low / len(pieces), largest / len(pieces))
        return jnp.repeat(jnp.exp(draws), extent[position] // blocks).reshape((-1,) + (1,) * (len(extent) - position - 1))

    factor_of = one(*pieces[0])
    for cut in pieces[1:]:
        factor_of = factor_of * one(*cut)
    return factor_of


def scatter_about(rng, extent, deviation, most, shards=(), held_as=jnp.bfloat16):
    values = deviation * jax.random.normal(rng, extent, jnp.float32)
    if shards:
        values = values * shard_levels(rng, extent, shards, -0.22, 0.18)
    return jnp.clip(values, -most, most).astype(held_as)


def setup_inputs(seed: int = 0) -> dict:
    key_of = jax.random.split(jax.random.key(seed), 18)
    return {
        "tokens": scatter_about(key_of[0], (ITEMS, LENGTH, D), 1.0, 6.0, ((0, 8), (1, 4))),
        "cotangent": scatter_about(key_of[1], (ITEMS, LENGTH, D), 1.0, 6.0, ((0, 8), (1, 4))),
        "item_count": draw_item_count(jax.random.fold_in(key_of[17], 71), 0),
        "valid_len": draw_valid_len(jax.random.fold_in(key_of[17], 71), 0),
        "w_qkv": scatter_about(key_of[4], (D, 3 * D), (D // 2) ** -0.5, 0.25, ((0, 32),)),
        "q_bias": scatter_about(key_of[5], (D,), 0.3, 1.796875, ((0, 32),)),
        "v_bias": scatter_about(key_of[6], (D,), 0.3, 1.796875, ((0, 32),)),
        "w_out": scatter_about(key_of[7], (D, D), (D // 16) ** -0.5, 0.75, ((0, 32),)),
        "out_bias": scatter_about(key_of[8], (D,), 0.3, 1.796875, ((0, 32),)),
        "w_up": scatter_about(key_of[9], (D, FF), D ** -0.5, 0.1875, ((0, 32),)),
        "up_bias": scatter_about(key_of[10], (FF,), 0.3, 1.796875, ((0, 32),)),
        "w_down": scatter_about(key_of[11], (FF, D), (FF // 2) ** -0.5, 0.125, ((0, 32),)),
        "down_bias": scatter_about(key_of[12], (D,), 0.3, 1.796875, ((0, 32),)),
        "gain_one": jnp.clip(1.0 + 0.15 * jax.random.normal(key_of[13], (D,), jnp.float32), 0.25, 1.75).astype(jnp.bfloat16),
        "shift_one": scatter_about(key_of[14], (D,), 0.3, 1.796875, ((0, 32),)),
        "gain_two": jnp.clip(1.0 + 0.15 * jax.random.normal(key_of[15], (D,), jnp.float32), 0.25, 1.75).astype(jnp.bfloat16),
        "shift_two": scatter_about(key_of[16], (D,), 0.3, 1.796875, ((0, 32),)),
    }


@jax.custom_vjp
def low(v):
    return lax.optimization_barrier(v.astype(jnp.bfloat16)).astype(jnp.float32)

@jax.custom_vjp
def low_back(v):
    return v

def low_keep(v):
    return (low(v), None)

def low_pass(kept, grad):
    return (grad,)

def back_keep(v):
    return (v, None)

def back_low(kept, grad):
    return (low(grad),)
low.defvjp(low_keep, low_pass)
low_back.defvjp(back_keep, back_low)
EPSILON = 1e-06

def layer_norm(values, gain, shift):
    center = values - lax.optimization_barrier(jnp.mean(values, axis=-1, keepdims=True))
    spread = lax.optimization_barrier(jnp.mean(center * center, axis=-1, keepdims=True))
    return center * lax.rsqrt(spread + EPSILON) * gain + shift

def gelu_exact(values):
    return 0.5 * values * (1.0 + lax.erf(values * 0.7071067811865476))

def matmul(left, right):
    return jnp.dot(left, right, precision=lax.Precision.HIGHEST, preferred_element_type=jnp.float32)

def item_forward(tokens, row_mask, key_ok, params):
    w_qkv, q_bias, v_bias, w_out, out_bias, w_up, up_bias, w_down, down_bias, gain_one, shift_one, gain_two, shift_two = params
    length = tokens.shape[0]
    first = low(layer_norm(tokens, gain_one, shift_one))
    bias = jnp.concatenate([q_bias, jnp.zeros_like(q_bias), v_bias])
    qkv = low(low_back(matmul(first, w_qkv) + bias))
    query = qkv[:, :D].reshape(length, HEADS, HEAD_DIM)
    keys = qkv[:, D:2 * D].reshape(length, HEADS, HEAD_DIM)
    values = qkv[:, 2 * D:].reshape(length, HEADS, HEAD_DIM)
    scores = jnp.einsum('qhd,khd->hqk', query, keys, precision=lax.Precision.HIGHEST) * HEAD_DIM ** (-0.5)
    scores = low_back(scores)
    scores = jnp.where(key_ok[None, None, :], scores, -1e+30)
    peak = lax.optimization_barrier(jnp.max(scores, axis=-1, keepdims=True))
    expo = jnp.exp(scores - peak)
    probs = low(expo / lax.optimization_barrier(jnp.sum(expo, axis=-1, keepdims=True)))
    mixed = jnp.einsum('hqk,khd->qhd', probs, values, precision=lax.Precision.HIGHEST).reshape(length, D)
    mixed = low(low_back(mixed))
    second_in = tokens + low_back(matmul(mixed, w_out) + out_bias)
    second = low(layer_norm(second_in, gain_two, shift_two))
    hidden = low(gelu_exact(low_back(matmul(second, w_up) + up_bias)))
    return row_mask[:, None] * (second_in + matmul(hidden, w_down) + down_bias)

def reference(tokens, cotangent, item_count, valid_len, w_qkv, q_bias, v_bias, w_out, out_bias, w_up, up_bias, w_down, down_bias, gain_one, shift_one, gain_two, shift_two):
    params = tuple((arr.astype(jnp.float32) for arr in (w_qkv, q_bias, v_bias, w_out, out_bias, w_up, up_bias, w_down, down_bias, gain_one, shift_one, gain_two, shift_two)))
    items = jnp.arange(ITEMS).astype(jnp.int32)
    live = items % SLOTS < item_count[items // SLOTS]
    key_ok = jnp.arange(LENGTH).astype(jnp.int32)[None, :] < valid_len[:, None]
    row_mask = (key_ok & live[:, None]).astype(jnp.float32)

    def one_item(carry, inputs):
        tokens_one, cot_one, ok_one, mask_one = inputs

        def forward(values, weights):
            return item_forward(values, mask_one, ok_one, weights)
        result, pull = jax.vjp(forward, tokens_one.astype(jnp.float32), params)
        grad_in, grad_params = pull(cot_one.astype(jnp.float32))
        carry = jax.tree.map(lambda left, right: left + right, carry, grad_params)
        return (carry, (result, grad_in))
    start = jax.tree.map(jnp.zeros_like, params)
    totals, (block_out, grad_tokens) = lax.scan(one_item, start, (tokens, cotangent, key_ok, row_mask))
    return (block_out, grad_tokens, totals[0], totals[1], totals[2], totals[3], totals[4], totals[5], totals[6], totals[7], totals[8], totals[9], totals[10], totals[11], totals[12])
```

```python
import jax
import jax.numpy as jnp
from jax import lax
from jax.sharding import PartitionSpec as P

HEAD_DIM = 64
EPSILON = 1e-06
F32 = jnp.float32
BF16 = jnp.bfloat16
OUTER = 4


def dot(left, right):
    return jnp.dot(left, right, preferred_element_type=F32)


def dot_nt(left, right):
    return lax.dot_general(left, right, (((1,), (1,)), ((), ())), preferred_element_type=F32)


def dot_tn(left, right):
    return lax.dot_general(left, right, (((0,), (0,)), ((), ())), preferred_element_type=F32)


def swap(values, axis, mask):
    size = lax.axis_size(axis)
    return lax.ppermute(values, axis, [(i, i ^ mask) for i in range(size)])


def gather_seq(block):
    half = lax.axis_size("seq") // 2
    parts = [block] + [swap(block, "seq", 2 * j) for j in range(1, half)]
    mine = jnp.concatenate(parts, 0)
    return jnp.concatenate([mine, swap(mine, "seq", 1)], 0)


def scatter_seq(low, high):
    half = lax.axis_size("seq") // 2
    rows = low.shape[0] // half
    mine = low + swap(high, "seq", 1).astype(F32)
    total = mine[:rows]
    for j in range(1, half):
        part = mine[j * rows : (j + 1) * rows].astype(BF16)
        total = total + swap(part, "seq", 2 * j).astype(F32)
    return total


def exchange_seq(pieces):
    size = lax.axis_size("seq")
    own = lax.axis_index("seq")
    take = lambda k: lax.dynamic_index_in_dim(pieces, k, 0, keepdims=False)
    out = jnp.zeros_like(pieces)
    for mask in range(size):
        part = take(own ^ mask)
        if mask:
            part = swap(part, "seq", mask)
        out = lax.dynamic_update_index_in_dim(out, part, own ^ mask, 0)
    return out


def gather_dp(block):
    size = lax.axis_size("dp")
    inner = size // OUTER
    own = lax.axis_index("dp")
    got = [(0, block)]
    for k in range(1, OUTER):
        got.append((k * inner, swap(block, "dp", k * inner)))
    out = jnp.zeros((size,) + block.shape, block.dtype)
    for mask, part in got:
        out = lax.dynamic_update_index_in_dim(out, part, own ^ mask, 0)
    for j in range(1, inner):
        for mask, part in got:
            out = lax.dynamic_update_index_in_dim(
                out, swap(part, "dp", j), own ^ (mask ^ j), 0
            )
    return out


def scatter_dp(grad, wide=False):
    size = lax.axis_size("dp")
    inner = size // OUTER
    own = lax.axis_index("dp")
    low = own % inner
    high = own // inner
    kind = F32 if wide else BF16
    split = grad.reshape((OUTER, inner) + grad.shape[1:])
    take = lambda k: lax.dynamic_index_in_dim(split, k, 1, keepdims=False)
    mine = take(low)
    for j in range(1, inner):
        mine = mine + swap(take(low ^ j).astype(kind), "dp", j).astype(F32)
    pick = lambda k: lax.dynamic_index_in_dim(mine, k, 0, keepdims=False)
    total = pick(high)
    for k in range(1, OUTER):
        total = total + swap(pick(high ^ k).astype(kind), "dp", k * inner).astype(F32)
    return total


def norm_stats(values):
    center = values - jnp.mean(values, axis=-1, keepdims=True)
    spread = jnp.mean(center * center, axis=-1, keepdims=True)
    rate = lax.rsqrt(spread + EPSILON)
    return center * rate, rate


def norm_back(grad, gain, hat, rate):
    scaled = grad * gain
    return rate * (
        scaled
        - jnp.mean(scaled, axis=-1, keepdims=True)
        - hat * jnp.mean(scaled * hat, axis=-1, keepdims=True)
    )


def gelu_exact(values):
    return 0.5 * values * (1.0 + lax.erf(values * 0.7071067811865476))


def attention(qkv, key_ok, heads):
    rows = qkv.shape[0]
    split = qkv.reshape(rows, 3, heads, HEAD_DIM)
    query, keys, vals = split[:, 0], split[:, 1], split[:, 2]
    scores = jnp.einsum("qhd,khd->hqk", query, keys, preferred_element_type=F32)
    scores = jnp.where(key_ok[None, None, :], scores * HEAD_DIM ** (-0.5), -1e30)
    peak = jnp.max(scores, axis=-1, keepdims=True)
    expo = jnp.exp(scores - peak)
    probs = expo / jnp.sum(expo, axis=-1, keepdims=True)
    mixed = jnp.einsum("hqk,khd->qhd", probs.astype(BF16), vals, preferred_element_type=F32)
    return mixed.reshape(rows, heads * HEAD_DIM).astype(BF16), probs


def attention_back(qkv, probs, grad, heads):
    rows = qkv.shape[0]
    split = qkv.reshape(rows, 3, heads, HEAD_DIM)
    query, keys, vals = split[:, 0], split[:, 1], split[:, 2]
    grad = grad.reshape(rows, heads, HEAD_DIM)
    scale = HEAD_DIM ** (-0.5)
    grad_probs = jnp.einsum("qhd,khd->hqk", grad, vals, preferred_element_type=F32)
    row_sum = jnp.sum(grad_probs * probs, axis=-1, keepdims=True)
    grad_scores = (probs * (grad_probs - row_sum)).astype(BF16)
    dq = jnp.einsum("hqk,khd->qhd", grad_scores, keys, preferred_element_type=F32) * scale
    dk = jnp.einsum("hqk,qhd->khd", grad_scores, query, preferred_element_type=F32) * scale
    dv = jnp.einsum("hqk,qhd->khd", probs.astype(BF16), grad, preferred_element_type=F32)
    return jnp.stack([dq, dk, dv], 1).astype(BF16).reshape(rows, 3 * heads * HEAD_DIM)


def body(
    tokens,
    cotangent,
    item_count,
    valid_len,
    w_qkv,
    q_bias,
    v_bias,
    w_out,
    out_bias,
    w_up,
    up_bias,
    w_down,
    down_bias,
    gain_one,
    shift_one,
    gain_two,
    shift_two,
):
    slots, rows, width = tokens.shape
    n_seq = lax.axis_size("seq")
    n_dp = lax.axis_size("dp")
    d = lax.axis_index("dp")
    s = lax.axis_index("seq")
    half = n_seq // 2
    cols = width // n_seq
    heads = cols // HEAD_DIM
    piece = width // (n_dp * n_seq)
    hidden_all = w_up.shape[1]
    hidden = hidden_all // n_seq
    hpiece = hidden_all // (n_dp * n_seq)

    order = jnp.arange(n_seq)
    owner = s ^ (2 * (order % half) + order // half)
    place = (owner[:, None] * rows + jnp.arange(rows)[None, :]).reshape(-1)
    live = jnp.arange(slots) < item_count[0]

    small = jnp.concatenate(
        [q_bias, v_bias, out_bias, down_bias, gain_one, shift_one, gain_two, shift_two, up_bias]
    )
    small = gather_dp(small[None])
    small = exchange_all(small)
    vectors = jnp.transpose(small[:, :, 0, : 8 * piece].reshape(n_seq, n_dp, 8, piece), (2, 1, 0, 3))
    vectors = vectors.reshape(8, width).astype(F32)
    full_obias, full_dbias, gain1, shift1, gain2, shift2 = [vectors[i] for i in range(2, 8)]
    own_small = lax.dynamic_index_in_dim(small, s, 0, keepdims=False)
    ubias = own_small[:, 0, 8 * piece :].reshape(hidden).astype(F32)
    qb = lax.dynamic_slice_in_dim(vectors[0], s * cols, cols)
    vb = lax.dynamic_slice_in_dim(vectors[1], s * cols, cols)
    qkv_bias = jnp.concatenate([qb, jnp.zeros_like(qb), vb])

    qkv_pieces = jnp.transpose(w_qkv.reshape(piece, 3, n_seq, cols), (2, 0, 1, 3)).reshape(
        n_seq, piece, 3 * cols
    )
    wqkv = gather_dp(exchange_seq(qkv_pieces).reshape(n_seq * piece, 3 * cols))
    wqkv = wqkv.reshape(width, 3 * cols)
    blocks = n_dp // n_seq
    wout = gather_dp(w_out).reshape(n_seq, blocks * piece, width)
    wout = exchange_seq(wout).reshape(n_seq, blocks, piece, width)
    wout = jnp.transpose(wout, (1, 0, 2, 3)).reshape(cols, width)
    up_pieces = jnp.transpose(w_up.reshape(piece, n_dp, n_seq, hpiece), (2, 0, 1, 3)).reshape(
        n_seq, piece, hidden
    )
    wup = gather_dp(exchange_seq(up_pieces).reshape(n_seq * piece, hidden)).reshape(width, hidden)
    wdown = gather_dp(w_down).reshape(hidden, width)

    xs, a1s, qkvs, probss, atts, x2s, hat2s, rate2s = [], [], [], [], [], [], [], []
    a2s, acts, pulls, outs, dys, masks, dy_owns = [], [], [], [], [], [], []
    for i in range(slots):
        x = gather_seq(tokens[i]).astype(F32)
        key_ok = place < valid_len[i]
        mask = (key_ok & live[i]).astype(F32)[:, None]
        dy = gather_seq(cotangent[i]).astype(F32) * mask
        hat1, rate1 = norm_stats(x)
        a1 = (hat1 * gain1 + shift1).astype(BF16)
        qkv = (dot(a1, wqkv) + qkv_bias).astype(BF16)
        att, probs = attention(qkv, key_ok, heads)
        cut = half * rows
        high = dot(att[cut:], wout).astype(BF16)
        low = dot(att[:cut], wout)
        x2 = x[:rows] + (scatter_seq(low, high) + full_obias)
        hat2, rate2 = norm_stats(x2)
        a2 = gather_seq((hat2 * gain2 + shift2).astype(BF16))
        act, pull = jax.vjp(gelu_exact, dot(a2, wup) + ubias)
        act = act.astype(BF16)
        high = dot(act[cut:], wdown).astype(BF16)
        low = dot(act[:cut], wdown)
        out = mask[:rows] * (x2 + scatter_seq(low, high) + full_dbias)
        for store, value in zip(
            (a1s, qkvs, probss, atts, hat2s, rate2s, a2s, acts, pulls, outs, dys, masks, dy_owns),
            (a1, qkv, probs, att, hat2, rate2, a2, act, pull, out, dy.astype(BF16), mask, dy[:rows]),
        ):
            store.append(value)
    hat1_rates = [norm_stats(tokens[i].astype(F32)) for i in range(slots)]

    dus = []
    dxs = []
    dattns = []
    g_gain2 = g_shift2 = 0.0
    for i in range(slots):
        (du,) = pulls[i](dot_nt(dys[i], wdown))
        du = du.astype(BF16)
        dus.append(du)
        high = dot_nt(du[cut:], wup).astype(BF16)
        low = dot_nt(du[:cut], wup)
        dh2 = scatter_seq(low, high)
        g_gain2 = g_gain2 + jnp.sum(dh2 * hat2s[i], axis=0)
        g_shift2 = g_shift2 + jnp.sum(dh2, axis=0)
        dx2 = dy_owns[i] + norm_back(dh2, gain2, hat2s[i], rate2s[i])
        dxs.append(dx2)
        dattns.append(dx2.astype(BF16))
    rows_of = lambda parts: jnp.concatenate(parts, 0)
    g_wdown = scatter_dp(dot_tn(rows_of(acts), rows_of(dys)).reshape(n_dp, hpiece, width))
    g_dbias = jnp.sum(rows_of(dy_owns), axis=0)
    g_wup = scatter_dp(dot_tn(rows_of(a2s), rows_of(dus)).reshape(n_dp, n_seq * piece, hidden))
    g_wup = exchange_seq(g_wup.reshape(n_seq, piece, hidden).astype(BF16)).astype(F32)
    g_wup = jnp.transpose(g_wup.reshape(n_seq, piece, n_dp, hpiece), (1, 2, 0, 3)).reshape(
        piece, hidden_all
    )
    g_ubias = sum(jnp.sum(du.astype(F32), axis=0) for du in dus)
    g_obias = sum(jnp.sum(v.astype(F32), axis=0) for v in dattns)

    full_dattns = [gather_seq(v) for v in dattns]
    g_wout = dot_tn(rows_of(atts), rows_of(full_dattns)).reshape(blocks, n_seq, piece, width)
    g_wout = jnp.transpose(g_wout, (1, 0, 2, 3)).reshape(n_seq, blocks * piece, width)
    g_wout = exchange_seq(g_wout.astype(BF16)).reshape(n_dp, piece, width)
    g_wout = scatter_dp(g_wout.astype(F32))
    dqkvs = []
    grads = []
    g_gain1 = g_shift1 = 0.0
    for i in range(slots):
        datt = dot_nt(full_dattns[i], wout).astype(BF16)
        dqkv = attention_back(qkvs[i], probss[i], datt, heads)
        dqkvs.append(dqkv)
        high = dot_nt(dqkv[cut:], wqkv).astype(BF16)
        low = dot_nt(dqkv[:cut], wqkv)
        dh1 = scatter_seq(low, high)
        hat1, rate1 = hat1_rates[i]
        g_gain1 = g_gain1 + jnp.sum(dh1 * hat1, axis=0)
        g_shift1 = g_shift1 + jnp.sum(dh1, axis=0)
        grads.append(dxs[i] + norm_back(dh1, gain1, hat1, rate1))
    g_wqkv = scatter_dp(
        dot_tn(rows_of(a1s), rows_of(dqkvs)).reshape(n_dp, n_seq * piece, 3 * cols)
    )
    g_wqkv = exchange_seq(g_wqkv.reshape(n_seq, piece, 3 * cols).astype(BF16)).astype(F32)
    g_wqkv = jnp.transpose(g_wqkv.reshape(n_seq, piece, 3, cols), (1, 2, 0, 3)).reshape(
        piece, 3 * width
    )
    g_bias = sum(jnp.sum(v.astype(F32), axis=0) for v in dqkvs)
    spread = lambda v: lax.dynamic_update_slice_in_dim(jnp.zeros((width,), F32), v, s * cols, 0)
    stack = jnp.stack(
        [
            spread(g_bias[:cols]),
            spread(g_bias[2 * cols :]),
            g_obias,
            g_dbias,
            g_gain1,
            g_shift1,
            g_gain2,
            g_shift2,
        ]
    )
    stack = jnp.transpose(stack.reshape(8, n_dp, n_seq, piece), (1, 2, 0, 3)).reshape(
        n_dp, n_seq, 8 * piece
    )
    wide_ubias = lax.dynamic_update_slice(
        jnp.zeros((n_dp, n_seq, hpiece), F32), g_ubias.reshape(n_dp, 1, hpiece), (0, s, 0)
    )
    small = scatter_dp(jnp.concatenate([stack, wide_ubias], -1), wide=True)
    small = jnp.sum(exchange_seq(small), axis=0)
    vec = small[: 8 * piece].reshape(8, piece)
    return (
        jnp.stack(outs, 0),
        jnp.stack(grads, 0),
        g_wqkv,
        vec[0],
        vec[1],
        g_wout,
        vec[2],
        g_wup,
        small[8 * piece :],
        g_wdown,
        vec[3],
        vec[4],
        vec[5],
        vec[6],
        vec[7],
    )


def exchange_all(values):
    size = lax.axis_size("seq")
    own = lax.axis_index("seq")
    out = jnp.zeros((size,) + values.shape, values.dtype)
    for mask in range(size):
        part = swap(values, "seq", mask) if mask else values
        out = lax.dynamic_update_index_in_dim(out, part, own ^ mask, 0)
    return out


def solution(mesh):
    both = ("dp", "seq")
    act = P("dp", "seq", None)
    mat = P(both, None)
    vec = P(both)
    return jax.shard_map(
        body,
        mesh=mesh,
        in_specs=(act, act, P("dp"), P("dp"), mat, vec, vec, mat, vec, mat, vec, mat)
        + (vec,) * 5,
        out_specs=(act, act, mat, vec, vec, mat, vec, mat, vec, mat) + (vec,) * 5,
        check_vma=False,
    )
```

```python
import functools

import jax
import jax.numpy as jnp
from jax import lax
from jax.experimental import pallas as pl
from jax.experimental.pallas import tpu as pltpu
from jax.sharding import PartitionSpec as P

HEAD_DIM = 64
LANES = 128
EPSILON = 1e-06
F32 = jnp.float32
BF16 = jnp.bfloat16
OUTER = 4
ORDER = (0, 2, 1, 3)
VMEM = pl.BlockSpec(memory_space=pltpu.VMEM)
ANY = pl.BlockSpec(memory_space=pl.ANY)
LIMIT = 14 * 1024 * 1024
SOFTMAX_RATE = HEAD_DIM**-0.5 * 1.4426950408889634
N_VEC = 8
VEC_ROWS = 16


def dot(left, right):
    return jnp.dot(left, right, preferred_element_type=F32)


def dot_nt(left, right):
    return lax.dot_general(left, right, (((1,), (1,)), ((), ())), preferred_element_type=F32)


def dot_tn(left, right):
    return lax.dot_general(left, right, (((0,), (0,)), ((), ())), preferred_element_type=F32)


def swap(values, axis, mask):
    size = lax.axis_size(axis)
    return lax.ppermute(values, axis, [(i, i ^ mask) for i in range(size)])


def shape(dims, kind):
    return jax.ShapeDtypeStruct(tuple(dims), kind)


def after(values, *others):
    return lax.optimization_barrier((values,) + others)[0]


def fence(*values):
    return lax.optimization_barrier(values)


def call(kernel, name, ins, outs, scratch=(), specs=None, flops=0):
    return pl.pallas_call(
        kernel,
        name=name,
        out_shape=tuple(outs),
        in_specs=specs or [VMEM] * len(ins),
        out_specs=tuple([VMEM] * len(outs)),
        scratch_shapes=list(scratch),
        compiler_params=pltpu.CompilerParams(vmem_limit_bytes=LIMIT),
        cost_estimate=pl.CostEstimate(
            flops=int(flops), bytes_accessed=0, transcendentals=0
        ),
    )(*ins)


def aligned(index, size):
    return pl.multiple_of(index * size, size)


def start_copies(jobs, scratch, sems):
    copies = []
    for src, block, rows in jobs:
        copy = pltpu.make_async_copy(
            src, scratch.at[pl.ds(aligned(block, rows), rows)], sems.at[len(copies)]
        )
        copy.start()
        copies.append(copy)
    return copies


def dp_jobs(refs, masks):
    own = lax.axis_index("dp")
    jobs = []
    for ref, group in zip(refs, masks):
        for i, mask in enumerate(group):
            jobs.append((ref.at[i], own ^ mask, ref.shape[1]))
    return jobs


def out_jobs(refs, tile, blocks):
    own = lax.axis_index("seq")
    size = len(refs)
    rows = (refs[0].shape[0] - tile) // blocks
    return [
        (ref.at[pl.ds(tile + b * rows, rows)], b * size + (own ^ r), rows)
        for r, ref in enumerate(refs)
        for b in range(blocks)
    ]


def pack_kernel(cols, hpiece, wqkv, wup, *outs):
    own = lax.axis_index("seq")
    size = len(outs)
    hidden = wup.shape[1] // size
    width = wqkv.shape[1] // 3
    for r, out in enumerate(outs):
        dest = own ^ r
        for i in range(3):
            at = pl.multiple_of(dest * cols + i * width, LANES)
            out[:, i * cols : (i + 1) * cols] = wqkv[:, pl.ds(at, cols)]
        for i in range(hidden // hpiece):
            at = pl.multiple_of((i * size + dest) * hpiece, LANES)
            start = 3 * cols + i * hpiece
            out[:, start : start + hpiece] = wup[:, pl.ds(at, hpiece)]


def place_kernel(*refs):
    size = len(refs) - 2
    qkv, up = refs[size:]
    own = lax.axis_index("seq")
    cut = qkv.shape[2]
    for r in range(size):
        rows = refs[r].shape[0]
        at = pl.ds(aligned(own ^ r, rows), rows)
        qkv[0, at, :] = refs[r][:, :cut]
        up[0, at, :] = refs[r][:, cut:]


def unplace_kernel(cols, hpiece, *refs):
    size = (len(refs) - 2) // 2
    qkv, up = refs[2 * size :]
    own = lax.axis_index("seq")
    width = qkv.shape[1] // 3
    for r in range(size):
        src = own ^ r
        part = refs[r]
        for i in range(3):
            at = pl.multiple_of(src * cols + i * width, LANES)
            qkv[:, pl.ds(at, cols)] = part[:, i * cols : (i + 1) * cols].astype(F32)
        part = refs[size + r]
        for i in range(part.shape[1] // hpiece):
            at = pl.multiple_of((i * size + src) * hpiece, LANES)
            up[:, pl.ds(at, hpiece)] = part[:, i * hpiece : (i + 1) * hpiece].astype(F32)


def out_pack_kernel(tile, wout, *refs):
    n = N_VEC + 1
    vecs, out, landed, scratch, sems = refs[:n], refs[n], refs[n + 1 : -2], refs[-2], refs[-1]
    copies = [pltpu.make_async_copy(v, l, sems.at[i]) for i, (v, l) in enumerate(zip(vecs, landed))]
    for copy in copies:
        copy.start()
    out[0, tile:, :] = wout[...]
    scratch[...] = jnp.zeros_like(scratch)
    for copy in copies:
        copy.wait()
    for i, vec in enumerate(landed):
        row, lane = (0, i * LANES) if i < N_VEC else (1, 0)
        scratch[row : row + 1, lane : lane + vec.shape[1]] = vec[...].astype(F32)
    out[0, :tile, :] = scratch[...].astype(BF16)


def out_pieces_kernel(masks, tile, blocks, *refs):
    n = len(masks)
    outs, mixed = refs[n:-1], refs[-1]
    d = lax.axis_index("dp")
    s = lax.axis_index("seq")
    flat = [(i, j) for i, group in enumerate(masks) for j in range(len(group))]
    mask_of = [mask for group in masks for mask in group]
    total = None
    for n, (i, j) in enumerate(flat):
        part = refs[i][j, :tile, :].astype(F32)
        part = pltpu.roll(part, 2 * n, 0) if n else part
        total = part if total is None else total + part
    mixed[...] = total.astype(BF16)
    piece = refs[0].shape[1] - tile
    for r, out in enumerate(outs):
        out[:tile, :] = mixed[...]
        for b in range(blocks):
            want = d ^ ((s ^ r) * blocks + b)
            for (i, j), mask in zip(flat, mask_of):

                @pl.when(want == mask)
                def _(out=out, b=b, i=i, j=j):
                    start = tile + b * piece
                    out[start : start + piece, :] = refs[i][j, tile:, :]


def vector_unpack_kernel(masks, tile, n_seq, cols, hpiece, *refs):
    parts, (vectors, qkv_bias, ubias) = refs[:n_seq], refs[n_seq:]
    width = vectors.shape[1]
    hidden = ubias.shape[1]
    mask_of = [mask for group in masks for mask in group]
    piece = width // (n_seq * len(mask_of))
    s = lax.axis_index("seq")
    d = lax.axis_index("dp")
    row = lax.broadcasted_iota(jnp.int32, (tile, 1), 0)
    dist = jnp.zeros_like(row)
    for n, mask in enumerate(mask_of):
        dist = jnp.where(row // 2 == n, mask, dist)
    source = d ^ dist
    lane = lax.broadcasted_iota(jnp.int32, (LANES, width), 1)
    sub = lax.broadcasted_iota(jnp.int32, (LANES, width), 0)
    spread = jnp.where(lane % piece == sub, 1.0, 0.0).astype(BF16)
    target = lax.broadcasted_iota(jnp.int32, (1, width), 1) // piece
    even = row % 2 == 0
    for i in range(N_VEC):
        total = None
        for r, part in enumerate(parts):
            tiled = dot(part[:tile, i * LANES : (i + 1) * LANES], spread)
            here = even & (source * n_seq + (s ^ r) == target)
            tiled = jnp.sum(jnp.where(here, tiled, 0.0), axis=0, keepdims=True)
            total = tiled if total is None else total + tiled
        vectors[i : i + 1, :] = total
    lane = lax.broadcasted_iota(jnp.int32, (LANES, hidden), 1)
    sub = lax.broadcasted_iota(jnp.int32, (LANES, hidden), 0)
    spread = jnp.where(lane % hpiece == sub, 1.0, 0.0).astype(BF16)
    target = lax.broadcasted_iota(jnp.int32, (1, hidden), 1) // hpiece
    tiled = dot(parts[0][:tile, :LANES], spread)
    here = (row % 2 == 1) & (source == target)
    ubias[...] = jnp.sum(jnp.where(here, tiled, 0.0), axis=0, keepdims=True)
    at = pl.ds(pl.multiple_of(s * cols, LANES), cols)
    qkv_bias[...] = jnp.zeros_like(qkv_bias)
    qkv_bias[:, :cols] = vectors[0:1, at]
    qkv_bias[:, 2 * cols :] = vectors[1:2, at]


def positions(block, rows, n_seq, axis):
    half = n_seq // 2
    owner = lax.axis_index("seq") ^ (2 * (block % half) + block // half)
    dims = (rows, 1) if axis == 0 else (1, rows)
    return owner * rows + lax.broadcasted_iota(jnp.int32, dims, axis)


def attention_kernel(masks, tile, blocks, cols, n_seq, item, *refs):
    n = len(masks)
    a1, bias, lens = refs[:3]
    pieces = refs[3 : 3 + n]
    outs = refs[3 + n : 3 + n + n_seq]
    qkv, att, probs, own, rest, high, wqkv, wout, ok, sems, out_sems = refs[3 + n + n_seq :]
    rows = a1.shape[0]
    cut = rows // 2
    blk = own.shape[0]
    copies = start_copies(dp_jobs(pieces, masks), wqkv, sems)
    out_copies = start_copies(out_jobs(outs, tile, blocks), wout, out_sems)
    for q in range(n_seq):
        good = positions(q, blk, n_seq, 1) < lens[item]
        ok[:, q * blk : (q + 1) * blk] = jnp.where(good, 0.0, -1e30)
    for copy in copies:
        copy.wait()
    for i in range(3):
        part = slice(i * cols, (i + 1) * cols)
        qkv[:, part] = (dot(a1[...], wqkv[:, part]) + bias[:, part]).astype(BF16)
    step_rows = min(256, rows)
    lane = lax.broadcasted_iota(jnp.int32, (1, LANES), 1)
    sides = [(lane < HEAD_DIM), (lane >= HEAD_DIM)]
    for pair in range(cols // LANES):
        at = slice(pair * LANES, (pair + 1) * LANES)
        keys = qkv[:, cols + pair * LANES : cols + (pair + 1) * LANES]
        vals = qkv[:, 2 * cols + pair * LANES : 2 * cols + (pair + 1) * LANES]
        split = [jnp.where(side, vals, jnp.zeros_like(vals)) for side in sides]

        def step(block, carry, pair=pair, at=at, keys=keys, split=split):
            place = pl.ds(aligned(block, step_rows), step_rows)
            query = qkv[place, at]
            total = None
            for h in range(2):
                q = jnp.where(sides[h], query, jnp.zeros_like(query))
                scores = dot_nt(q, keys) + ok[...]
                peak = jnp.max(scores, axis=-1, keepdims=True)
                expo = jnp.exp2((scores - peak) * SOFTMAX_RATE)
                rate = 1.0 / jnp.sum(expo, axis=-1, keepdims=True)
                low = (expo * rate).astype(BF16)
                probs[2 * pair + h, place, :] = low
                out = dot(low, split[h])
                total = out if total is None else total + out
            att[place, at] = total.astype(BF16)
            return carry

        lax.fori_loop(0, rows // step_rows, step, 0)
    for copy in out_copies:
        copy.wait()
    high[...] = dot(att[cut:, :], wout[...]).astype(BF16)
    own[...] = dot(att[:blk, :], wout[...])
    rest[...] = dot(att[blk:cut, :], wout[...])


def attention_back_kernel(masks, tile, blocks, cols, n_seq, *refs):
    n = len(masks)
    parts = refs[:n_seq]
    qkv, probs, hat = refs[n_seq : n_seq + 3]
    refs = refs[n_seq + 3 :]
    pieces, outs = refs[:n], refs[n : n + n_seq]
    dqkv, own, rest, high, sums, sums_one, wqkv, wout, grad, datt, dkt, dvt, sems, out_sems = refs[
        n + n_seq :
    ]
    rows = dqkv.shape[0]
    cut = rows // 2
    blk = own.shape[0]
    out_copies = start_copies(out_jobs(outs, tile, blocks), wout, out_sems)
    copies = start_copies(dp_jobs(pieces, masks), wqkv, sems)
    for i, part in enumerate(parts):
        grad[i * blk : (i + 1) * blk, :] = part[...]
    for copy in out_copies:
        copy.wait()
    datt[...] = dot_nt(grad[...], wout[...]).astype(BF16)
    step_rows = min(256, rows)
    lane = lax.broadcasted_iota(jnp.int32, (1, LANES), 1)
    sides = [(lane < HEAD_DIM), (lane >= HEAD_DIM)]
    scale = HEAD_DIM**-0.5
    for pair in range(cols // LANES):
        at = slice(pair * LANES, (pair + 1) * LANES)
        at_k = slice(cols + pair * LANES, cols + (pair + 1) * LANES)
        at_v = slice(2 * cols + pair * LANES, 2 * cols + (pair + 1) * LANES)
        keys = qkv[:, at_k]
        vals = qkv[:, at_v]
        split = [jnp.where(side, keys, jnp.zeros_like(keys)) for side in sides]
        dkt[...] = jnp.zeros_like(dkt)
        dvt[...] = jnp.zeros_like(dvt)

        def step(block, carry, pair=pair, at=at, vals=vals, split=split):
            place = pl.ds(aligned(block, step_rows), step_rows)
            gatt = datt[place, at]
            query = qkv[place, at]
            gatt_t = gatt.T
            query_t = query.T
            total = None
            for h in range(2):
                g = jnp.where(sides[h], gatt, jnp.zeros_like(gatt))
                gp = dot_nt(g, vals)
                low = probs[2 * pair + h, place, :]
                p = low.astype(F32)
                mean = jnp.sum(gp * p, axis=-1, keepdims=True)
                gs = (p * (gp - mean)).astype(BF16)
                half = slice(h * HEAD_DIM, (h + 1) * HEAD_DIM)
                dvt[half, :] += dot(gatt_t[half, :], low)
                dkt[half, :] += dot(query_t[half, :], gs)
                out = dot(gs, split[h])
                total = out if total is None else total + out
            dqkv[place, at] = (total * scale).astype(BF16)
            return carry

        lax.fori_loop(0, rows // step_rows, step, 0)
        dqkv[:, at_k] = (dkt[...].T * scale).astype(BF16)
        dqkv[:, at_v] = dvt[...].T.astype(BF16)
    for copy in copies:
        copy.wait()
    sums[...] = jnp.sum(dqkv[...].astype(F32), axis=0, keepdims=True)
    sums_one[...] = jnp.zeros_like(sums_one)

    def last(block, carry):
        at = pl.ds(aligned(block, 256), 256)
        value = dot_nt(dqkv[...], wqkv[at, :])
        own[:, at] = value[:blk]
        rest[:, at] = value[blk:cut]
        high[:, at] = value[cut:].astype(BF16)
        sums_one[0:1, at] = jnp.sum(value * hat[:, at].astype(F32), axis=0, keepdims=True)
        sums_one[1:2, at] = jnp.sum(value, axis=0, keepdims=True)
        return carry

    lax.fori_loop(0, wqkv.shape[0] // 256, last, 0)


def up_kernel(masks, n_seq, *refs):
    n = len(masks)
    parts, bias = refs[:n_seq], refs[n_seq]
    pieces = refs[n_seq + 1 : n_seq + 1 + n]
    a2, act, slope, wup, sems = refs[n_seq + 1 + n :]
    blk = parts[0].shape[0]
    rows = a2.shape[0]
    width = min(256, act.shape[1])
    copies = start_copies(dp_jobs(pieces, masks), wup, sems)
    for i, part in enumerate(parts):
        a2[i * blk : (i + 1) * blk, :] = part[...]
    for copy in copies:
        copy.wait()
    half = min(256, rows)
    for i in range(rows // half):
        place = slice(i * half, (i + 1) * half)

        def step(block, carry, place=place):
            at = pl.ds(aligned(block, width), width)
            u = dot(a2[place, :], wup[:, at]) + bias[:, at]
            cdf = 0.5 * (1.0 + lax.erf(u * 0.7071067811865476))
            bell = jnp.exp2(u * u * -0.7213475204444817) * 0.3989422804014327
            act[place, at] = (u * cdf).astype(BF16)
            slope[place, at] = cdf + u * bell
            return carry

        lax.fori_loop(0, act.shape[1] // width, step, 0)


def down_kernel(masks, *refs):
    n = len(masks)
    dy, act, slope = refs[:3]
    ups = refs[3 : 3 + n]
    downs = refs[3 + n : 3 + 2 * n]
    du, own, rest, high, oown, orest, ohigh, sums, wup, wdown, sems_up, sems_down = refs[3 + 2 * n :]
    rows = dy.shape[0]
    cut = rows // 2
    blk = own.shape[0]
    hidden = act.shape[1]
    width = min(256, hidden)
    down_copies = start_copies(dp_jobs(downs, masks), wdown, sems_down)
    up_copies = start_copies(dp_jobs(ups, masks), wup, sems_up)
    for copy in down_copies:
        copy.wait()

    def first(block, carry):
        at = pl.ds(aligned(block, width), width)
        value = (slope[:, at] * dot_nt(dy[...], wdown[at, :])).astype(BF16)
        du[:, at] = value
        sums[:, at] = jnp.sum(value.astype(F32), axis=0, keepdims=True)
        return carry

    lax.fori_loop(0, hidden // width, first, 0)
    for copy in up_copies:
        copy.wait()

    def second(block, carry):
        at = pl.ds(aligned(block, 256), 256)
        value = dot_nt(du[...], wup[at, :])
        own[:, at] = value[:blk]
        rest[:, at] = value[blk:cut]
        high[:, at] = value[cut:].astype(BF16)
        value = dot(act[...], wdown[:, at])
        oown[:, at] = value[:blk]
        orest[:, at] = value[blk:cut]
        ohigh[:, at] = value[cut:].astype(BF16)
        return carry

    lax.fori_loop(0, wup.shape[0] // 256, second, 0)


def grad_kernel(j, inner, slots, *refs):
    lefts, rights = refs[:slots], refs[slots : 2 * slots]
    *outs, turned = refs[2 * slots :]
    rows = lefts[0].shape[0]
    each, blk = outs[0].shape[:2]
    own = lax.axis_index("dp")
    for n, k in enumerate(ORDER):
        at = pl.ds(aligned(own ^ (k * inner + j), blk), blk)
        for i, left in enumerate(lefts):
            turned[n * blk : (n + 1) * blk, i * rows : (i + 1) * rows] = left[:, at].T
    width = min(256, outs[0].shape[2])

    def step(block, carry):
        at = pl.ds(aligned(block, width), width)
        total = None
        for i, right in enumerate(rights):
            out = dot(turned[:, i * rows : (i + 1) * rows], right[:, at])
            total = out if total is None else total + out
        for n in range(len(ORDER)):
            out = outs[n // each]
            out[n % each, :, at] = total[n * blk : (n + 1) * blk].astype(out.dtype)
        return carry

    lax.fori_loop(0, outs[0].shape[2] // width, step, 0)


def grad_out_kernel(masks, tile, cols, hpiece, slots, n_seq, *refs):
    take = lambda n: (refs[:n], refs[n:])
    lefts, refs = take(slots)
    rights, refs = take(slots * n_seq)
    sums1, refs = take(slots)
    sums2, refs = take(slots)
    sums_q, refs = take(slots)
    sums_u, refs = take(slots)
    outs, (scratch, wide) = take(n_seq)[0], refs[n_seq:]
    width = wide.shape[1]
    s = lax.axis_index("seq")
    d = lax.axis_index("dp")
    total = lambda refs: functools.reduce(lambda a, b: a + b, [ref[...] for ref in refs])
    q, u = total(sums_q), total(sums_u)
    one, two = total(sums1), total(sums2)
    wide[...] = jnp.zeros_like(wide)
    at = pl.ds(pl.multiple_of(s * cols, LANES), cols)
    wide[0:1, at] = q[:, :cols]
    wide[1:2, at] = q[:, 2 * cols :]
    wide[2:4, :] = two[:2]
    wide[4:6, :] = one[:2]
    wide[6:8, :] = two[2:4]
    piece = width // (n_seq * len(masks))
    row = lax.broadcasted_iota(jnp.int32, (n_seq * tile, 1), 0)
    near = row % tile
    dist = jnp.zeros_like(row)
    for n, mask in enumerate(masks):
        dist = jnp.where(near // 2 == n, mask, dist)
    dest = (d ^ dist) * n_seq + (s ^ (row // tile))
    dest = jnp.where(near % 2 == 0, dest, -1)
    spread = jnp.where(
        lax.broadcasted_iota(jnp.int32, (width, LANES), 0) % piece
        == lax.broadcasted_iota(jnp.int32, (width, LANES), 1),
        1.0,
        0.0,
    ).astype(BF16)
    here = lax.broadcasted_iota(jnp.int32, (1, width), 1) // piece == dest
    vecs = []
    for i in range(N_VEC):
        vecs.append(dot(jnp.where(here, wide[i : i + 1, :], 0.0).astype(BF16), spread))
    hidden = u.shape[1]
    spread = jnp.where(
        lax.broadcasted_iota(jnp.int32, (hidden, LANES), 0) % hpiece
        == lax.broadcasted_iota(jnp.int32, (hidden, LANES), 1),
        1.0,
        0.0,
    ).astype(BF16)
    dest = jnp.where(near % 2 == 1, d ^ dist, -1)[:tile]
    here = lax.broadcasted_iota(jnp.int32, (1, hidden), 1) // hpiece == dest
    long = dot(jnp.where(here, u, 0.0).astype(BF16), spread)
    for r, out in enumerate(outs):
        for i, vec in enumerate(vecs):
            value = vec[r * tile : (r + 1) * tile]
            if r == 0 and i == 0:
                value = value + long
            out[:tile, i * LANES : (i + 1) * LANES] = value.astype(BF16)
    rows = rights[0].shape[0]
    blocks = (outs[0].shape[0] - tile) // piece
    grad = None
    for i, left in enumerate(lefts):
        for q in range(n_seq):
            scratch[q * rows : (q + 1) * rows, :] = rights[i * n_seq + q][...]
        part = dot_tn(left[...], scratch[...])
        grad = part if grad is None else grad + part
    grad = grad.astype(BF16)
    for other in range(n_seq):
        for r in range(n_seq):

            @pl.when(s ^ r == other)
            def _(other=other, r=r):
                for b in range(blocks):
                    at = (b * n_seq + other) * piece
                    start = tile + b * piece
                    outs[r][start : start + piece, :] = grad[at : at + piece]


def grad_out_groups_kernel(masks, tile, *refs):
    inner = len(masks) // len(ORDER)
    pieces, outs = refs[:-inner], refs[-inner:]
    size = len(pieces)
    head = VEC_ROWS
    rows = outs[0].shape[1] - head
    blocks = (pieces[0].shape[0] - tile) // rows
    d = lax.axis_index("dp")
    s = lax.axis_index("seq")
    total = None
    for piece in pieces:
        part = piece[:tile, :].astype(F32)
        total = part if total is None else total + part
    row = lax.broadcasted_iota(jnp.int32, (tile, 1), 0)
    for n, mask in enumerate(masks):
        out = outs[n // len(ORDER)]
        i = n % len(ORDER)
        value = pltpu.roll(total, tile - 2 * n, 0) if n else total
        out[i, :head, :] = jnp.where(row < 2, value, 0.0)[:head].astype(out.dtype)
        for r in range(size):
            for b in range(blocks):

                @pl.when(d ^ mask == (s ^ r) * blocks + b)
                def _(out=out, i=i, r=r, b=b):
                    start = tile + b * rows
                    out[i, head:, :] = pieces[r][start : start + rows, :].astype(out.dtype)


def out_final_kernel(total, grad, *vecs):
    grad[...] = total[VEC_ROWS:, :]
    for i, vec in enumerate(vecs[:-1]):
        vec[...] = total[0:1, i * LANES : i * LANES + vec.shape[1]]
    vecs[-1][...] = total[1:2, : vecs[-1].shape[1]]


def gathered_sum(own, near, far, blk):
    total = own[...] + near[:blk, :].astype(F32)
    for ref in far:
        total = total + ref[...].astype(F32)
    return total


def stats(values):
    center = values - jnp.mean(values, axis=-1, keepdims=True)
    rate = lax.rsqrt(jnp.mean(center * center, axis=-1, keepdims=True) + EPSILON)
    return center * rate, rate


def norm_kernel(n_seq, *refs):
    parts, vectors, outs = refs[:n_seq], refs[n_seq], refs[n_seq + 1 :]
    rows = parts[0].shape[1]
    outs, hats = outs[: len(outs) // 2], outs[len(outs) // 2 :]
    for i, (out, kept) in enumerate(zip(outs, hats)):
        for q, part in enumerate(parts):
            hat, _ = stats(part[i].astype(F32))
            kept[q * rows : (q + 1) * rows, :] = hat.astype(BF16)
            out[q * rows : (q + 1) * rows, :] = (
                hat * vectors[4:5, :] + vectors[5:6, :]
            ).astype(BF16)


def mask_kernel(n_seq, *refs):
    parts, limits, outs = refs[:n_seq], refs[n_seq], refs[n_seq + 1 :]
    rows = parts[0].shape[1]
    for i, out in enumerate(outs):
        for q, part in enumerate(parts):
            good = jnp.where(positions(q, rows, n_seq, 0) < limits[i], 1.0, 0.0)
            out[q * rows : (q + 1) * rows, :] = (part[i].astype(F32) * good).astype(BF16)


def norm_two_kernel(item, own, near, *refs):
    *far, x, vectors, x2, a2 = refs
    value = x[item].astype(F32) + (
        gathered_sum(own, near, far, x2.shape[0]) + vectors[2:3, :]
    )
    x2[...] = value
    hat, _ = stats(value)
    a2[...] = (hat * vectors[6:7, :] + vectors[7:8, :]).astype(BF16)


def norm_back(grad, gain, hat, rate):
    scaled = grad * gain
    return rate * (
        scaled
        - jnp.mean(scaled, axis=-1, keepdims=True)
        - hat * jnp.mean(scaled * hat, axis=-1, keepdims=True)
    )


def norm_two_back_kernel(own, near, *refs):
    *far, x2, dy, vectors, dx2, low, sums = refs
    grad = gathered_sum(own, near, far, x2.shape[0])
    hat, rate = stats(x2[...])
    rows = dy[: x2.shape[0], :].astype(F32)
    value = rows + norm_back(grad, vectors[6:7, :], hat, rate)
    dx2[...] = value
    rounded = value.astype(BF16)
    low[...] = rounded
    sums[0:1, :] = jnp.sum(rounded.astype(F32), axis=0, keepdims=True)
    sums[1:2, :] = jnp.sum(rows, axis=0, keepdims=True)
    sums[2:3, :] = jnp.sum(grad * hat, axis=0, keepdims=True)
    sums[3:4, :] = jnp.sum(grad, axis=0, keepdims=True)
    sums[4:8, :] = jnp.zeros_like(sums[4:8, :])


def norm_one_back_kernel(slots, *refs):
    size = (len(refs) - slots - 3) // slots
    sums_of = [refs[i * size : (i + 1) * size] for i in range(slots)]
    refs = refs[slots * size :]
    dxs, (x, vectors, out) = refs[:slots], refs[slots:]
    for i, ((own, near, *far), dx2) in enumerate(zip(sums_of, dxs)):
        grad = gathered_sum(own, near, far, x.shape[1])
        hat, rate = stats(x[i].astype(F32))
        out[i] = dx2[...] + norm_back(grad, vectors[4:5, :], hat, rate)


def block_out_kernel(slots, n_seq, *refs):
    size = (len(refs) - slots - 3) // slots
    sums_of = [refs[i * size : (i + 1) * size] for i in range(slots)]
    refs = refs[slots * size :]
    x2s, (limits, vectors, out) = refs[:slots], refs[slots:]
    for i, ((own, near, *far), x2) in enumerate(zip(sums_of, x2s)):
        blk = x2.shape[0]
        value = x2[...] + gathered_sum(own, near, far, blk) + vectors[3:4, :]
        good = jnp.where(positions(0, blk, n_seq, 0) < limits[i], 1.0, 0.0)
        out[i] = value * good


def far_blocks(block):
    half = lax.axis_size("seq") // 2
    return [swap(block, "seq", 2 * j) for j in range(1, half)]


def gather_seq(block):
    mine = [block] + far_blocks(block)
    return mine + [swap(part, "seq", 1) for part in mine]


def start_scatter(rest, high):
    near = swap(high, "seq", 1)
    blk = near.shape[0] - rest.shape[0]
    return near, (rest + near[blk:].astype(F32)).astype(BF16)


def end_scatter(send):
    half = lax.axis_size("seq") // 2
    blk = send.shape[0] // (half - 1)
    return [swap(send[(j - 1) * blk : j * blk], "seq", 2 * j) for j in range(1, half)]


def exchange_seq(pieces):
    return [swap(piece, "seq", r) if r else piece for r, piece in enumerate(pieces)]


class Gather:
    def __init__(self, block):
        self.inner = lax.axis_size("dp") // OUTER
        self.block = block
        self.far = swap(block, "dp", 2 * self.inner)

    def middle(self):
        self.pair = jnp.concatenate([self.block, self.far], 0)
        self.other = swap(self.pair, "dp", self.inner)
        self.first = self.spread(self.pair)

    def last(self):
        self.second = self.spread(self.other)

    def spread(self, pair):
        group = [pair]
        bit = 1
        while bit < self.inner:
            group += [swap(part, "dp", bit) for part in group]
            bit *= 2
        return group

    def all(self):
        return self.first + self.second


def gather_masks():
    inner = lax.axis_size("dp") // OUTER
    return [
        tuple(k * inner ^ j for k in pair) for pair in (ORDER[:2], ORDER[2:]) for j in range(inner)
    ]


def halve_inner(groups):
    inner = len(groups)
    groups = [list(group) for group in groups]
    bit = 1
    while bit < inner:
        for j in range(0, inner, 2 * bit):
            for part in reversed(range(len(groups[j]))):
                got = swap(groups[j + bit][part].astype(BF16), "dp", bit)
                groups[j][part] = groups[j][part].astype(F32) + got.astype(F32)
        bit *= 2
    return groups[0]


def halve_outer(near, far):
    inner = lax.axis_size("dp") // OUTER
    got = swap(far.astype(BF16), "dp", inner)
    last = swap((near[1:] + got[1:].astype(F32)).astype(BF16), "dp", 2 * inner)
    return near[0] + got[0].astype(F32) + last[0].astype(F32)


def scatter_dp(groups):
    kept = halve_inner(groups)
    if len(kept) == 1:
        kept = (kept[0][:2], kept[0][2:])
    return halve_outer(*kept)


def grad_groups(lefts, rights, name, merged=True):
    lefts, rights = list(lefts), list(rights)
    inner = lax.axis_size("dp") // OUTER
    slots = len(lefts)
    blk = lefts[0].shape[1] // (OUTER * inner)
    width = rights[0].shape[1]
    rows = lefts[0].shape[0]
    parts = 1 if merged else 2
    each = len(ORDER) // parts
    groups = []
    if blk % LANES:
        own = lax.axis_index("dp")
        whole = sum(dot_tn(a, b) for a, b in zip(lefts, rights)).reshape(-1, blk, width)
        take = lambda k: lax.dynamic_index_in_dim(whole, own ^ k, 0)
        for j in range(inner):
            got = [take(k * inner + j) for k in ORDER]
            groups.append(
                [jnp.concatenate(got[i * each : (i + 1) * each], 0) for i in range(parts)]
            )
        return groups
    for j in reversed(range(inner)):
        kind = BF16 if j else F32
        groups.append(
            call(
                functools.partial(grad_kernel, j, inner, slots),
                name,
                lefts + rights,
                [shape((each, blk, width), kind)] * parts,
                [pltpu.VMEM((4 * blk, slots * rows), BF16)],
            )
        )
    return groups[::-1]


def body(
    tokens,
    cotangent,
    item_count,
    valid_len,
    w_qkv,
    q_bias,
    v_bias,
    w_out,
    out_bias,
    w_up,
    up_bias,
    w_down,
    down_bias,
    gain_one,
    shift_one,
    gain_two,
    shift_two,
):
    slots, rows, width = tokens.shape
    n_seq = lax.axis_size("seq")
    n_dp = lax.axis_size("dp")
    inner = n_dp // OUTER
    count = n_seq * n_dp
    s = lax.axis_index("seq")
    half = n_seq // 2
    cut = half * rows
    full = n_seq * rows
    cols = width // n_seq
    heads = cols // HEAD_DIM
    piece = width // count
    hidden_all = w_up.shape[1]
    hidden = hidden_all // n_seq
    hpiece = hidden_all // count
    blocks = n_dp // n_seq
    regular = hpiece % LANES == 0 and piece % 16 == 0

    limits = jnp.where(jnp.arange(slots) < item_count[0], valid_len, 0)
    smem = pl.BlockSpec(memory_space=pltpu.SMEM)
    dma = lambda n: pltpu.SemaphoreType.DMA((n,))

    if regular:
        packed = call(
            functools.partial(pack_kernel, cols, hpiece),
            "pack",
            [w_qkv, w_up],
            [shape((piece, 3 * cols + hidden), BF16)] * n_seq,
        )
        own_qkv, own_up = call(
            place_kernel,
            "place",
            exchange_seq(packed),
            [
                shape((1, n_seq * piece, 3 * cols), BF16),
                shape((1, n_seq * piece, hidden), BF16),
            ],
        )
    else:
        split = jnp.concatenate(
            [
                w_qkv.reshape(piece, 3, n_seq, cols).transpose(2, 0, 1, 3).reshape(n_seq, piece, -1),
                w_up.reshape(piece, n_dp, n_seq, hpiece)
                .transpose(2, 0, 1, 3)
                .reshape(n_seq, piece, -1),
            ],
            -1,
        )
        packed = [lax.dynamic_index_in_dim(split, s ^ r, 0, False) for r in range(n_seq)]
        placed = jnp.zeros_like(split)
        for r, part in enumerate(exchange_seq(packed)):
            placed = lax.dynamic_update_index_in_dim(placed, part, s ^ r, 0)
        placed = placed.reshape(1, n_seq * piece, -1)
        own_qkv, own_up = placed[:, :, : 3 * cols], placed[:, :, 3 * cols :]
    rows_in = [
        v.reshape(1, -1)
        for v in (
            q_bias,
            v_bias,
            out_bias,
            down_bias,
            gain_one,
            shift_one,
            gain_two,
            shift_two,
            up_bias,
        )
    ]
    tile = max(16, 2 * n_dp)
    masks = gather_masks()
    n_parts = len(masks)
    flat_masks = [k * inner + j for j in range(inner) for k in ORDER]
    out_block = call(
        functools.partial(out_pack_kernel, tile),
        "out_pack",
        [w_out] + rows_in,
        [shape((1, tile + piece, width), BF16)],
        [pltpu.VMEM(v.shape, BF16) for v in rows_in]
        + [pltpu.VMEM((tile, width), F32), dma(N_VEC + 1)],
        [VMEM] + [ANY] * (N_VEC + 1),
    )[0]
    out_gather = Gather(out_block)
    own_qkv, own_up, out_gather.block, out_gather.far, tok = fence(
        own_qkv, own_up, out_gather.block, out_gather.far, tokens
    )
    qkv_gather = Gather(own_qkv)
    out_gather.middle()
    tok = [tok] + far_blocks(tok)
    tok.append(swap(tok[0], "seq", 1))
    out_gather.other, out_gather.first, tok[-1] = fence(
        out_gather.other, out_gather.first, tok[-1]
    )
    out_gather.last()
    qkv_gather.far, qkv_gather.block = fence(qkv_gather.far, qkv_gather.block)
    qkv_gather.middle()
    out_gather.second, tok[1:-1] = fence(out_gather.second, tok[1:-1])
    tok = tok + [swap(part, "seq", 1) for part in tok[1:-1]]
    qkv_gather.other, qkv_gather.first, out_gather.second, own_up = fence(
        qkv_gather.other, qkv_gather.first, out_gather.second, own_up
    )
    qkv_gather.last()
    up_gather = Gather(own_up)
    wout = exchange_seq(
        call(
            functools.partial(out_pieces_kernel, masks, tile, blocks),
            "out_pieces",
            out_gather.all(),
            [shape((tile + blocks * piece, width), BF16)] * n_seq,
            [pltpu.VMEM((tile, width), BF16)],
        )
    )
    wout, tok, cot = fence(wout, tok, cotangent)
    cot = [cot] + far_blocks(cot)
    cot.append(swap(cot[0], "seq", 1))
    vectors, qkv_bias, ubias = call(
        functools.partial(vector_unpack_kernel, masks, tile, n_seq, cols, hpiece),
        "vector_unpack",
        wout,
        [shape((N_VEC, width), F32), shape((1, 3 * cols), F32), shape((1, hidden), F32)],
    )
    a1 = call(
        functools.partial(norm_kernel, n_seq),
        "norm_one",
        tok + [vectors],
        [shape((full, width), BF16)] * (2 * slots),
    )
    a1, hats = list(a1[:slots]), list(a1[slots:])
    qkv_gather.second, a1 = fence(qkv_gather.second, a1)
    wqkv = qkv_gather.all()

    outs3 = [shape((rows, width), F32), shape((cut - rows, width), F32), shape((cut, width), BF16)]
    wide = pltpu.VMEM((width, 3 * cols), BF16)
    narrow = pltpu.VMEM((cols, width), BF16)
    qkvs, atts, probss, x2s, a2s, acts, slopes = [], [], [], [], [], [], []
    up_gather.far, up_gather.block, a1 = fence(up_gather.far, up_gather.block, a1)
    up_gather.middle()
    sums_in = []
    for i in range(slots):
        qkv, att, probs, own, rest, high = call(
            functools.partial(attention_kernel, masks, tile, blocks, cols, n_seq, i),
            "attention",
            [a1[i], qkv_bias, valid_len] + wqkv + wout,
            [
                shape((full, 3 * cols), BF16),
                shape((full, cols), BF16),
                shape((heads, full, full), BF16),
            ]
            + outs3,
            [wide, narrow, pltpu.VMEM((1, full), F32), dma(n_dp), dma(n_dp)],
            [VMEM] * 2 + [smem] + [ANY] * (n_parts + n_seq),
        )
        if i == 0:
            up_gather.other, up_gather.first, high, down_block, cot = fence(
                up_gather.other, up_gather.first, high, w_down[None], cot
            )
            up_gather.last()
            down_gather = Gather(down_block)
            near, send = start_scatter(rest, high)
            send, a1[1:] = fence(send, a1[1:])
            far = end_scatter(send)
        else:
            if i == 1:
                down_gather.far, up_gather.second, high, sums_in[0][2] = fence(
                    down_gather.far, up_gather.second, high, sums_in[0][2]
                )
                down_gather.middle()
            near, send = start_scatter(rest, high)
            far = end_scatter(send)
        sums_in.append([own, near, far])
        for store, value in zip((qkvs, atts, probss), (qkv, att, probs)):
            store.append(value)
    wup = up_gather.all()
    for i, (own, near, far) in enumerate(sums_in):
        x2, a2 = call(
            functools.partial(norm_two_kernel, i),
            "norm_two",
            [own, near] + far + [tokens, vectors],
            [shape((rows, width), F32), shape((rows, width), BF16)],
        )
        x2s.append(x2)
        parts = gather_seq(a2)
        a2, act, slope = call(
            functools.partial(up_kernel, masks, n_seq),
            "up",
            parts + [ubias] + wup,
            [
                shape((full, width), BF16),
                shape((full, hidden), BF16),
                shape((full, hidden), F32),
            ],
            [pltpu.VMEM((width, hidden), BF16), dma(n_dp)],
            [VMEM] * (n_seq + 1) + [ANY] * n_parts,
        )
        for store, value in zip((a2s, acts, slopes), (a2, act, slope)):
            store.append(value)
    down_gather.last()
    cot = cot + [swap(part, "seq", 1) for part in cot[1:-1]]
    dys = call(
        functools.partial(mask_kernel, n_seq),
        "mask",
        cot + [limits],
        [shape((full, width), BF16)] * slots,
        specs=[VMEM] * n_seq + [smem],
    )
    wdown = down_gather.all()
    down_groups = grad_groups(acts, dys, "grad_down")

    dus, dxs, dattns, sums2, sums_u, downs, outs_in = [], [], [], [], [], [], []
    wait = [group[0] for group in down_groups]
    for i in range(slots):
        du, own, rest, high, oown, orest, ohigh, usum = call(
            functools.partial(down_kernel, masks),
            "down",
            [after(dys[i], *wait), acts[i], slopes[i]] + wup + wdown,
            [shape((full, hidden), BF16)] + outs3 + outs3 + [shape((1, hidden), F32)],
            [
                pltpu.VMEM((width, hidden), BF16),
                pltpu.VMEM((hidden, width), BF16),
                dma(n_dp),
                dma(n_dp),
            ],
            [VMEM] * 3 + [ANY] * (2 * n_parts),
        )
        near, send = start_scatter(rest, high)
        wait = [send]
        downs.append((own, near, send))
        outs_in.append((oown, orest, ohigh))
        dus.append(du)
        sums_u.append(usum)
    for i, (own, near, send) in enumerate(downs):
        dx2, low, sums = call(
            norm_two_back_kernel,
            "norm_two_back",
            [own, near] + end_scatter(send) + [x2s[i], dys[i], vectors],
            [shape((rows, width), F32), shape((rows, width), BF16), shape((8, width), F32)],
        )
        for store, value in zip((dxs, dattns, sums2), (dx2, low, sums)):
            store.append(value)
    up_groups = grad_groups(a2s, dus, "grad_up")
    parts = [gather_seq(v) for v in dattns]
    dqkvs, sums_q, sums1, backs = [], [], [], []
    wait = [group[0] for group in up_groups]
    for i in range(slots):
        dqkv, own, rest, high, qsum, sums = call(
            functools.partial(attention_back_kernel, masks, tile, blocks, cols, n_seq),
            "attention_back",
            [after(parts[i][0], *wait)]
            + parts[i][1:]
            + [qkvs[i], probss[i], hats[i]]
            + wqkv
            + wout,
            [shape((full, 3 * cols), BF16)]
            + outs3
            + [shape((1, 3 * cols), F32), shape((8, width), F32)],
            [
                wide,
                narrow,
                pltpu.VMEM((full, width), BF16),
                pltpu.VMEM((full, cols), BF16),
                pltpu.VMEM((LANES, full), F32),
                pltpu.VMEM((LANES, full), F32),
                dma(n_dp),
                dma(n_dp),
            ],
            [VMEM] * (n_seq + 3) + [ANY] * (n_parts + n_seq),
        )
        near, send = start_scatter(rest, high)
        wait = [send]
        backs.append([own, near, send])
        for store, value in zip((dqkvs, sums_q, sums1), (dqkv, qsum, sums)):
            store.append(value)
    qkv_groups = grad_groups(a1, dqkvs, "grad_qkv", merged=False)
    ready = qkv_groups[-1][0]
    g_out = exchange_seq(
        call(
            functools.partial(grad_out_kernel, flat_masks, tile, cols, hpiece, slots, n_seq),
            "grad_out",
            [after(atts[0], ready)]
            + atts[1:]
            + sum(parts, [])
            + sums1
            + sums2
            + sums_q
            + sums_u,
            [shape((tile + blocks * piece, width), BF16)] * n_seq,
            [pltpu.VMEM((full, width), BF16), pltpu.VMEM((N_VEC, width), F32)],
        )
    )
    block_out_in = []
    for own, rest, high in outs_in:
        near, send = start_scatter(rest, after(high, ready))
        block_out_in += [own, near] + end_scatter(send)
    block_out = call(
        functools.partial(block_out_kernel, slots, n_seq),
        "block_out",
        block_out_in + x2s + [limits, vectors],
        [shape((slots, rows, width), F32)],
        specs=[VMEM] * (len(block_out_in) + slots) + [smem, VMEM],
    )[0]
    back_in = []
    for own, near, send in backs:
        back_in += [own, near] + end_scatter(send)
    grad_tokens = call(
        functools.partial(norm_one_back_kernel, slots),
        "norm_one_back",
        back_in + dxs + [tokens, vectors],
        [shape((slots, rows, width), F32)],
    )[0]
    g_wdown = scatter_dp(down_groups)
    g_wup = scatter_dp(up_groups)
    g_out = call(
        functools.partial(grad_out_groups_kernel, flat_masks, tile),
        "grad_out_groups",
        g_out,
        [shape((len(ORDER), VEC_ROWS + piece, width), BF16 if j else F32) for j in range(inner)],
    )
    g_wout, *vecs = call(
        out_final_kernel,
        "out_final",
        [scatter_dp([[part] for part in g_out])],
        [shape((piece, width), F32)]
        + [shape((1, piece), F32)] * N_VEC
        + [shape((1, hpiece), F32)],
    )
    g_wqkv = scatter_dp(qkv_groups)

    def to_owners(grad):
        parts = grad.astype(BF16).reshape(n_seq, piece, -1)
        return exchange_seq(
            [lax.dynamic_index_in_dim(parts, s ^ r, 0, False) for r in range(n_seq)]
        )

    qkv_parts, up_parts = to_owners(g_wqkv), to_owners(g_wup)
    if regular:
        g_wqkv, g_wup = call(
            functools.partial(unplace_kernel, cols, hpiece),
            "unplace",
            qkv_parts + up_parts,
            [shape((piece, 3 * width), F32), shape((piece, hidden_all), F32)],
        )
    else:
        placed = []
        for parts in (qkv_parts, up_parts):
            out = jnp.zeros((n_seq,) + parts[0].shape, BF16)
            for r, part in enumerate(parts):
                out = lax.dynamic_update_index_in_dim(out, part, s ^ r, 0)
            placed.append(out.astype(F32))
        g_wqkv = placed[0].reshape(n_seq, piece, 3, cols).transpose(1, 2, 0, 3).reshape(piece, -1)
        g_wup = (
            placed[1].reshape(n_seq, piece, n_dp, hpiece).transpose(1, 2, 0, 3).reshape(piece, -1)
        )

    vecs = [v.reshape(-1) for v in vecs]
    return (
        block_out,
        grad_tokens,
        g_wqkv,
        vecs[0],
        vecs[1],
        g_wout,
        vecs[2],
        g_wup,
        vecs[8],
        g_wdown,
        vecs[3],
        vecs[4],
        vecs[5],
        vecs[6],
        vecs[7],
    )


def solution(mesh):
    both = ("dp", "seq")
    act = P("dp", "seq", None)
    mat = P(both, None)
    vec = P(both)
    return jax.shard_map(
        body,
        mesh=mesh,
        in_specs=(act, act, P("dp"), P("dp"), mat, vec, vec, mat, vec, mat, vec, mat)
        + (vec,) * 5,
        out_specs=(act, act, mat, vec, vec, mat, vec, mat, vec, mat) + (vec,) * 5,
        check_vma=False,
    )
```

```python
import functools

import jax
import jax.numpy as jnp
from jax import lax
from jax.experimental import pallas as pl
from jax.experimental.pallas import tpu as pltpu
from jax.sharding import PartitionSpec as P

HEAD_DIM = 64
LANES = 128
EPSILON = 1e-06
F32 = jnp.float32
BF16 = jnp.bfloat16
OUTER = 4
ORDER = (0, 2, 1, 3)
VMEM = pl.BlockSpec(memory_space=pltpu.VMEM)
ANY = pl.BlockSpec(memory_space=pl.ANY)
HBM = pl.BlockSpec(memory_space=pltpu.HBM)
SMEM = pl.BlockSpec(memory_space=pltpu.SMEM)
LIMIT = 14 * 1024 * 1024
WHOLE = 60 * 1024 * 1024
SOFTMAX_RATE = HEAD_DIM**-0.5 * 1.4426950408889634
N_VEC = 8
VEC_ROWS = 8


def dot(left, right):
    return jnp.dot(left, right, preferred_element_type=F32)


def dot_nt(left, right):
    return lax.dot_general(left, right, (((1,), (1,)), ((), ())), preferred_element_type=F32)


def dot_tn(left, right):
    return lax.dot_general(left, right, (((0,), (0,)), ((), ())), preferred_element_type=F32)


def swap(values, axis, mask):
    size = lax.axis_size(axis)
    return lax.ppermute(values, axis, [(i, i ^ mask) for i in range(size)])


def shape(dims, kind):
    return jax.ShapeDtypeStruct(tuple(dims), kind)


def after(values, *others):
    return lax.optimization_barrier((values,) + others)[0]


def fence(*values):
    return lax.optimization_barrier(values)


def call(kernel, name, ins, outs, scratch=(), specs=None, limit=LIMIT):
    return pl.pallas_call(
        kernel,
        name=name,
        out_shape=tuple(outs),
        in_specs=specs or [VMEM] * len(ins),
        out_specs=tuple([VMEM] * len(outs)),
        scratch_shapes=list(scratch),
        compiler_params=pltpu.CompilerParams(vmem_limit_bytes=limit),
        cost_estimate=pl.CostEstimate(
            flops=0, bytes_accessed=0, transcendentals=0
        ),
    )(*ins)


def aligned(index, size):
    return pl.multiple_of(index * size, size)


def start_copies(jobs, scratch, sems):
    copies = []
    for src, block, rows in jobs:
        copy = pltpu.make_async_copy(
            src, scratch.at[pl.ds(aligned(block, rows), rows)], sems.at[len(copies)]
        )
        copy.start()
        copies.append(copy)
    return copies


def dp_jobs(refs, masks):
    own = lax.axis_index("dp")
    jobs = []
    for ref, group in zip(refs, masks):
        for i, mask in enumerate(group):
            jobs.append((ref.at[i], own ^ mask, ref.shape[1]))
    return jobs


def out_jobs(refs, tile, blocks):
    own = lax.axis_index("seq")
    size = len(refs)
    rows = (refs[0].shape[0] - tile) // blocks
    return [
        (ref.at[pl.ds(tile + b * rows, rows)], b * size + (own ^ r), rows)
        for r, ref in enumerate(refs)
        for b in range(blocks)
    ]


def pack_kernel(cols, hpiece, wqkv, wup, *outs):
    own = lax.axis_index("seq")
    size = len(outs)
    hidden = wup.shape[1] // size
    width = wqkv.shape[1] // 3
    for r, out in enumerate(outs):
        dest = own ^ r
        for i in range(3):
            at = pl.multiple_of(dest * cols + i * width, LANES)
            out[:, i * cols : (i + 1) * cols] = wqkv[:, pl.ds(at, cols)]
        for i in range(hidden // hpiece):
            at = pl.multiple_of((i * size + dest) * hpiece, LANES)
            start = 3 * cols + i * hpiece
            out[:, start : start + hpiece] = wup[:, pl.ds(at, hpiece)]


def place_kernel(*refs):
    size = len(refs) - 2
    qkv, up = refs[size:]
    own = lax.axis_index("seq")
    cut = qkv.shape[2]
    for r in range(size):
        rows = refs[r].shape[0]
        at = pl.ds(aligned(own ^ r, rows), rows)
        qkv[0, at, :] = refs[r][:, :cut]
        up[0, at, :] = refs[r][:, cut:]


def owners_kernel(near, got, last, *outs):
    own = lax.axis_index("seq")
    rows = outs[0].shape[0]
    for r, out in enumerate(outs):
        at = pl.ds(aligned(own ^ r, rows), rows)
        out[...] = (
            near[0, at, :].astype(F32) + got[0, at, :].astype(F32) + last[0, at, :].astype(F32)
        ).astype(BF16)


def unplace_kernel(cols, hpiece, *refs):
    size = (len(refs) - 2) // 2
    qkv, up = refs[2 * size :]
    own = lax.axis_index("seq")
    width = qkv.shape[1] // 3
    for r in range(size):
        src = own ^ r
        part = refs[r]
        for i in range(3):
            at = pl.multiple_of(src * cols + i * width, LANES)
            qkv[:, pl.ds(at, cols)] = part[:, i * cols : (i + 1) * cols].astype(F32)
        part = refs[size + r]
        for i in range(part.shape[1] // hpiece):
            at = pl.multiple_of((i * size + src) * hpiece, LANES)
            up[:, pl.ds(at, hpiece)] = part[:, i * hpiece : (i + 1) * hpiece].astype(F32)


def out_pack_kernel(tile, wout, *refs):
    n = N_VEC + 1
    vecs, out, landed, scratch, sems = refs[:n], refs[n], refs[n + 1 : -2], refs[-2], refs[-1]
    copies = [pltpu.make_async_copy(v, l, sems.at[i]) for i, (v, l) in enumerate(zip(vecs, landed))]
    for copy in copies:
        copy.start()
    out[0, tile:, :] = wout[...]
    scratch[...] = jnp.zeros_like(scratch)
    for copy in copies:
        copy.wait()
    for i, vec in enumerate(landed):
        row, lane = (0, i * LANES) if i < N_VEC else (1, 0)
        scratch[row : row + 1, lane : lane + vec.shape[0]] = vec[...].astype(F32)[None, :]
    out[0, :tile, :] = scratch[...].astype(BF16)


def out_pieces_kernel(masks, tile, blocks, *refs):
    n = len(masks)
    outs, mixed = refs[n:-1], refs[-1]
    d = lax.axis_index("dp")
    s = lax.axis_index("seq")
    flat = [(i, j) for i, group in enumerate(masks) for j in range(len(group))]
    mask_of = [mask for group in masks for mask in group]
    total = None
    for n, (i, j) in enumerate(flat):
        part = refs[i][j, :tile, :].astype(F32)
        part = pltpu.roll(part, 2 * n, 0) if n else part
        total = part if total is None else total + part
    mixed[...] = total.astype(BF16)
    piece = refs[0].shape[1] - tile
    for r, out in enumerate(outs):
        out[:tile, :] = mixed[...]
        for b in range(blocks):
            want = d ^ ((s ^ r) * blocks + b)
            for (i, j), mask in zip(flat, mask_of):

                @pl.when(want == mask)
                def _(out=out, b=b, i=i, j=j):
                    start = tile + b * piece
                    out[start : start + piece, :] = refs[i][j, tile:, :]


def vector_unpack_kernel(masks, tile, n_seq, cols, hpiece, *refs):
    parts, (vectors, qkv_bias, ubias) = refs[:n_seq], refs[n_seq:]
    width = vectors.shape[1]
    hidden = ubias.shape[1]
    mask_of = [mask for group in masks for mask in group]
    piece = width // (n_seq * len(mask_of))
    s = lax.axis_index("seq")
    d = lax.axis_index("dp")
    row = lax.broadcasted_iota(jnp.int32, (tile, 1), 0)
    dist = jnp.zeros_like(row)
    for n, mask in enumerate(mask_of):
        dist = jnp.where(row // 2 == n, mask, dist)
    source = d ^ dist
    lane = lax.broadcasted_iota(jnp.int32, (LANES, width), 1)
    sub = lax.broadcasted_iota(jnp.int32, (LANES, width), 0)
    spread = jnp.where(lane % piece == sub, 1.0, 0.0).astype(BF16)
    target = lax.broadcasted_iota(jnp.int32, (1, width), 1) // piece
    even = row % 2 == 0
    for i in range(N_VEC):
        total = None
        for r, part in enumerate(parts):
            tiled = dot(part[:tile, i * LANES : (i + 1) * LANES], spread)
            here = even & (source * n_seq + (s ^ r) == target)
            tiled = jnp.sum(jnp.where(here, tiled, 0.0), axis=0, keepdims=True)
            total = tiled if total is None else total + tiled
        vectors[i : i + 1, :] = total
    lane = lax.broadcasted_iota(jnp.int32, (LANES, hidden), 1)
    sub = lax.broadcasted_iota(jnp.int32, (LANES, hidden), 0)
    spread = jnp.where(lane % hpiece == sub, 1.0, 0.0).astype(BF16)
    target = lax.broadcasted_iota(jnp.int32, (1, hidden), 1) // hpiece
    tiled = dot(parts[0][:tile, :LANES], spread)
    here = (row % 2 == 1) & (source == target)
    ubias[...] = jnp.sum(jnp.where(here, tiled, 0.0), axis=0, keepdims=True)
    at = pl.ds(pl.multiple_of(s * cols, LANES), cols)
    qkv_bias[...] = jnp.zeros_like(qkv_bias)
    qkv_bias[:, :cols] = vectors[0:1, at]
    qkv_bias[:, 2 * cols :] = vectors[1:2, at]


def positions(block, rows, n_seq, axis):
    half = n_seq // 2
    owner = lax.axis_index("seq") ^ (2 * (block % half) + block // half)
    dims = (rows, 1) if axis == 0 else (1, rows)
    return owner * rows + lax.broadcasted_iota(jnp.int32, dims, axis)


def attention_kernel(masks, tile, blocks, cols, n_seq, item, *refs):
    first = item == 0
    a1, bias, lens = refs[:3]
    n = len(masks) if first else 1
    pieces, outs = refs[3 : 3 + n], refs[3 + n : 3 + n + (n_seq if first else 1)]
    refs = refs[3 + n + len(outs) :]
    if first:
        qkv, att, probs, own, rest, high, wqkv, wout, ok, sems, out_sems = refs
    else:
        qkv, att, probs, own, rest, high, ok = refs
        (wqkv,), (wout,) = pieces, outs
    rows = a1.shape[0]
    cut = rows // 2
    blk = own.shape[0]
    copies, out_copies = [], []
    if first:
        copies = start_copies(dp_jobs(pieces, masks), wqkv, sems)
        out_copies = start_copies(out_jobs(outs, tile, blocks), wout, out_sems)
    for q in range(n_seq):
        good = positions(q, blk, n_seq, 1) < lens[item]
        ok[:, q * blk : (q + 1) * blk] = jnp.where(good, 0.0, -1e30)
    for copy in copies:
        copy.wait()
    for i in range(3):
        part = slice(i * cols, (i + 1) * cols)
        qkv[:, part] = (dot(a1[...], wqkv[:, part]) + bias[:, part]).astype(BF16)
    step_rows = min(256, rows)
    lane = lax.broadcasted_iota(jnp.int32, (1, LANES), 1)
    sides = [(lane < HEAD_DIM), (lane >= HEAD_DIM)]
    for pair in range(cols // LANES):
        at = slice(pair * LANES, (pair + 1) * LANES)
        keys = qkv[:, cols + pair * LANES : cols + (pair + 1) * LANES]
        vals = qkv[:, 2 * cols + pair * LANES : 2 * cols + (pair + 1) * LANES]
        split = [jnp.where(side, vals, jnp.zeros_like(vals)) for side in sides]

        def step(block, carry, pair=pair, at=at, keys=keys, split=split):
            place = pl.ds(aligned(block, step_rows), step_rows)
            query = qkv[place, at]
            total = None
            for h in range(2):
                q = jnp.where(sides[h], query, jnp.zeros_like(query))
                scores = dot_nt(q, keys) + ok[...]
                peak = jnp.max(scores, axis=-1, keepdims=True)
                expo = jnp.exp2((scores - peak) * SOFTMAX_RATE)
                rate = 1.0 / jnp.sum(expo, axis=-1, keepdims=True)
                low = (expo * rate).astype(BF16)
                probs[2 * pair + h, place, :] = low
                out = dot(low, split[h])
                total = out if total is None else total + out
            att[place, at] = total.astype(BF16)
            return carry

        lax.fori_loop(0, rows // step_rows, step, 0)
    for copy in out_copies:
        copy.wait()
    high[...] = dot(att[cut:, :], wout[...]).astype(BF16)
    own[...] = dot(att[:blk, :], wout[...])
    rest[...] = dot(att[blk:cut, :], wout[...])


def attention_back_kernel(cols, n_seq, *refs):
    parts = refs[:n_seq]
    qkv, probs, hat, wqkv, wout = refs[n_seq : n_seq + 5]
    dqkv, own, rest, high, sums, sums_one, grad, datt, dkt, dvt = refs[n_seq + 5 :]
    rows = dqkv.shape[0]
    cut = rows // 2
    blk = own.shape[0]
    for i, part in enumerate(parts):
        grad[i * blk : (i + 1) * blk, :] = part[...]
    datt[...] = dot_nt(grad[...], wout[...]).astype(BF16)
    step_rows = min(256, rows)
    lane = lax.broadcasted_iota(jnp.int32, (1, LANES), 1)
    sides = [(lane < HEAD_DIM), (lane >= HEAD_DIM)]
    scale = HEAD_DIM**-0.5
    for pair in range(cols // LANES):
        at = slice(pair * LANES, (pair + 1) * LANES)
        at_k = slice(cols + pair * LANES, cols + (pair + 1) * LANES)
        at_v = slice(2 * cols + pair * LANES, 2 * cols + (pair + 1) * LANES)
        keys = qkv[:, at_k]
        vals = qkv[:, at_v]
        split = [jnp.where(side, keys, jnp.zeros_like(keys)) for side in sides]
        dkt[...] = jnp.zeros_like(dkt)
        dvt[...] = jnp.zeros_like(dvt)

        def step(block, carry, pair=pair, at=at, vals=vals, split=split):
            place = pl.ds(aligned(block, step_rows), step_rows)
            gatt = datt[place, at]
            query = qkv[place, at]
            gatt_t = gatt.T
            query_t = query.T
            total = None
            for h in range(2):
                g = jnp.where(sides[h], gatt, jnp.zeros_like(gatt))
                gp = dot_nt(g, vals)
                low = probs[2 * pair + h, place, :]
                p = low.astype(F32)
                mean = jnp.sum(gp * p, axis=-1, keepdims=True)
                gs = (p * (gp - mean)).astype(BF16)
                half = slice(h * HEAD_DIM, (h + 1) * HEAD_DIM)
                dvt[half, :] += dot(gatt_t[half, :], low)
                dkt[half, :] += dot(query_t[half, :], gs)
                out = dot(gs, split[h])
                total = out if total is None else total + out
            dqkv[place, at] = (total * scale).astype(BF16)
            return carry

        lax.fori_loop(0, rows // step_rows, step, 0)
        dqkv[:, at_k] = (dkt[...].T * scale).astype(BF16)
        dqkv[:, at_v] = dvt[...].T.astype(BF16)
    sums[...] = jnp.sum(dqkv[...].astype(F32), axis=0, keepdims=True)
    sums_one[...] = jnp.zeros_like(sums_one)

    def last(block, carry):
        at = pl.ds(aligned(block, 256), 256)
        value = dot_nt(dqkv[...], wqkv[at, :])
        own[:, at] = value[:blk]
        rest[:, at] = value[blk:cut]
        high[:, at] = value[cut:].astype(BF16)
        sums_one[0:1, at] = jnp.sum(value * hat[:, at].astype(F32), axis=0, keepdims=True)
        sums_one[1:2, at] = jnp.sum(value, axis=0, keepdims=True)
        return carry

    lax.fori_loop(0, wqkv.shape[0] // 256, last, 0)


def up_kernel(masks, n_seq, item, *refs):
    first = item == 0
    n = len(masks) if first else 1
    parts, bias = refs[:n_seq], refs[n_seq]
    pieces = refs[n_seq + 1 : n_seq + 1 + n]
    if first:
        a2, act, slope, wup, sems = refs[n_seq + 1 + n :]
    else:
        a2, act, slope = refs[n_seq + 1 + n :]
        (wup,) = pieces
    blk = parts[0].shape[0]
    rows = a2.shape[0]
    width = min(256, act.shape[1])
    copies = start_copies(dp_jobs(pieces, masks), wup, sems) if first else []
    for i, part in enumerate(parts):
        a2[i * blk : (i + 1) * blk, :] = part[...]
    for copy in copies:
        copy.wait()
    half = min(256, rows)
    for i in range(rows // half):
        place = slice(i * half, (i + 1) * half)

        def step(block, carry, place=place):
            at = pl.ds(aligned(block, width), width)
            u = dot(a2[place, :], wup[:, at]) + bias[:, at]
            cdf = 0.5 * (1.0 + lax.erf(u * 0.7071067811865476))
            bell = jnp.exp2(u * u * -0.7213475204444817) * 0.3989422804014327
            act[place, at] = (u * cdf).astype(BF16)
            slope[place, at] = cdf + u * bell
            return carry

        lax.fori_loop(0, act.shape[1] // width, step, 0)


def down_kernel(masks, item, *refs):
    n = len(masks) if item == 0 else 1
    dy, act, slope, wup = refs[:4]
    downs = refs[4 : 4 + n]
    if item == 0:
        du, own, rest, high, oown, orest, ohigh, sums, wdown, sems = refs[4 + n :]
        for copy in start_copies(dp_jobs(downs, masks), wdown, sems):
            copy.wait()
    else:
        du, own, rest, high, oown, orest, ohigh, sums = refs[4 + n :]
        (wdown,) = downs
    rows = dy.shape[0]
    cut = rows // 2
    blk = own.shape[0]
    hidden = act.shape[1]
    width = min(256, hidden)

    def first(block, carry):
        at = pl.ds(aligned(block, width), width)
        value = (slope[:, at] * dot_nt(dy[...], wdown[at, :])).astype(BF16)
        du[:, at] = value
        sums[:, at] = jnp.sum(value.astype(F32), axis=0, keepdims=True)
        return carry

    lax.fori_loop(0, hidden // width, first, 0)

    def second(block, carry):
        at = pl.ds(aligned(block, 256), 256)
        value = dot_nt(du[...], wup[at, :])
        own[:, at] = value[:blk]
        rest[:, at] = value[blk:cut]
        high[:, at] = value[cut:].astype(BF16)
        value = dot(act[...], wdown[:, at])
        oown[:, at] = value[:blk]
        orest[:, at] = value[blk:cut]
        ohigh[:, at] = value[cut:].astype(BF16)
        return carry

    lax.fori_loop(0, wup.shape[0] // 256, second, 0)


def grad_kernel(j, inner, slots, *refs):
    lefts, rights = refs[:slots], refs[slots : 2 * slots]
    *outs, turned = refs[2 * slots :]
    rows = lefts[0].shape[0]
    each, blk = outs[0].shape[:2]
    own = lax.axis_index("dp")
    for n, k in enumerate(ORDER):
        at = pl.ds(aligned(own ^ (k * inner + j), blk), blk)
        for i, left in enumerate(lefts):
            turned[n * blk : (n + 1) * blk, i * rows : (i + 1) * rows] = left[:, at].T
    width = min(256, outs[0].shape[2])

    def step(block, carry):
        at = pl.ds(aligned(block, width), width)
        total = None
        for i, right in enumerate(rights):
            out = dot(turned[:, i * rows : (i + 1) * rows], right[:, at])
            total = out if total is None else total + out
        for n in range(len(ORDER)):
            out = outs[n // each]
            out[n % each, :, at] = total[n * blk : (n + 1) * blk].astype(out.dtype)
        return carry

    lax.fori_loop(0, outs[0].shape[2] // width, step, 0)


def grad_out_kernel(masks, tile, cols, hpiece, slots, n_seq, *refs):
    take = lambda n: (refs[:n], refs[n:])
    lefts, refs = take(slots)
    rights, refs = take(slots * n_seq)
    sums1, refs = take(slots)
    sums2, refs = take(slots)
    sums_q, refs = take(slots)
    sums_u, refs = take(slots)
    outs, (scratch, wide) = take(n_seq)[0], refs[n_seq:]
    width = wide.shape[1]
    s = lax.axis_index("seq")
    d = lax.axis_index("dp")
    total = lambda refs: functools.reduce(lambda a, b: a + b, [ref[...] for ref in refs])
    q, u = total(sums_q), total(sums_u)
    one, two = total(sums1), total(sums2)
    wide[...] = jnp.zeros_like(wide)
    at = pl.ds(pl.multiple_of(s * cols, LANES), cols)
    wide[0:1, at] = q[:, :cols]
    wide[1:2, at] = q[:, 2 * cols :]
    wide[2:4, :] = two[:2]
    wide[4:6, :] = one[:2]
    wide[6:8, :] = two[2:4]
    piece = width // (n_seq * len(masks))
    row = lax.broadcasted_iota(jnp.int32, (n_seq * tile, 1), 0)
    near = row % tile
    dist = jnp.zeros_like(row)
    for n, mask in enumerate(masks):
        dist = jnp.where(near // 2 == n, mask, dist)
    dest = (d ^ dist) * n_seq + (s ^ (row // tile))
    dest = jnp.where(near % 2 == 0, dest, -1)
    spread = jnp.where(
        lax.broadcasted_iota(jnp.int32, (width, LANES), 0) % piece
        == lax.broadcasted_iota(jnp.int32, (width, LANES), 1),
        1.0,
        0.0,
    ).astype(BF16)
    here = lax.broadcasted_iota(jnp.int32, (1, width), 1) // piece == dest
    vecs = []
    for i in range(N_VEC):
        vecs.append(dot(jnp.where(here, wide[i : i + 1, :], 0.0).astype(BF16), spread))
    hidden = u.shape[1]
    spread = jnp.where(
        lax.broadcasted_iota(jnp.int32, (hidden, LANES), 0) % hpiece
        == lax.broadcasted_iota(jnp.int32, (hidden, LANES), 1),
        1.0,
        0.0,
    ).astype(BF16)
    dest = jnp.where(near % 2 == 1, d ^ dist, -1)[:tile]
    here = lax.broadcasted_iota(jnp.int32, (1, hidden), 1) // hpiece == dest
    long = dot(jnp.where(here, u, 0.0).astype(BF16), spread)
    for r, out in enumerate(outs):
        for i, vec in enumerate(vecs):
            value = vec[r * tile : (r + 1) * tile]
            if r == 0 and i == 0:
                value = value + long
            out[:tile, i * LANES : (i + 1) * LANES] = value.astype(BF16)
    rows = rights[0].shape[0]
    blocks = (outs[0].shape[0] - tile) // piece
    grad = None
    for i, left in enumerate(lefts):
        for q in range(n_seq):
            scratch[q * rows : (q + 1) * rows, :] = rights[i * n_seq + q][...]
        part = dot_tn(left[...], scratch[...])
        grad = part if grad is None else grad + part
    grad = grad.astype(BF16)
    for other in range(n_seq):
        for r in range(n_seq):

            @pl.when(s ^ r == other)
            def _(other=other, r=r):
                for b in range(blocks):
                    at = (b * n_seq + other) * piece
                    start = tile + b * piece
                    outs[r][start : start + piece, :] = grad[at : at + piece]


def grad_out_groups_kernel(masks, tile, *refs):
    inner = len(masks) // len(ORDER)
    pieces, outs = refs[:-inner], refs[-inner:]
    size = len(pieces)
    head = VEC_ROWS
    rows = outs[0].shape[1] - head
    blocks = (pieces[0].shape[0] - tile) // rows
    d = lax.axis_index("dp")
    s = lax.axis_index("seq")
    total = None
    for piece in pieces:
        part = piece[:tile, :].astype(F32)
        total = part if total is None else total + part
    row = lax.broadcasted_iota(jnp.int32, (tile, 1), 0)
    for n, mask in enumerate(masks):
        out = outs[n // len(ORDER)]
        i = n % len(ORDER)
        value = pltpu.roll(total, tile - 2 * n, 0) if n else total
        out[i, :head, :] = jnp.where(row < 2, value, 0.0)[:head].astype(out.dtype)
        for r in range(size):
            for b in range(blocks):

                @pl.when(d ^ mask == (s ^ r) * blocks + b)
                def _(out=out, i=i, r=r, b=b):
                    start = tile + b * rows
                    out[i, head:, :] = pieces[r][start : start + rows, :].astype(out.dtype)


def out_final_kernel(total, grad, *vecs):
    grad[...] = total[VEC_ROWS:, :]
    for i, vec in enumerate(vecs[:-1]):
        vec[...] = total[0:1, i * LANES : i * LANES + vec.shape[1]]
    vecs[-1][...] = total[1:2, : vecs[-1].shape[1]]


def gathered_sum(own, near, far, blk):
    total = own[...] + near[:blk, :].astype(F32)
    for ref in far:
        total = total + ref[...].astype(F32)
    return total


def stats(values):
    center = values - jnp.mean(values, axis=-1, keepdims=True)
    rate = lax.rsqrt(jnp.mean(center * center, axis=-1, keepdims=True) + EPSILON)
    return center * rate, rate


def norm_kernel(n_seq, *refs):
    parts, vectors, outs = refs[:n_seq], refs[n_seq], refs[n_seq + 1 :]
    rows = parts[0].shape[1]
    outs, hats = outs[: len(outs) // 2], outs[len(outs) // 2 :]
    for i, (out, kept) in enumerate(zip(outs, hats)):
        for q, part in enumerate(parts):
            hat, _ = stats(part[i].astype(F32))
            kept[q * rows : (q + 1) * rows, :] = hat.astype(BF16)
            out[q * rows : (q + 1) * rows, :] = (
                hat * vectors[4:5, :] + vectors[5:6, :]
            ).astype(BF16)


def mask_kernel(n_seq, *refs):
    parts, limits, outs = refs[:n_seq], refs[n_seq], refs[n_seq + 1 :]
    rows = parts[0].shape[1]
    for i, out in enumerate(outs):
        for q, part in enumerate(parts):
            good = jnp.where(positions(q, rows, n_seq, 0) < limits[i], 1.0, 0.0)
            out[q * rows : (q + 1) * rows, :] = (part[i].astype(F32) * good).astype(BF16)


def norm_two_kernel(item, own, near, *refs):
    *far, x, vectors, x2, a2 = refs
    value = x[item].astype(F32) + (
        gathered_sum(own, near, far, x2.shape[0]) + vectors[2:3, :]
    )
    x2[...] = value
    hat, _ = stats(value)
    a2[...] = (hat * vectors[6:7, :] + vectors[7:8, :]).astype(BF16)


def norm_back(grad, gain, hat, rate):
    scaled = grad * gain
    return rate * (
        scaled
        - jnp.mean(scaled, axis=-1, keepdims=True)
        - hat * jnp.mean(scaled * hat, axis=-1, keepdims=True)
    )


def norm_two_back_kernel(own, near, *refs):
    *far, x2, dy, vectors, dx2, low, sums = refs
    grad = gathered_sum(own, near, far, x2.shape[0])
    hat, rate = stats(x2[...])
    rows = dy[: x2.shape[0], :].astype(F32)
    value = rows + norm_back(grad, vectors[6:7, :], hat, rate)
    dx2[...] = value
    rounded = value.astype(BF16)
    low[...] = rounded
    sums[0:1, :] = jnp.sum(rounded.astype(F32), axis=0, keepdims=True)
    sums[1:2, :] = jnp.sum(rows, axis=0, keepdims=True)
    sums[2:3, :] = jnp.sum(grad * hat, axis=0, keepdims=True)
    sums[3:4, :] = jnp.sum(grad, axis=0, keepdims=True)
    sums[4:8, :] = jnp.zeros_like(sums[4:8, :])


def norm_one_back_kernel(slots, *refs):
    size = (len(refs) - slots - 3) // slots
    sums_of = [refs[i * size : (i + 1) * size] for i in range(slots)]
    refs = refs[slots * size :]
    dxs, (x, vectors, out) = refs[:slots], refs[slots:]
    for i, ((own, near, *far), dx2) in enumerate(zip(sums_of, dxs)):
        grad = gathered_sum(own, near, far, x.shape[1])
        hat, rate = stats(x[i].astype(F32))
        out[i] = dx2[...] + norm_back(grad, vectors[4:5, :], hat, rate)


def block_out_kernel(slots, n_seq, *refs):
    size = (len(refs) - slots - 3) // slots
    sums_of = [refs[i * size : (i + 1) * size] for i in range(slots)]
    refs = refs[slots * size :]
    x2s, (limits, vectors, out) = refs[:slots], refs[slots:]
    for i, ((own, near, *far), x2) in enumerate(zip(sums_of, x2s)):
        blk = x2.shape[0]
        value = x2[...] + gathered_sum(own, near, far, blk) + vectors[3:4, :]
        good = jnp.where(positions(0, blk, n_seq, 0) < limits[i], 1.0, 0.0)
        out[i] = value * good


def far_blocks(block):
    half = lax.axis_size("seq") // 2
    return [swap(block, "seq", 2 * j) for j in range(1, half)]


def gather_seq(block):
    mine = [block] + far_blocks(block)
    return mine + [swap(part, "seq", 1) for part in mine]


def start_scatter(rest, high):
    near = swap(high, "seq", 1)
    blk = near.shape[0] - rest.shape[0]
    return near, (rest + near[blk:].astype(F32)).astype(BF16)


def end_scatter(send):
    half = lax.axis_size("seq") // 2
    blk = send.shape[0] // (half - 1)
    return [swap(send[(j - 1) * blk : j * blk], "seq", 2 * j) for j in range(1, half)]


def exchange_seq(pieces):
    return [swap(piece, "seq", r) if r else piece for r, piece in enumerate(pieces)]


class Gather:
    def __init__(self, block):
        self.inner = lax.axis_size("dp") // OUTER
        self.block = block
        self.far = swap(block, "dp", 2 * self.inner)

    def middle(self):
        self.pair = jnp.concatenate([self.block, self.far], 0)
        self.other = swap(self.pair, "dp", self.inner)
        self.first = self.spread(self.pair)

    def last(self):
        self.second = self.spread(self.other)

    def spread(self, pair):
        group = [pair]
        bit = 1
        while bit < self.inner:
            group += [swap(part, "dp", bit) for part in group]
            bit *= 2
        return group

    def all(self):
        return self.first + self.second


def gather_masks():
    inner = lax.axis_size("dp") // OUTER
    return [
        tuple(k * inner ^ j for k in pair) for pair in (ORDER[:2], ORDER[2:]) for j in range(inner)
    ]


def halve_inner(groups):
    inner = len(groups)
    groups = [list(group) for group in groups]
    bit = 1
    while bit < inner:
        for j in range(0, inner, 2 * bit):
            for part in reversed(range(len(groups[j]))):
                got = swap(groups[j + bit][part].astype(BF16), "dp", bit)
                groups[j][part] = groups[j][part].astype(F32) + got.astype(F32)
        bit *= 2
    return groups[0]


def halve_outer(near, far):
    inner = lax.axis_size("dp") // OUTER
    got = swap(far.astype(BF16), "dp", inner)
    last = swap((near[1:] + got[1:].astype(F32)).astype(BF16), "dp", 2 * inner)
    return near, got, last


def scatter_dp(groups):
    kept = halve_inner(groups)
    if len(kept) == 1:
        kept = (kept[0][:2], kept[0][2:])
    return halve_outer(*kept)


def total_of(parts):
    return functools.reduce(lambda a, b: a + b, [part[0].astype(F32) for part in parts])


def grad_groups(lefts, rights, name, merged=True, later=None):
    lefts, rights = list(lefts), list(rights)
    inner = lax.axis_size("dp") // OUTER
    slots = len(lefts)
    blk = lefts[0].shape[1] // (OUTER * inner)
    width = rights[0].shape[1]
    rows = lefts[0].shape[0]
    parts = 1 if merged else 2
    each = len(ORDER) // parts
    groups = []
    if blk % LANES:
        own = lax.axis_index("dp")
        whole = sum(dot_tn(a, b) for a, b in zip(lefts, rights)).reshape(-1, blk, width)
        take = lambda k: lax.dynamic_index_in_dim(whole, own ^ k, 0)
        for j in range(inner):
            got = [take(k * inner + j) for k in ORDER]
            groups.append(
                [jnp.concatenate(got[i * each : (i + 1) * each], 0) for i in range(parts)]
            )
        if later is not None:
            later(groups)
        return groups
    for j in reversed(range(inner)):
        kind = BF16 if j else F32
        if j == 0 and later is not None:
            lefts[0] = after(lefts[0], later(groups))
        groups.append(
            list(
                call(
                    functools.partial(grad_kernel, j, inner, slots),
                    name,
                    lefts + rights,
                    [shape((each, blk, width), kind)] * parts,
                    [pltpu.VMEM((4 * blk, slots * rows), BF16)],
                )
            )
        )
    return groups[::-1]


def body(
    tokens,
    cotangent,
    item_count,
    valid_len,
    w_qkv,
    q_bias,
    v_bias,
    w_out,
    out_bias,
    w_up,
    up_bias,
    w_down,
    down_bias,
    gain_one,
    shift_one,
    gain_two,
    shift_two,
):
    slots, rows, width = tokens.shape
    n_seq = lax.axis_size("seq")
    n_dp = lax.axis_size("dp")
    inner = n_dp // OUTER
    count = n_seq * n_dp
    half = n_seq // 2
    cut = half * rows
    full = n_seq * rows
    cols = width // n_seq
    heads = cols // HEAD_DIM
    piece = width // count
    hidden_all = w_up.shape[1]
    hidden = hidden_all // n_seq
    hpiece = hidden_all // count
    blocks = n_dp // n_seq
    regular = hpiece % LANES == 0 and piece % 16 == 0

    limits = jnp.where(jnp.arange(slots) < item_count[0], valid_len, 0)
    dma = lambda n: pltpu.SemaphoreType.DMA((n,))

    rows_in = [
        q_bias,
        v_bias,
        out_bias,
        down_bias,
        gain_one,
        shift_one,
        gain_two,
        shift_two,
        up_bias,
    ]
    tile = max(16, 2 * n_dp)
    masks = gather_masks()
    n_parts = len(masks)
    flat_masks = [k * inner + j for j in range(inner) for k in ORDER]
    out_gather = Gather(
        call(
            functools.partial(out_pack_kernel, tile),
            "out_pack",
            [w_out] + rows_in,
            [shape((1, tile + piece, width), BF16)],
            [pltpu.VMEM(v.shape, BF16) for v in rows_in]
            + [pltpu.VMEM((tile, width), F32), dma(N_VEC + 1)],
            [VMEM] + [HBM] * (N_VEC + 1),
            WHOLE,
        )[0]
    )
    if regular:
        packed = call(
            functools.partial(pack_kernel, cols, hpiece),
            "pack",
            [w_qkv, w_up],
            [shape((piece, 3 * cols + hidden), BF16)] * n_seq,
        )
        own_qkv, own_up = call(
            place_kernel,
            "place",
            exchange_seq(packed),
            [
                shape((1, n_seq * piece, 3 * cols), BF16),
                shape((1, n_seq * piece, hidden), BF16),
            ],
        )
    else:
        s = lax.axis_index("seq")
        split = jnp.concatenate(
            [
                w_qkv.reshape(piece, 3, n_seq, cols).transpose(2, 0, 1, 3).reshape(n_seq, piece, -1),
                w_up.reshape(piece, n_dp, n_seq, hpiece)
                .transpose(2, 0, 1, 3)
                .reshape(n_seq, piece, -1),
            ],
            -1,
        )
        packed = [lax.dynamic_index_in_dim(split, s ^ r, 0, False) for r in range(n_seq)]
        placed = jnp.zeros_like(split)
        for r, part in enumerate(exchange_seq(packed)):
            placed = lax.dynamic_update_index_in_dim(placed, part, s ^ r, 0)
        placed = placed.reshape(1, n_seq * piece, -1)
        own_qkv, own_up = placed[:, :, : 3 * cols], placed[:, :, 3 * cols :]

    out_gather.middle()
    own_qkv, own_up, out_gather.other, out_gather.first, tok = fence(
        own_qkv, own_up, out_gather.other, out_gather.first, tokens
    )
    qkv_gather = Gather(own_qkv)
    out_gather.last()
    tok = [tok] + far_blocks(tok)
    tok.append(swap(tok[0], "seq", 1))
    qkv_gather.far, qkv_gather.block, out_gather.second, tok[-1] = fence(
        qkv_gather.far, qkv_gather.block, out_gather.second, tok[-1]
    )
    qkv_gather.middle()
    wout = exchange_seq(
        call(
            functools.partial(out_pieces_kernel, masks, tile, blocks),
            "out_pieces",
            out_gather.all(),
            [shape((tile + blocks * piece, width), BF16)] * n_seq,
            [pltpu.VMEM((tile, width), BF16)],
        )
    )
    qkv_gather.other, qkv_gather.first, tok[1:-1], own_up = fence(
        qkv_gather.other, qkv_gather.first, tok[1:-1], own_up
    )
    qkv_gather.last()
    up_gather = Gather(own_up)
    tok = tok + [swap(part, "seq", 1) for part in tok[1:-1]]
    wout, tok, cot = fence(wout, tok, cotangent)
    cot = [cot] + far_blocks(cot)
    cot.append(swap(cot[0], "seq", 1))
    vectors, qkv_bias, ubias = call(
        functools.partial(vector_unpack_kernel, masks, tile, n_seq, cols, hpiece),
        "vector_unpack",
        wout,
        [shape((N_VEC, width), F32), shape((1, 3 * cols), F32), shape((1, hidden), F32)],
    )
    a1 = call(
        functools.partial(norm_kernel, n_seq),
        "norm_one",
        tok + [vectors],
        [shape((full, width), BF16)] * (2 * slots),
    )
    a1, hats = list(a1[:slots]), list(a1[slots:])
    qkv_gather.second, up_gather.far, up_gather.block, a1 = fence(
        qkv_gather.second, up_gather.far, up_gather.block, a1
    )
    wqkv = qkv_gather.all()
    up_gather.middle()

    outs3 = [shape((rows, width), F32), shape((cut - rows, width), F32), shape((cut, width), BF16)]
    qkvs, atts, probss, x2s, a2s, acts, slopes, mids = [], [], [], [], [], [], [], []

    def norm_two(i):
        x2, a2 = call(
            functools.partial(norm_two_kernel, i),
            "norm_two",
            mids[i] + [tokens, vectors],
            [shape((rows, width), F32), shape((rows, width), BF16)],
        )
        x2s.append(x2)
        return a2

    a2_of = {}
    for i in range(slots):
        first = i == 0
        qkv, att, probs, own, rest, high, *kept = call(
            functools.partial(attention_kernel, masks, tile, blocks, cols, n_seq, i),
            "attention",
            [a1[i], qkv_bias, valid_len] + wqkv + wout,
            [
                shape((full, 3 * cols), BF16),
                shape((full, cols), BF16),
                shape((heads, full, full), BF16),
            ]
            + outs3
            + ([shape((width, 3 * cols), BF16), shape((cols, width), BF16)] if first else []),
            [pltpu.VMEM((1, full), F32)] + ([dma(n_dp), dma(n_dp)] if first else []),
            [VMEM] * 2 + [SMEM] + ([ANY] * (n_parts + n_seq) if first else [VMEM] * 2),
        )
        if first:
            wqkv, wout = [kept[0]], [kept[1]]
            up_gather.other, up_gather.first, high, down_block, cot = fence(
                up_gather.other, up_gather.first, high, w_down[None], cot
            )
            up_gather.last()
            down_gather = Gather(down_block)
            near, send = start_scatter(rest, high)
            send, a1[1:] = fence(send, a1[1:])
        else:
            if i == 1:
                down_gather.far, up_gather.second, high, mids[0] = fence(
                    down_gather.far, up_gather.second, high, mids[0]
                )
                a2, high = fence(norm_two(0), high)
                a2_of[0] = gather_seq(a2)
                down_gather.middle()
            near, send = start_scatter(rest, high)
        mids.append([own, near] + end_scatter(send))
        for store, value in zip((qkvs, atts, probss), (qkv, att, probs)):
            store.append(value)
    wup = up_gather.all()

    for i in range(slots):
        first = i == 0
        if i == 1:
            mids[1], acts[0] = fence(mids[1], acts[0])
            a2 = norm_two(1)
            a2, down_gather.other, down_gather.first = fence(
                a2, down_gather.other, down_gather.first
            )
            a2_of[1] = gather_seq(a2)
            down_gather.last()
        elif i > 1:
            a2_of[i] = gather_seq(norm_two(i))
        a2, act, slope, *kept = call(
            functools.partial(up_kernel, masks, n_seq, i),
            "up",
            a2_of[i] + [ubias] + wup,
            [
                shape((full, width), BF16),
                shape((full, hidden), BF16),
                shape((full, hidden), F32),
            ]
            + ([shape((width, hidden), BF16)] if first else []),
            [dma(n_dp)] if first else [],
            [VMEM] * (n_seq + 1) + ([ANY] * n_parts if first else [VMEM]),
        )
        if first:
            wup = kept
        for store, value in zip((a2s, acts, slopes), (a2, act, slope)):
            store.append(value)
    wdown = down_gather.all()
    cot = cot + [swap(part, "seq", 1) for part in cot[1:-1]]
    dys = call(
        functools.partial(mask_kernel, n_seq),
        "mask",
        cot + [limits],
        [shape((full, width), BF16)] * slots,
        specs=[VMEM] * n_seq + [SMEM],
    )

    dus, dxs, dattns, sums2, sums_u, downs, outs_in = [], [], [], [], [], [], []

    def norm_two_back(i):
        dx2, low, sums = call(
            norm_two_back_kernel,
            "norm_two_back",
            downs[i] + [x2s[i], dys[i], vectors],
            [shape((rows, width), F32), shape((rows, width), BF16), shape((8, width), F32)],
        )
        for store, value in zip((dxs, sums2), (dx2, sums)):
            store.append(value)
        return low

    def down_calls(groups):
        nonlocal wdown
        wait = [group[0] for group in groups]
        for i in range(slots):
            first = i == 0
            du, own, rest, high, oown, orest, ohigh, usum, *kept = call(
                functools.partial(down_kernel, masks, i),
                "down",
                [after(dys[i], *wait), acts[i], slopes[i]] + wup + wdown,
                [shape((full, hidden), BF16)]
                + outs3
                + outs3
                + [shape((1, hidden), F32)]
                + ([shape((hidden, width), BF16)] if first else []),
                [dma(n_dp)] if first else [],
                [VMEM] * 4 + ([ANY] * n_parts if first else [VMEM]),
            )
            if first:
                wdown = kept
            if i == 1:
                high, downs[0] = fence(high, downs[0])
                low, high = fence(norm_two_back(0), high)
                dattns.append(gather_seq(low))
            near, send = start_scatter(rest, high)
            wait = [send]
            downs.append([own, near] + end_scatter(send))
            outs_in.append((oown, orest, ohigh))
            dus.append(du)
            sums_u.append(usum)
        return wait[0]

    down_groups = grad_groups(acts, dys, "grad_down", later=down_calls)
    up_groups = grad_groups(
        a2s, [after(dus[0], down_groups[0][0])] + dus[1:], "grad_up"
    )
    out_sums = []
    for own, rest, high in outs_in:
        near, send = start_scatter(rest, after(high, down_groups[0][0]))
        out_sums.append((own, near, send))
    for i in range(1, slots):
        downs[i][2:], up_kept = fence(downs[i][2:], up_groups[0])
        up_groups[0] = up_kept
        low = norm_two_back(i)
        low, *sends = fence(low, *[send for _, _, send in out_sums])
        dattns.append(gather_seq(low))
        out_sums = [(own, near, send) for (own, near, _), send in zip(out_sums, sends)]
    block_out_in = []
    for own, near, send in out_sums:
        block_out_in += [own, near] + end_scatter(after(send, dattns[-1][1]))

    dqkvs, sums_q, sums1, backs = [], [], [], []
    wait = [dattns[-1][0]]
    for i in range(slots):
        dqkv, own, rest, high, qsum, sums = call(
            functools.partial(attention_back_kernel, cols, n_seq),
            "attention_back",
            [after(dattns[i][0], *wait)]
            + dattns[i][1:]
            + [qkvs[i], probss[i], hats[i]]
            + wqkv
            + wout,
            [shape((full, 3 * cols), BF16)]
            + outs3
            + [shape((1, 3 * cols), F32), shape((8, width), F32)],
            [
                pltpu.VMEM((full, width), BF16),
                pltpu.VMEM((full, cols), BF16),
                pltpu.VMEM((LANES, full), F32),
                pltpu.VMEM((LANES, full), F32),
            ],
        )
        near, send = start_scatter(rest, high)
        wait = [send]
        backs.append([own, near, send])
        for store, value in zip((dqkvs, sums_q, sums1), (dqkv, qsum, sums)):
            store.append(value)
    grads_out = []

    def later_qkv(groups):
        ready = groups[0][0]
        pieces = call(
            functools.partial(grad_out_kernel, flat_masks, tile, cols, hpiece, slots, n_seq),
            "grad_out",
            [after(atts[0], ready)]
            + atts[1:]
            + sum(dattns, [])
            + sums1
            + sums2
            + sums_q
            + sums_u,
            [shape((tile + blocks * piece, width), BF16)] * n_seq,
            [pltpu.VMEM((full, width), BF16), pltpu.VMEM((N_VEC, width), F32)],
        )
        grads_out.extend(exchange_seq(pieces))
        return pieces[0]

    qkv_groups = grad_groups(a1, dqkvs, "grad_qkv", merged=False, later=later_qkv)
    back_in = []
    for own, near, send in backs:
        back_in += [own, near] + end_scatter(send)
    g_down = scatter_dp(down_groups)
    g_wdown = total_of(g_down)
    g_up = scatter_dp(up_groups)
    g_out = call(
        functools.partial(grad_out_groups_kernel, flat_masks, tile),
        "grad_out_groups",
        grads_out,
        [shape((len(ORDER), VEC_ROWS + piece, width), BF16 if j else F32) for j in range(inner)],
    )
    g_out = scatter_dp([[part] for part in g_out])
    g_qkv = scatter_dp(qkv_groups)
    block_out = call(
        functools.partial(block_out_kernel, slots, n_seq),
        "block_out",
        block_out_in + x2s + [limits, vectors],
        [shape((slots, rows, width), F32)],
        specs=[VMEM] * (len(block_out_in) + slots) + [SMEM, VMEM],
    )[0]
    grad_tokens = call(
        functools.partial(norm_one_back_kernel, slots),
        "norm_one_back",
        back_in + dxs + [tokens, vectors],
        [shape((slots, rows, width), F32)],
    )[0]
    g_wout, *vecs = call(
        out_final_kernel,
        "out_final",
        [total_of(g_out)],
        [shape((piece, width), F32)]
        + [shape((1, piece), F32)] * N_VEC
        + [shape((1, hpiece), F32)],
    )

    if regular:
        to_owners = lambda parts: exchange_seq(
            call(
                owners_kernel,
                "owners",
                list(parts),
                [shape((piece, parts[0].shape[2]), BF16)] * n_seq,
            )
        )
        g_wqkv, g_wup = call(
            functools.partial(unplace_kernel, cols, hpiece),
            "unplace",
            to_owners(g_qkv) + to_owners(g_up),
            [shape((piece, 3 * width), F32), shape((piece, hidden_all), F32)],
        )
    else:
        placed = []
        for parts in (g_qkv, g_up):
            parts = total_of(parts).astype(BF16).reshape(n_seq, piece, -1)
            parts = exchange_seq(
                [lax.dynamic_index_in_dim(parts, s ^ r, 0, False) for r in range(n_seq)]
            )
            out = jnp.zeros((n_seq,) + parts[0].shape, BF16)
            for r, part in enumerate(parts):
                out = lax.dynamic_update_index_in_dim(out, part, s ^ r, 0)
            placed.append(out.astype(F32))
        g_wqkv = placed[0].reshape(n_seq, piece, 3, cols).transpose(1, 2, 0, 3).reshape(piece, -1)
        g_wup = (
            placed[1].reshape(n_seq, piece, n_dp, hpiece).transpose(1, 2, 0, 3).reshape(piece, -1)
        )
    vecs = [v.reshape(-1) for v in vecs]
    return (
        block_out,
        grad_tokens,
        g_wqkv,
        vecs[0],
        vecs[1],
        g_wout,
        vecs[2],
        g_wup,
        vecs[8],
        g_wdown,
        vecs[3],
        vecs[4],
        vecs[5],
        vecs[6],
        vecs[7],
    )


def solution(mesh):
    both = ("dp", "seq")
    act = P("dp", "seq", None)
    mat = P(both, None)
    vec = P(both)
    return jax.shard_map(
        body,
        mesh=mesh,
        in_specs=(act, act, P("dp"), P("dp"), mat, vec, vec, mat, vec, mat, vec, mat)
        + (vec,) * 5,
        out_specs=(act, act, mat, vec, vec, mat, vec, mat, vec, mat) + (vec,) * 5,
        check_vma=False,
    )
```

```python
import functools

import jax
import jax.numpy as jnp
from jax import lax
from jax.experimental import pallas as pl
from jax.experimental.pallas import tpu as pltpu
from jax.sharding import PartitionSpec as P

HEAD_DIM = 64
LANES = 128
EPSILON = 1e-06
F32 = jnp.float32
BF16 = jnp.bfloat16
OUTER = 4
ORDER = (0, 2, 1, 3)
VMEM = pl.BlockSpec(memory_space=pltpu.VMEM)
ANY = pl.BlockSpec(memory_space=pl.ANY)
HBM = pl.BlockSpec(memory_space=pltpu.HBM)
SMEM = pl.BlockSpec(memory_space=pltpu.SMEM)
LIMIT = 14 * 1024 * 1024
WHOLE = 60 * 1024 * 1024
SOFTMAX_RATE = HEAD_DIM**-0.5 * 1.4426950408889634
WAITS = {
    "out_xb": ["out_z2"],
    "up_z2": ["out_xb"],
    "down_z1": ["qkv_xa"],
    "down_xb": ["down_xa"],
    "cot_y": ["out_seq"],
    "mask": ["norm_one"],
    "x2_0_core": ["out_seq"],
    "x2_0_y": ["up_xa"],
    "norm0": ["up_z1", "qkv_xb", "x2_0_y"],
    "a2_0_y": ["out_seq"],
    "x2_1_y": ["tok_core", "cot_core"],
    "up0": ["att1"],
    "up1": ["a2_0_y", "a2_1_y"],
    "dh2_0_core": ["down_z1"],
    "dh2_0_y": ["norm0", "down0"],
    "down1": ["up1"],
    "back0": ["x2_0_send"],
    "dx_0_y": ["x2_1_y"],
    "gdown_z1": ["gup_sent", "norm1"],
    "gdown_z2": ["cot_y", "dh2_1_y"],
    "gup_kept": ["dx_0_core"],
    "back1": ["out_core0"],
    "dx_1_y": ["qkv_z2", "dx_0_y"],
    "gup_z1": ["dx_1_core", "out_send", "gup_far"],
    "gup_z2": ["dh2_0_y"],
    "dh1_core0": ["place", "gdown_z1", "attb1"],
    "dh1_core1": ["dh2_1_core"],
    "dh1_y": ["dh2_1_send", "dx_0_core"],
    "gqkv_near": ["gqkv_sent"],
    "gout": ["dh1_core0"],
    "gout_far": ["back0"],
    "gout_near": ["gout_far"],
    "gqkv_kept": ["gup_z2"],
    "gqkv_z1": ["dx_1_y"],
    "gqkv_z2": ["a2_0_core", "gqkv_kept"],
    "gout_z1": ["gdown_sent", "dh1_y", "gup_z1"],
    "owners": ["up_xb", "gqkv_z1", "block_out", "gqkv_near", "gout_z1", "gout_near"],
}
N_VEC = 8
VEC_ROWS = 8


def dot(left, right):
    return jnp.dot(left, right, preferred_element_type=F32)


def dot_nt(left, right):
    return lax.dot_general(left, right, (((1,), (1,)), ((), ())), preferred_element_type=F32)


def dot_tn(left, right):
    return lax.dot_general(left, right, (((0,), (0,)), ((), ())), preferred_element_type=F32)


def swap(values, axis, mask):
    size = lax.axis_size(axis)
    return lax.ppermute(values, axis, [(i, i ^ mask) for i in range(size)])


def shape(dims, kind):
    return jax.ShapeDtypeStruct(tuple(dims), kind)


def call(kernel, name, ins, outs, scratch=(), specs=None, limit=LIMIT):
    return pl.pallas_call(
        kernel,
        name=name,
        out_shape=tuple(outs),
        in_specs=specs or [VMEM] * len(ins),
        out_specs=tuple([VMEM] * len(outs)),
        scratch_shapes=list(scratch),
        compiler_params=pltpu.CompilerParams(vmem_limit_bytes=limit),
        cost_estimate=pl.CostEstimate(
            flops=0, bytes_accessed=0, transcendentals=0
        ),
    )(*ins)


def aligned(index, size):
    return pl.multiple_of(index * size, size)


def place_blocks(refs, masks, out):
    own = lax.axis_index("dp")
    for ref, group in zip(refs, masks):
        rows = ref.shape[1]
        for i, mask in enumerate(group):
            out[pl.ds(aligned(own ^ mask, rows), rows), :] = ref[i]


def start_copies(jobs, scratch, sems):
    copies = []
    for src, block, rows in jobs:
        copy = pltpu.make_async_copy(
            src, scratch.at[pl.ds(aligned(block, rows), rows)], sems.at[len(copies)]
        )
        copy.start()
        copies.append(copy)
    return copies


def out_jobs(refs, tile, blocks):
    own = lax.axis_index("seq")
    size = len(refs)
    rows = (refs[0].shape[0] - tile) // blocks
    return [
        (ref.at[pl.ds(tile + b * rows, rows)], b * size + (own ^ r), rows)
        for r, ref in enumerate(refs)
        for b in range(blocks)
    ]


def pack_kernel(cols, hpiece, wqkv, wup, *outs):
    own = lax.axis_index("seq")
    size = len(outs)
    hidden = wup.shape[1] // size
    width = wqkv.shape[1] // 3
    for r, out in enumerate(outs):
        dest = own ^ r
        for i in range(3):
            at = pl.multiple_of(dest * cols + i * width, LANES)
            out[:, i * cols : (i + 1) * cols] = wqkv[:, pl.ds(at, cols)]
        for i in range(hidden // hpiece):
            at = pl.multiple_of((i * size + dest) * hpiece, LANES)
            start = 3 * cols + i * hpiece
            out[:, start : start + hpiece] = wup[:, pl.ds(at, hpiece)]


def place_kernel(*refs):
    size = len(refs) - 2
    qkv, up = refs[size:]
    own = lax.axis_index("seq")
    cut = qkv.shape[2]
    for r in range(size):
        rows = refs[r].shape[0]
        at = pl.ds(aligned(own ^ r, rows), rows)
        qkv[0, at, :] = refs[r][:, :cut]
        up[0, at, :] = refs[r][:, cut:]


def owners_kernel(*refs):
    left, right, outs = refs[:3], refs[3:6], refs[6:]
    own = lax.axis_index("seq")
    rows = outs[0].shape[0]
    cut = left[0].shape[2]
    for r, out in enumerate(outs):
        at = pl.ds(aligned(own ^ r, rows), rows)
        for parts, cols in ((left, slice(0, cut)), (right, slice(cut, out.shape[1]))):
            total = parts[0][0, at, :].astype(F32) + parts[1][0, at, :].astype(F32)
            out[:, cols] = (total + parts[2][0, at, :].astype(F32)).astype(BF16)


def unplace_kernel(cols, hpiece, *refs):
    *parts, qkv, up = refs
    size = len(parts)
    own = lax.axis_index("seq")
    width = qkv.shape[1] // 3
    for r, part in enumerate(parts):
        src = own ^ r
        for i in range(3):
            at = pl.multiple_of(src * cols + i * width, LANES)
            qkv[:, pl.ds(at, cols)] = part[:, i * cols : (i + 1) * cols].astype(F32)
        for i in range((part.shape[1] - 3 * cols) // hpiece):
            at = pl.multiple_of((i * size + src) * hpiece, LANES)
            start = 3 * cols + i * hpiece
            up[:, pl.ds(at, hpiece)] = part[:, start : start + hpiece].astype(F32)


def out_pack_kernel(tile, wout, *refs):
    n = N_VEC + 1
    vecs, out, landed, scratch, sems = refs[:n], refs[n], refs[n + 1 : -2], refs[-2], refs[-1]
    copies = [pltpu.make_async_copy(v, l, sems.at[i]) for i, (v, l) in enumerate(zip(vecs, landed))]
    for copy in copies:
        copy.start()
    out[0, tile:, :] = wout[...]
    scratch[...] = jnp.zeros_like(scratch)
    for copy in copies:
        copy.wait()
    for i, vec in enumerate(landed):
        row, lane = (0, i * LANES) if i < N_VEC else (1, 0)
        scratch[row : row + 1, lane : lane + vec.shape[0]] = vec[...].astype(F32)[None, :]
    out[0, :tile, :] = scratch[...].astype(BF16)


def out_pieces_kernel(masks, tile, blocks, *refs):
    n = len(masks)
    outs, mixed = refs[n:-1], refs[-1]
    d = lax.axis_index("dp")
    s = lax.axis_index("seq")
    flat = [(i, j) for i, group in enumerate(masks) for j in range(len(group))]
    mask_of = [mask for group in masks for mask in group]
    total = None
    for n, (i, j) in enumerate(flat):
        part = refs[i][j, :tile, :].astype(F32)
        part = pltpu.roll(part, 2 * n, 0) if n else part
        total = part if total is None else total + part
    mixed[...] = total.astype(BF16)
    piece = refs[0].shape[1] - tile
    for r, out in enumerate(outs):
        out[:tile, :] = mixed[...]
        for b in range(blocks):
            want = d ^ ((s ^ r) * blocks + b)
            for (i, j), mask in zip(flat, mask_of):

                @pl.when(want == mask)
                def _(out=out, b=b, i=i, j=j):
                    start = tile + b * piece
                    out[start : start + piece, :] = refs[i][j, tile:, :]


def vector_unpack_kernel(masks, tile, n_seq, cols, hpiece, *refs):
    parts, (vectors, qkv_bias, ubias) = refs[:n_seq], refs[n_seq:]
    width = vectors.shape[1]
    hidden = ubias.shape[1]
    mask_of = [mask for group in masks for mask in group]
    piece = width // (n_seq * len(mask_of))
    s = lax.axis_index("seq")
    d = lax.axis_index("dp")
    row = lax.broadcasted_iota(jnp.int32, (tile, 1), 0)
    dist = jnp.zeros_like(row)
    for n, mask in enumerate(mask_of):
        dist = jnp.where(row // 2 == n, mask, dist)
    source = d ^ dist
    lane = lax.broadcasted_iota(jnp.int32, (LANES, width), 1)
    sub = lax.broadcasted_iota(jnp.int32, (LANES, width), 0)
    spread = jnp.where(lane % piece == sub, 1.0, 0.0).astype(BF16)
    target = lax.broadcasted_iota(jnp.int32, (1, width), 1) // piece
    even = row % 2 == 0
    for i in range(N_VEC):
        total = None
        for r, part in enumerate(parts):
            tiled = dot(part[:tile, i * LANES : (i + 1) * LANES], spread)
            here = even & (source * n_seq + (s ^ r) == target)
            tiled = jnp.sum(jnp.where(here, tiled, 0.0), axis=0, keepdims=True)
            total = tiled if total is None else total + tiled
        vectors[i : i + 1, :] = total
    lane = lax.broadcasted_iota(jnp.int32, (LANES, hidden), 1)
    sub = lax.broadcasted_iota(jnp.int32, (LANES, hidden), 0)
    spread = jnp.where(lane % hpiece == sub, 1.0, 0.0).astype(BF16)
    target = lax.broadcasted_iota(jnp.int32, (1, hidden), 1) // hpiece
    tiled = dot(parts[0][:tile, :LANES], spread)
    here = (row % 2 == 1) & (source == target)
    ubias[...] = jnp.sum(jnp.where(here, tiled, 0.0), axis=0, keepdims=True)
    at = pl.ds(pl.multiple_of(s * cols, LANES), cols)
    qkv_bias[...] = jnp.zeros_like(qkv_bias)
    qkv_bias[:, :cols] = vectors[0:1, at]
    qkv_bias[:, 2 * cols :] = vectors[1:2, at]


def positions(block, rows, n_seq, axis):
    half = n_seq // 2
    owner = lax.axis_index("seq") ^ (2 * (block % half) + block // half)
    dims = (rows, 1) if axis == 0 else (1, rows)
    return owner * rows + lax.broadcasted_iota(jnp.int32, dims, axis)


def attention_kernel(masks, tile, blocks, cols, n_seq, item, *refs):
    first = item == 0
    a1, bias, lens = refs[:3]
    n = len(masks) if first else 1
    pieces, outs = refs[3 : 3 + n], refs[3 + n : 3 + n + (n_seq if first else 1)]
    refs = refs[3 + n + len(outs) :]
    if first:
        qkv, att, probs, own, rest, high, wqkv, wout, ok, sems = refs
    else:
        qkv, att, probs, own, rest, high, ok = refs
        (wqkv,), (wout,) = pieces, outs
    rows = a1.shape[0]
    cut = rows // 2
    blk = own.shape[0]
    out_copies = []
    if first:
        out_copies = start_copies(out_jobs(outs, tile, blocks), wout, sems)
        place_blocks(pieces, masks, wqkv)
    for q in range(n_seq):
        good = positions(q, blk, n_seq, 1) < lens[item]
        ok[:, q * blk : (q + 1) * blk] = jnp.where(good, 0.0, -1e30)
    for i in range(3):
        part = slice(i * cols, (i + 1) * cols)
        qkv[:, part] = (dot(a1[...], wqkv[:, part]) + bias[:, part]).astype(BF16)
    step_rows = min(256, rows)
    lane = lax.broadcasted_iota(jnp.int32, (1, LANES), 1)
    sides = [(lane < HEAD_DIM), (lane >= HEAD_DIM)]
    for pair in range(cols // LANES):
        at = slice(pair * LANES, (pair + 1) * LANES)
        keys = qkv[:, cols + pair * LANES : cols + (pair + 1) * LANES]
        vals = qkv[:, 2 * cols + pair * LANES : 2 * cols + (pair + 1) * LANES]
        split = [jnp.where(side, vals, jnp.zeros_like(vals)) for side in sides]

        def step(block, carry, pair=pair, at=at, keys=keys, split=split):
            place = pl.ds(aligned(block, step_rows), step_rows)
            query = qkv[place, at]
            total = None
            for h in range(2):
                q = jnp.where(sides[h], query, jnp.zeros_like(query))
                scores = dot_nt(q, keys) + ok[...]
                peak = jnp.max(scores, axis=-1, keepdims=True)
                expo = jnp.exp2((scores - peak) * SOFTMAX_RATE)
                rate = 1.0 / jnp.sum(expo, axis=-1, keepdims=True)
                low = (expo * rate).astype(BF16)
                probs[2 * pair + h, place, :] = low
                out = dot(low, split[h])
                total = out if total is None else total + out
            att[place, at] = total.astype(BF16)
            return carry

        lax.fori_loop(0, rows // step_rows, step, 0)
    for copy in out_copies:
        copy.wait()
    high[...] = dot(att[cut:, :], wout[...]).astype(BF16)
    own[...] = dot(att[:blk, :], wout[...])
    rest[...] = dot(att[blk:cut, :], wout[...])


def attention_back_kernel(cols, n_seq, *refs):
    parts = refs[:n_seq]
    qkv, probs, hat, wqkv, wout = refs[n_seq : n_seq + 5]
    dqkv, own, rest, high, sums, sums_one, grad, datt, dkt, dvt = refs[n_seq + 5 :]
    rows = dqkv.shape[0]
    cut = rows // 2
    blk = own.shape[0]
    for i, part in enumerate(parts):
        grad[i * blk : (i + 1) * blk, :] = part[...]
    datt[...] = dot_nt(grad[...], wout[...]).astype(BF16)
    step_rows = min(256, rows)
    lane = lax.broadcasted_iota(jnp.int32, (1, LANES), 1)
    sides = [(lane < HEAD_DIM), (lane >= HEAD_DIM)]
    scale = HEAD_DIM**-0.5
    for pair in range(cols // LANES):
        at = slice(pair * LANES, (pair + 1) * LANES)
        at_k = slice(cols + pair * LANES, cols + (pair + 1) * LANES)
        at_v = slice(2 * cols + pair * LANES, 2 * cols + (pair + 1) * LANES)
        keys = qkv[:, at_k]
        vals = qkv[:, at_v]
        split = [jnp.where(side, keys, jnp.zeros_like(keys)) for side in sides]
        dkt[...] = jnp.zeros_like(dkt)
        dvt[...] = jnp.zeros_like(dvt)

        def step(block, carry, pair=pair, at=at, vals=vals, split=split):
            place = pl.ds(aligned(block, step_rows), step_rows)
            gatt = datt[place, at]
            query = qkv[place, at]
            gatt_t = gatt.T
            query_t = query.T
            total = None
            for h in range(2):
                g = jnp.where(sides[h], gatt, jnp.zeros_like(gatt))
                gp = dot_nt(g, vals)
                low = probs[2 * pair + h, place, :]
                p = low.astype(F32)
                mean = jnp.sum(gp * p, axis=-1, keepdims=True)
                gs = (p * (gp - mean)).astype(BF16)
                half = slice(h * HEAD_DIM, (h + 1) * HEAD_DIM)
                dvt[half, :] += dot(gatt_t[half, :], low)
                dkt[half, :] += dot(query_t[half, :], gs)
                out = dot(gs, split[h])
                total = out if total is None else total + out
            dqkv[place, at] = (total * scale).astype(BF16)
            return carry

        lax.fori_loop(0, rows // step_rows, step, 0)
        dqkv[:, at_k] = (dkt[...].T * scale).astype(BF16)
        dqkv[:, at_v] = dvt[...].T.astype(BF16)
    sums[...] = jnp.sum(dqkv[...].astype(F32), axis=0, keepdims=True)
    sums_one[...] = jnp.zeros_like(sums_one)

    def last(block, carry):
        at = pl.ds(aligned(block, 256), 256)
        value = dot_nt(dqkv[...], wqkv[at, :])
        own[:, at] = value[:blk]
        rest[:, at] = value[blk:cut]
        high[:, at] = value[cut:].astype(BF16)
        sums_one[0:1, at] = jnp.sum(value * hat[:, at].astype(F32), axis=0, keepdims=True)
        sums_one[1:2, at] = jnp.sum(value, axis=0, keepdims=True)
        return carry

    lax.fori_loop(0, wqkv.shape[0] // 256, last, 0)


def up_kernel(masks, n_seq, item, *refs):
    first = item == 0
    n = len(masks) if first else 1
    parts, bias = refs[:n_seq], refs[n_seq]
    pieces = refs[n_seq + 1 : n_seq + 1 + n]
    if first:
        a2, act, slope, wup = refs[n_seq + 1 + n :]
        place_blocks(pieces, masks, wup)
    else:
        a2, act, slope = refs[n_seq + 1 + n :]
        (wup,) = pieces
    blk = parts[0].shape[0]
    rows = a2.shape[0]
    width = min(256, act.shape[1])
    for i, part in enumerate(parts):
        a2[i * blk : (i + 1) * blk, :] = part[...]
    half = min(256, rows)
    for i in range(rows // half):
        place = slice(i * half, (i + 1) * half)

        def step(block, carry, place=place):
            at = pl.ds(aligned(block, width), width)
            u = dot(a2[place, :], wup[:, at]) + bias[:, at]
            cdf = 0.5 * (1.0 + lax.erf(u * 0.7071067811865476))
            bell = jnp.exp2(u * u * -0.7213475204444817) * 0.3989422804014327
            act[place, at] = (u * cdf).astype(BF16)
            slope[place, at] = cdf + u * bell
            return carry

        lax.fori_loop(0, act.shape[1] // width, step, 0)


def down_kernel(masks, item, *refs):
    n = len(masks) if item == 0 else 1
    dy, act, slope, wup = refs[:4]
    downs = refs[4 : 4 + n]
    if item == 0:
        du, own, rest, high, oown, orest, ohigh, sums, wdown = refs[4 + n :]
        place_blocks(downs, masks, wdown)
    else:
        du, own, rest, high, oown, orest, ohigh, sums = refs[4 + n :]
        (wdown,) = downs
    rows = dy.shape[0]
    cut = rows // 2
    blk = own.shape[0]
    hidden = act.shape[1]
    width = min(256, hidden)

    def first(block, carry):
        at = pl.ds(aligned(block, width), width)
        value = (slope[:, at] * dot_nt(dy[...], wdown[at, :])).astype(BF16)
        du[:, at] = value
        sums[:, at] = jnp.sum(value.astype(F32), axis=0, keepdims=True)
        return carry

    lax.fori_loop(0, hidden // width, first, 0)

    def second(block, carry):
        at = pl.ds(aligned(block, 256), 256)
        value = dot_nt(du[...], wup[at, :])
        own[:, at] = value[:blk]
        rest[:, at] = value[blk:cut]
        high[:, at] = value[cut:].astype(BF16)
        value = dot(act[...], wdown[:, at])
        oown[:, at] = value[:blk]
        orest[:, at] = value[blk:cut]
        ohigh[:, at] = value[cut:].astype(BF16)
        return carry

    lax.fori_loop(0, wup.shape[0] // 256, second, 0)


def grad_kernel(j, inner, slots, *refs):
    lefts, rights = refs[:slots], refs[slots : 2 * slots]
    *outs, turned = refs[2 * slots :]
    rows = lefts[0].shape[0]
    each, blk = outs[0].shape[:2]
    own = lax.axis_index("dp")
    for n, k in enumerate(ORDER):
        at = pl.ds(aligned(own ^ (k * inner + j), blk), blk)
        for i, left in enumerate(lefts):
            turned[n * blk : (n + 1) * blk, i * rows : (i + 1) * rows] = left[:, at].T
    width = min(256, outs[0].shape[2])

    def step(block, carry):
        at = pl.ds(aligned(block, width), width)
        total = None
        for i, right in enumerate(rights):
            out = dot(turned[:, i * rows : (i + 1) * rows], right[:, at])
            total = out if total is None else total + out
        for n in range(len(ORDER)):
            out = outs[n // each]
            out[n % each, :, at] = total[n * blk : (n + 1) * blk].astype(out.dtype)
        return carry

    lax.fori_loop(0, outs[0].shape[2] // width, step, 0)


def grad_out_kernel(masks, tile, cols, hpiece, slots, n_seq, *refs):
    take = lambda n: (refs[:n], refs[n:])
    lefts, refs = take(slots)
    rights, refs = take(slots * n_seq)
    sums1, refs = take(slots)
    sums2, refs = take(slots)
    sums_q, refs = take(slots)
    sums_u, refs = take(slots)
    outs, (scratch, wide) = take(n_seq)[0], refs[n_seq:]
    width = wide.shape[1]
    s = lax.axis_index("seq")
    d = lax.axis_index("dp")
    total = lambda refs: functools.reduce(lambda a, b: a + b, [ref[...] for ref in refs])
    q, u = total(sums_q), total(sums_u)
    one, two = total(sums1), total(sums2)
    wide[...] = jnp.zeros_like(wide)
    at = pl.ds(pl.multiple_of(s * cols, LANES), cols)
    wide[0:1, at] = q[:, :cols]
    wide[1:2, at] = q[:, 2 * cols :]
    wide[2:4, :] = two[:2]
    wide[4:6, :] = one[:2]
    wide[6:8, :] = two[2:4]
    piece = width // (n_seq * len(masks))
    row = lax.broadcasted_iota(jnp.int32, (n_seq * tile, 1), 0)
    near = row % tile
    dist = jnp.zeros_like(row)
    for n, mask in enumerate(masks):
        dist = jnp.where(near // 2 == n, mask, dist)
    dest = (d ^ dist) * n_seq + (s ^ (row // tile))
    dest = jnp.where(near % 2 == 0, dest, -1)
    spread = jnp.where(
        lax.broadcasted_iota(jnp.int32, (width, LANES), 0) % piece
        == lax.broadcasted_iota(jnp.int32, (width, LANES), 1),
        1.0,
        0.0,
    ).astype(BF16)
    here = lax.broadcasted_iota(jnp.int32, (1, width), 1) // piece == dest
    vecs = []
    for i in range(N_VEC):
        vecs.append(dot(jnp.where(here, wide[i : i + 1, :], 0.0).astype(BF16), spread))
    hidden = u.shape[1]
    spread = jnp.where(
        lax.broadcasted_iota(jnp.int32, (hidden, LANES), 0) % hpiece
        == lax.broadcasted_iota(jnp.int32, (hidden, LANES), 1),
        1.0,
        0.0,
    ).astype(BF16)
    dest = jnp.where(near % 2 == 1, d ^ dist, -1)[:tile]
    here = lax.broadcasted_iota(jnp.int32, (1, hidden), 1) // hpiece == dest
    long = dot(jnp.where(here, u, 0.0).astype(BF16), spread)
    for r, out in enumerate(outs):
        for i, vec in enumerate(vecs):
            value = vec[r * tile : (r + 1) * tile]
            if r == 0 and i == 0:
                value = value + long
            out[:tile, i * LANES : (i + 1) * LANES] = value.astype(BF16)
    rows = rights[0].shape[0]
    blocks = (outs[0].shape[0] - tile) // piece
    grad = None
    for i, left in enumerate(lefts):
        for q in range(n_seq):
            scratch[q * rows : (q + 1) * rows, :] = rights[i * n_seq + q][...]
        part = dot_tn(left[...], scratch[...])
        grad = part if grad is None else grad + part
    grad = grad.astype(BF16)
    for other in range(n_seq):
        for r in range(n_seq):

            @pl.when(s ^ r == other)
            def _(other=other, r=r):
                for b in range(blocks):
                    at = (b * n_seq + other) * piece
                    start = tile + b * piece
                    outs[r][start : start + piece, :] = grad[at : at + piece]


def grad_out_groups_kernel(masks, tile, *refs):
    n_out = len(masks) // 2
    pieces, outs = refs[:-n_out], refs[-n_out:]
    size = len(pieces)
    head = VEC_ROWS
    rows = outs[0].shape[1] - head
    blocks = (pieces[0].shape[0] - tile) // rows
    d = lax.axis_index("dp")
    s = lax.axis_index("seq")
    total = None
    for piece in pieces:
        part = piece[:tile, :].astype(F32)
        total = part if total is None else total + part
    row = lax.broadcasted_iota(jnp.int32, (tile, 1), 0)
    for n, mask in enumerate(masks):
        out, i = outs[n // 2], n % 2
        value = pltpu.roll(total, tile - 2 * n, 0) if n else total
        out[i, :head, :] = jnp.where(row < 2, value, 0.0)[:head].astype(out.dtype)
        for r in range(size):
            for b in range(blocks):

                @pl.when(d ^ mask == (s ^ r) * blocks + b)
                def _(out=out, i=i, r=r, b=b):
                    start = tile + b * rows
                    out[i, head:, :] = pieces[r][start : start + rows, :].astype(out.dtype)


def out_final_kernel(total, grad, *vecs):
    grad[...] = total[VEC_ROWS:, :]
    for i, vec in enumerate(vecs[:-1]):
        vec[...] = total[0:1, i * LANES : i * LANES + vec.shape[1]]
    vecs[-1][...] = total[1:2, : vecs[-1].shape[1]]


def items_kernel(*refs):
    slots, blk = refs[-1].shape[:2]
    rests, nears, outs = refs[:slots], refs[slots : 2 * slots], refs[2 * slots :]
    for i in range(slots):
        for j, out in enumerate(outs):
            near = nears[i][(j + 1) * blk : (j + 2) * blk, :].astype(F32)
            out[i] = (rests[i][j * blk : (j + 1) * blk, :] + near).astype(BF16)


def item_sum(item, own, near, far, blk):
    total = own[...] + near[:blk, :].astype(F32)
    for ref in far:
        total = total + ref[item].astype(F32)
    return total


def gathered_sum(own, near, far, blk):
    total = own[...] + near[:blk, :].astype(F32)
    for ref in far:
        total = total + ref[...].astype(F32)
    return total


def stats(values):
    center = values - jnp.mean(values, axis=-1, keepdims=True)
    rate = lax.rsqrt(jnp.mean(center * center, axis=-1, keepdims=True) + EPSILON)
    return center * rate, rate


def norm_kernel(n_seq, *refs):
    parts, vectors, outs = refs[:n_seq], refs[n_seq], refs[n_seq + 1 :]
    rows = parts[0].shape[1]
    outs, hats = outs[: len(outs) // 2], outs[len(outs) // 2 :]
    for i, (out, kept) in enumerate(zip(outs, hats)):
        for q, part in enumerate(parts):
            hat, _ = stats(part[i].astype(F32))
            kept[q * rows : (q + 1) * rows, :] = hat.astype(BF16)
            out[q * rows : (q + 1) * rows, :] = (
                hat * vectors[4:5, :] + vectors[5:6, :]
            ).astype(BF16)


def mask_kernel(n_seq, *refs):
    parts, limits, outs = refs[:n_seq], refs[n_seq], refs[n_seq + 1 :]
    rows = parts[0].shape[1]
    for i, out in enumerate(outs):
        for q, part in enumerate(parts):
            good = jnp.where(positions(q, rows, n_seq, 0) < limits[i], 1.0, 0.0)
            out[q * rows : (q + 1) * rows, :] = (part[i].astype(F32) * good).astype(BF16)


def norm_two_kernel(item, own, near, *refs):
    *far, x, vectors, x2, a2 = refs
    value = x[item].astype(F32) + (
        gathered_sum(own, near, far, x2.shape[0]) + vectors[2:3, :]
    )
    x2[...] = value
    hat, _ = stats(value)
    a2[...] = (hat * vectors[6:7, :] + vectors[7:8, :]).astype(BF16)


def norm_back(grad, gain, hat, rate):
    scaled = grad * gain
    return rate * (
        scaled
        - jnp.mean(scaled, axis=-1, keepdims=True)
        - hat * jnp.mean(scaled * hat, axis=-1, keepdims=True)
    )


def norm_two_back_kernel(own, near, *refs):
    *far, x2, dy, vectors, dx2, low, sums = refs
    grad = gathered_sum(own, near, far, x2.shape[0])
    hat, rate = stats(x2[...])
    rows = dy[: x2.shape[0], :].astype(F32)
    value = rows + norm_back(grad, vectors[6:7, :], hat, rate)
    dx2[...] = value
    rounded = value.astype(BF16)
    low[...] = rounded
    sums[0:1, :] = jnp.sum(rounded.astype(F32), axis=0, keepdims=True)
    sums[1:2, :] = jnp.sum(rows, axis=0, keepdims=True)
    sums[2:3, :] = jnp.sum(grad * hat, axis=0, keepdims=True)
    sums[3:4, :] = jnp.sum(grad, axis=0, keepdims=True)
    sums[4:8, :] = jnp.zeros_like(sums[4:8, :])


def norm_one_back_kernel(slots, *refs):
    owns, nears, refs = refs[:slots], refs[slots : 2 * slots], refs[2 * slots :]
    *far, x, vectors, out = refs
    far, dxs = far[:-slots], far[-slots:]
    for i in range(slots):
        grad = item_sum(i, owns[i], nears[i], far, x.shape[1])
        hat, rate = stats(x[i].astype(F32))
        out[i] = dxs[i][...] + norm_back(grad, vectors[4:5, :], hat, rate)


def block_out_kernel(slots, n_seq, *refs):
    owns, nears, refs = refs[:slots], refs[slots : 2 * slots], refs[2 * slots :]
    *far, limits, vectors, out = refs
    far, x2s = far[:-slots], far[-slots:]
    for i, x2 in enumerate(x2s):
        blk = x2.shape[0]
        value = x2[...] + item_sum(i, owns[i], nears[i], far, blk) + vectors[3:4, :]
        good = jnp.where(positions(0, blk, n_seq, 0) < limits[i], 1.0, 0.0)
        out[i] = value * good


def exchange_seq(pieces):
    return [swap(piece, "seq", r) if r else piece for r, piece in enumerate(pieces)]


def gather_masks():
    inner = lax.axis_size("dp") // OUTER
    return [
        tuple(k * inner ^ j for k in pair) for pair in (ORDER[:2], ORDER[2:]) for j in range(inner)
    ]


def total_of(parts):
    return functools.reduce(lambda a, b: a + b, [part[0].astype(F32) for part in parts])


class Steps:
    def __init__(self):
        self.known = {}

    def keep(self, name, value):
        self.known[name] = value
        return value

    def send(self, name, value, axis, mask):
        return self.keep(name, swap(value, axis, mask))

    def gate(self, name, value):
        others = [self.known[key] for key in WAITS.get(name, ()) if key in self.known]
        return lax.optimization_barrier((value, others))[0] if others else value


def inner_masks():
    inner = lax.axis_size("dp") // OUTER
    out, bit = [], 1
    while bit < inner:
        out.append(bit)
        bit *= 2
    return out


def gather_dp(steps, name, block):
    inner = lax.axis_size("dp") // OUTER
    far = steps.send(name + "_z2", steps.gate(name + "_z2", block), "dp", 2 * inner)
    pair = jnp.concatenate([block, far], 0)
    other = steps.send(name + "_z1", steps.gate(name + "_z1", pair), "dp", inner)
    out = []
    for part, key in ((pair, name + "_xa"), (other, name + "_xb")):
        group = [part]
        for bit in inner_masks():
            group += [swap(steps.gate(key, p), "dp", bit) for p in group]
        steps.keep(key, group[1:])
        out += group
    return out


def scatter_first(steps, name, made, part):
    pairs = [group[part] for group in made[1:2] if len(made) == 2]
    steps.keep(name, [swap(steps.gate(name, pair), "dp", 1) for pair in pairs])
    return steps.known[name]


def inner_sum(parts, early):
    parts = [parts[0].astype(F32)] + list(parts[1:])
    for bit in inner_masks():
        for j in range(0, len(parts), 2 * bit):
            if len(parts) == 2:
                got = early[0]
            else:
                got = swap(parts[j + bit].astype(BF16), "dp", bit)
            parts[j] = parts[j].astype(F32) + got.astype(F32)
    return parts[0]


class Scatter:
    def __init__(self, steps, name):
        self.steps, self.name = steps, name

    def send(self, made):
        self.far = scatter_first(self.steps, self.name + "_far", made, 1)
        self.near = scatter_first(self.steps, self.name + "_near", made, 0)

    def finish(self, groups):
        steps, name = self.steps, self.name
        inner = len(groups)
        far = inner_sum([group[1] for group in groups], self.far).astype(BF16)
        got = steps.send(name + "_z1", steps.gate(name + "_z1", far), "dp", inner)
        near = inner_sum([group[0] for group in groups], self.near)
        send = (near[1:] + got[1:].astype(F32)).astype(BF16)
        tail = steps.send(name + "_z2", steps.gate(name + "_z2", send), "dp", 2 * inner)
        return near, got, tail


def scatter_seq(steps, name, rest, high):
    half = lax.axis_size("seq") // 2
    near = steps.send(name + "_core", steps.gate(name + "_core", high), "seq", 1)
    blk = near.shape[0] // half
    send = (rest + near[blk:].astype(F32)).astype(BF16)
    send = steps.gate(name + "_y", steps.keep(name + "_send", send))
    far = [swap(send[(j - 1) * blk : j * blk], "seq", 2 * j) for j in range(1, half)]
    return [near] + steps.keep(name + "_y", far)


def scatter_items(steps, name, parts):
    half = lax.axis_size("seq") // 2
    slots = len(parts)
    nears = [
        steps.send(f"{name}_core{i}", steps.gate(f"{name}_core{i}", high), "seq", 1)
        for i, (_, high) in enumerate(parts)
    ]
    rests = [rest for rest, _ in parts]
    blk = nears[0].shape[0] // half
    width = nears[0].shape[1]
    sends = call(
        items_kernel,
        "items",
        rests + nears,
        [shape((slots, blk, width), BF16)] * (half - 1),
    )
    sends = steps.gate(name + "_y", steps.keep(name + "_send", list(sends)))
    far = [swap(send, "seq", 2 * (j + 1)) for j, send in enumerate(sends)]
    steps.keep(name + "_y", far)
    return nears, far


def gather_seq(steps, name, block):
    half = lax.axis_size("seq") // 2
    block = steps.gate(name + "_y", block)
    far = steps.keep(name + "_y", [swap(block, "seq", 2 * j) for j in range(1, half)])
    mine = [block] + far
    other = [swap(block, "seq", 1)]
    other += [swap(steps.gate(name + "_core", part), "seq", 1) for part in far]
    steps.keep(name + "_core", other)
    return mine + other


def grad_kernels(steps, name, lefts, rights):
    lefts, rights = list(lefts), list(rights)
    inner = lax.axis_size("dp") // OUTER
    slots = len(lefts)
    blk = lefts[0].shape[1] // (OUTER * inner)
    width = rights[0].shape[1]
    rows = lefts[0].shape[0]
    if blk % LANES:
        own = lax.axis_index("dp")
        whole = sum(dot_tn(a, b) for a, b in zip(lefts, rights)).reshape(-1, blk, width)
        take = lambda k: lax.dynamic_index_in_dim(whole, own ^ k, 0)
        made = []
        for j in range(inner):
            got = [take(k * inner + j) for k in ORDER]
            made.append([jnp.concatenate(got[:2], 0), jnp.concatenate(got[2:], 0)])
        return made, lambda: made
    made = [None] * inner

    def make(j):
        key = name + ("_sent" if j else "_kept")
        made[j] = steps.keep(
            key,
            list(
                call(
                    functools.partial(grad_kernel, j, inner, slots),
                    key,
                    [steps.gate(key, lefts[0])] + lefts[1:] + rights,
                    [shape((2, blk, width), BF16 if j else F32)] * 2,
                    [pltpu.VMEM((4 * blk, slots * rows), BF16)],
                )
            ),
        )

    def rest():
        make(0)
        return made

    for j in range(1, inner):
        make(j)
    return made, rest


def body(
    tokens,
    cotangent,
    item_count,
    valid_len,
    w_qkv,
    q_bias,
    v_bias,
    w_out,
    out_bias,
    w_up,
    up_bias,
    w_down,
    down_bias,
    gain_one,
    shift_one,
    gain_two,
    shift_two,
):
    slots, rows, width = tokens.shape
    n_seq = lax.axis_size("seq")
    n_dp = lax.axis_size("dp")
    inner = n_dp // OUTER
    count = n_seq * n_dp
    half = n_seq // 2
    cut = half * rows
    full = n_seq * rows
    cols = width // n_seq
    heads = cols // HEAD_DIM
    piece = width // count
    hidden_all = w_up.shape[1]
    hidden = hidden_all // n_seq
    hpiece = hidden_all // count
    blocks = n_dp // n_seq
    regular = hpiece % LANES == 0 and piece % 16 == 0

    limits = jnp.where(jnp.arange(slots) < item_count[0], valid_len, 0)
    dma = lambda n: pltpu.SemaphoreType.DMA((n,))

    rows_in = [
        q_bias,
        v_bias,
        out_bias,
        down_bias,
        gain_one,
        shift_one,
        gain_two,
        shift_two,
        up_bias,
    ]
    tile = max(16, 2 * n_dp)
    masks = gather_masks()
    n_parts = len(masks)
    flat_masks = [k * inner + j for j in range(inner) for k in ORDER]
    steps = Steps()
    out_block = call(
        functools.partial(out_pack_kernel, tile),
        "out_pack",
        [w_out] + rows_in,
        [shape((1, tile + piece, width), BF16)],
        [pltpu.VMEM(v.shape, BF16) for v in rows_in]
        + [pltpu.VMEM((tile, width), F32), dma(N_VEC + 1)],
        [VMEM] + [HBM] * (N_VEC + 1),
        WHOLE,
    )[0]
    if regular:
        packed = call(
            functools.partial(pack_kernel, cols, hpiece),
            "pack",
            [w_qkv, w_up],
            [shape((piece, 3 * cols + hidden), BF16)] * n_seq,
        )
        own_qkv, own_up = call(
            place_kernel,
            "place",
            exchange_seq(packed),
            [
                shape((1, n_seq * piece, 3 * cols), BF16),
                shape((1, n_seq * piece, hidden), BF16),
            ],
        )
    else:
        s = lax.axis_index("seq")
        split = jnp.concatenate(
            [
                w_qkv.reshape(piece, 3, n_seq, cols).transpose(2, 0, 1, 3).reshape(n_seq, piece, -1),
                w_up.reshape(piece, n_dp, n_seq, hpiece)
                .transpose(2, 0, 1, 3)
                .reshape(n_seq, piece, -1),
            ],
            -1,
        )
        packed = [lax.dynamic_index_in_dim(split, s ^ r, 0, False) for r in range(n_seq)]
        placed = jnp.zeros_like(split)
        for r, part in enumerate(exchange_seq(packed)):
            placed = lax.dynamic_update_index_in_dim(placed, part, s ^ r, 0)
        placed = placed.reshape(1, n_seq * piece, -1)
        own_qkv, own_up = placed[:, :, : 3 * cols], placed[:, :, 3 * cols :]

    steps.keep("place", [own_qkv, own_up])
    out_all = gather_dp(steps, "out", out_block)
    wqkv = gather_dp(steps, "qkv", own_qkv)
    wup = gather_dp(steps, "up", own_up)
    wdown = gather_dp(steps, "down", w_down[None])
    wout = exchange_seq(
        call(
            functools.partial(out_pieces_kernel, masks, tile, blocks),
            "out_pieces",
            [steps.gate("out_pieces", out_all[0])] + out_all[1:],
            [shape((tile + blocks * piece, width), BF16)] * n_seq,
            [pltpu.VMEM((tile, width), BF16)],
        )
    )
    steps.keep("out_seq", wout[1:])
    tok = gather_seq(steps, "tok", tokens)
    cot = gather_seq(steps, "cot", cotangent)
    vectors, qkv_bias, ubias = call(
        functools.partial(vector_unpack_kernel, masks, tile, n_seq, cols, hpiece),
        "vector_unpack",
        [steps.gate("vectors", wout[0])] + wout[1:],
        [shape((N_VEC, width), F32), shape((1, 3 * cols), F32), shape((1, hidden), F32)],
    )
    a1 = call(
        functools.partial(norm_kernel, n_seq),
        "norm_one",
        [steps.gate("norm_one", tok[0])] + tok[1:] + [vectors],
        [shape((full, width), BF16)] * (2 * slots),
    )
    a1, hats = list(a1[:slots]), list(a1[slots:])
    steps.keep("norm_one", a1)
    dys = call(
        functools.partial(mask_kernel, n_seq),
        "mask",
        [steps.gate("mask", cot[0])] + cot[1:] + [limits],
        [shape((full, width), BF16)] * slots,
        specs=[VMEM] * n_seq + [SMEM],
    )
    steps.keep("mask", dys)

    outs3 = [shape((rows, width), F32), shape((cut - rows, width), F32), shape((cut, width), BF16)]
    qkvs, atts, probss, x2s, a2s, acts, slopes, a2_of = [], [], [], [], [], [], [], []
    for i in range(slots):
        first = i == 0
        qkv, att, probs, own, rest, high, *kept = call(
            functools.partial(attention_kernel, masks, tile, blocks, cols, n_seq, i),
            "attention",
            [steps.gate(f"att{i}", a1[i]), qkv_bias, valid_len] + wqkv + wout,
            [
                shape((full, 3 * cols), BF16),
                shape((full, cols), BF16),
                shape((heads, full, full), BF16),
            ]
            + outs3
            + ([shape((width, 3 * cols), BF16), shape((cols, width), BF16)] if first else []),
            [pltpu.VMEM((1, full), F32)] + ([dma(n_dp)] if first else []),
            [VMEM] * 2 + [SMEM] + ([VMEM] * n_parts + [ANY] * n_seq if first else [VMEM] * 2),
        )
        if first:
            wqkv, wout = [kept[0]], [kept[1]]
        steps.keep(f"att{i}", att)
        for store, value in zip((qkvs, atts, probss, a2_of), (qkv, att, probs, (own, rest, high))):
            store.append(value)
        if i == 0:
            a2_of[0] = [own] + scatter_seq(steps, "x2_0", rest, high)
        if i == 1 or slots == 1:
            norm_two_of = lambda i: call(
                functools.partial(norm_two_kernel, i),
                "norm_two",
                [steps.gate(f"norm{i}", a2_of[i][0])] + a2_of[i][1:] + [tokens, vectors],
                [shape((rows, width), F32), shape((rows, width), BF16)],
            )
            x2, a2 = norm_two_of(0)
            x2s.append(x2)
            a2_of[0] = gather_seq(steps, "a2_0", steps.keep("norm0", a2))
        if i:
            own, rest, high = a2_of[i]
            a2_of[i] = [own] + scatter_seq(steps, f"x2_{i}", rest, high)

    for i in range(slots):
        first = i == 0
        if i:
            x2, a2 = norm_two_of(i)
            x2s.append(x2)
            a2_of[i] = gather_seq(steps, f"a2_{i}", steps.keep(f"norm{i}", a2))
        a2, act, slope, *kept = call(
            functools.partial(up_kernel, masks, n_seq, i),
            "up",
            [steps.gate(f"up{i}", a2_of[i][0])] + a2_of[i][1:] + [ubias] + wup,
            [
                shape((full, width), BF16),
                shape((full, hidden), BF16),
                shape((full, hidden), F32),
            ]
            + ([shape((width, hidden), BF16)] if first else []),
        )
        if first:
            wup = kept
        steps.keep(f"up{i}", act)
        for store, value in zip((a2s, acts, slopes), (a2, act, slope)):
            store.append(value)

    dus, dxs, dattns, sums2, sums_u, downs = [], [], [], [], [], []
    down_sum, up_sum = Scatter(steps, "gdown"), Scatter(steps, "gup")
    made, down_rest = grad_kernels(steps, "gdown", acts, dys)
    down_sum.send(made)
    down_made = down_rest()

    def norm_two_back(i):
        dx2, low, sums = call(
            norm_two_back_kernel,
            "norm_two_back",
            [steps.gate(f"back{i}", downs[i][0])] + downs[i][1:] + [x2s[i], dys[i], vectors],
            [shape((rows, width), F32), shape((rows, width), BF16), shape((8, width), F32)],
        )
        for store, value in zip((dxs, sums2), (dx2, sums)):
            store.append(value)
        return steps.keep(f"back{i}", low)

    out_parts = []
    for i in range(slots):
        first = i == 0
        du, own, rest, high, oown, orest, ohigh, usum, *kept = call(
            functools.partial(down_kernel, masks, i),
            "down",
            [steps.gate(f"down{i}", dys[i]), acts[i], slopes[i]] + wup + wdown,
            [shape((full, hidden), BF16)]
            + outs3
            + outs3
            + [shape((1, hidden), F32)]
            + ([shape((hidden, width), BF16)] if first else []),
        )
        if first:
            wdown = kept
        steps.keep(f"down{i}", du)
        for store, value in zip(
            (dus, sums_u, downs, out_parts), (du, usum, (own, rest, high), (oown, orest, ohigh))
        ):
            store.append(value)
        if i == 0:
            downs[0] = [own] + scatter_seq(steps, "dh2_0", rest, high)
        if i == slots - 1:
            made, up_rest = grad_kernels(steps, "gup", a2s, dus)
            up_sum.send(made)
        if i == 1 or slots == 1:
            dattns.append(gather_seq(steps, "dx_0", norm_two_back(0)))
        if i:
            downs[i] = [own] + scatter_seq(steps, f"dh2_{i}", rest, high)
    g_down = down_sum.finish(down_made)
    up_made = up_rest()
    nears, far = scatter_items(steps, "out", [(rest, high) for _, rest, high in out_parts])
    block_out_in = [own for own, _, _ in out_parts] + nears + far
    for i in range(1, slots):
        dattns.append(gather_seq(steps, f"dx_{i}", norm_two_back(i)))

    g_up = up_sum.finish(up_made)
    dqkvs, sums_q, sums1, back_parts = [], [], [], []
    for i in range(slots):
        dqkv, own, rest, high, qsum, sums = call(
            functools.partial(attention_back_kernel, cols, n_seq),
            "attention_back",
            [steps.gate(f"attb{i}", dattns[i][0])]
            + dattns[i][1:]
            + [qkvs[i], probss[i], hats[i]]
            + wqkv
            + wout,
            [shape((full, 3 * cols), BF16)]
            + outs3
            + [shape((1, 3 * cols), F32), shape((8, width), F32)],
            [
                pltpu.VMEM((full, width), BF16),
                pltpu.VMEM((full, cols), BF16),
                pltpu.VMEM((LANES, full), F32),
                pltpu.VMEM((LANES, full), F32),
            ],
        )
        back_parts.append((own, rest, high))
        steps.keep(f"attb{i}", dqkv)
        for store, value in zip((dqkvs, sums_q, sums1), (dqkv, qsum, sums)):
            store.append(value)
    nears, far = scatter_items(steps, "dh1", [(rest, high) for _, rest, high in back_parts])
    back_in = [own for own, _, _ in back_parts] + nears + far
    qkv_sum, out_sum = Scatter(steps, "gqkv"), Scatter(steps, "gout")
    made, qkv_rest = grad_kernels(steps, "gqkv", a1, dqkvs)
    qkv_sum.send(made)
    pieces = call(
        functools.partial(grad_out_kernel, flat_masks, tile, cols, hpiece, slots, n_seq),
        "grad_out",
        [steps.gate("gout", atts[0])]
        + atts[1:]
        + sum(dattns, [])
        + sums1
        + sums2
        + sums_q
        + sums_u,
        [shape((tile + blocks * piece, width), BF16)] * n_seq,
        [pltpu.VMEM((full, width), BF16), pltpu.VMEM((N_VEC, width), F32)],
    )
    pieces = exchange_seq(pieces)
    steps.keep("gout_seq", pieces[1:])
    made = call(
        functools.partial(grad_out_groups_kernel, flat_masks, tile),
        "grad_out_groups",
        [steps.gate("gout_groups", pieces[0])] + pieces[1:],
        [
            shape((2, VEC_ROWS + piece, width), BF16 if j else F32)
            for j in range(inner)
            for _ in range(2)
        ],
    )
    made = [[made[2 * j], made[2 * j + 1]] for j in range(inner)]
    out_sum.send(made)
    g_qkv = qkv_sum.finish(qkv_rest())
    g_out = out_sum.finish(made)
    g_wdown = total_of(g_down)
    block_out = call(
        functools.partial(block_out_kernel, slots, n_seq),
        "block_out",
        [steps.gate("block_out", block_out_in[0])] + block_out_in[1:] + x2s + [limits, vectors],
        [shape((slots, rows, width), F32)],
        specs=[VMEM] * (len(block_out_in) + slots) + [SMEM, VMEM],
    )[0]
    grad_tokens = call(
        functools.partial(norm_one_back_kernel, slots),
        "norm_one_back",
        [steps.gate("norm_one_back", back_in[0])] + back_in[1:] + dxs + [tokens, vectors],
        [shape((slots, rows, width), F32)],
    )[0]
    g_wout, *vecs = call(
        out_final_kernel,
        "out_final",
        [total_of(g_out)],
        [shape((piece, width), F32)]
        + [shape((1, piece), F32)] * N_VEC
        + [shape((1, hpiece), F32)],
    )

    if regular:
        steps.keep("block_out", block_out)
        steps.keep("norm_one_back", grad_tokens)
        g_qkv = [steps.gate("owners", g_qkv[0])] + list(g_qkv[1:])
        parts = exchange_seq(
            call(
                owners_kernel,
                "owners",
                list(g_qkv) + list(g_up),
                [shape((piece, 3 * cols + hidden), BF16)] * n_seq,
            )
        )
        g_wqkv, g_wup = call(
            functools.partial(unplace_kernel, cols, hpiece),
            "unplace",
            parts,
            [shape((piece, 3 * width), F32), shape((piece, hidden_all), F32)],
        )
    else:
        placed = []
        for parts in (g_qkv, g_up):
            parts = total_of(parts).astype(BF16).reshape(n_seq, piece, -1)
            parts = exchange_seq(
                [lax.dynamic_index_in_dim(parts, s ^ r, 0, False) for r in range(n_seq)]
            )
            out = jnp.zeros((n_seq,) + parts[0].shape, BF16)
            for r, part in enumerate(parts):
                out = lax.dynamic_update_index_in_dim(out, part, s ^ r, 0)
            placed.append(out.astype(F32))
        g_wqkv = placed[0].reshape(n_seq, piece, 3, cols).transpose(1, 2, 0, 3).reshape(piece, -1)
        g_wup = (
            placed[1].reshape(n_seq, piece, n_dp, hpiece).transpose(1, 2, 0, 3).reshape(piece, -1)
        )
    vecs = [v.reshape(-1) for v in vecs]
    return (
        block_out,
        grad_tokens,
        g_wqkv,
        vecs[0],
        vecs[1],
        g_wout,
        vecs[2],
        g_wup,
        vecs[8],
        g_wdown,
        vecs[3],
        vecs[4],
        vecs[5],
        vecs[6],
        vecs[7],
    )


def solution(mesh):
    both = ("dp", "seq")
    act = P("dp", "seq", None)
    mat = P(both, None)
    vec = P(both)
    return jax.shard_map(
        body,
        mesh=mesh,
        in_specs=(act, act, P("dp"), P("dp"), mat, vec, vec, mat, vec, mat, vec, mat)
        + (vec,) * 5,
        out_specs=(act, act, mat, vec, vec, mat, vec, mat, vec, mat) + (vec,) * 5,
        check_vma=False,
    )
```

```python
import functools

import jax
import jax.numpy as jnp
from jax import lax
from jax.experimental import pallas as pl
from jax.experimental.pallas import tpu as pltpu
from jax.sharding import PartitionSpec as P

HEAD_DIM = 64
LANES = 128
EPSILON = 1e-06
F32 = jnp.float32
BF16 = jnp.bfloat16
OUTER = 4
ORDER = (0, 2, 1, 3)
VMEM = pl.BlockSpec(memory_space=pltpu.VMEM)
ANY = pl.BlockSpec(memory_space=pl.ANY)
HBM = pl.BlockSpec(memory_space=pltpu.HBM)
SMEM = pl.BlockSpec(memory_space=pltpu.SMEM)
LIMIT = 14 * 1024 * 1024
WHOLE = 60 * 1024 * 1024
SOFTMAX_RATE = HEAD_DIM**-0.5 * 1.4426950408889634
WAITS = {
    "out_xa": ["out_z1"],
    "qkv_z1": ["qkv_z2"],
    "qkv_xa": ["out_z2"],
    "qkv_xb": ["out_xa"],
    "up_z2": ["out_xb"],
    "up_z1": ["place"],
    "up_xa": ["up_z2"],
    "down_z2": ["qkv_z1"],
    "down_z1": ["qkv_xa"],
    "down_xb": ["down_xa"],
    "tok_core": ["tok_y"],
    "cot_y": ["out_seq"],
    "mask": ["norm_one", "down_z2"],
    "att0": ["qkv_xb"],
    "x2_0_core": ["out_seq"],
    "x2_0_y": ["up_xa"],
    "norm0": ["x2_0_y"],
    "a2_0_y": ["out_seq"],
    "a2_0_core": ["mask"],
    "x2_1_core": ["tok_core"],
    "x2_1_y": ["tok_core", "cot_core", "att0"],
    "up0": ["att1"],
    "up1": ["a2_1_y", "x2_1_core", "a2_0_y"],
    "gdown_kept": ["down_z1"],
    "down0": ["gdown_sent"],
    "dh2_0_core": ["mask"],
    "dh2_0_y": ["x2_1_y", "up1", "norm0"],
    "down1": ["a2_0_core", "cot_y"],
    "gup_far": ["gdown_kept"],
    "gup_near": ["dh2_0_core"],
    "back0": ["x2_0_send"],
    "dx_0_y": ["x2_1_y", "gup_sent"],
    "dh2_1_y": ["dh2_0_send"],
    "gup_kept": ["dx_0_core", "back0", "norm1"],
    "out_y": ["dh2_1_send", "dh2_1_core", "out_core1"],
    "back1": ["out_core0"],
    "gup_z1": ["dx_1_core", "out_send", "gup_far"],
    "gup_z2": ["dh2_0_y", "back1"],
    "attb1": ["dx_0_core"],
    "dh1_core0": ["place", "gdown_z1"],
    "dh1_core1": ["dh1_core0"],
    "dh1_y": ["dh2_1_send", "dh1_core1"],
    "gqkv_far": ["attb1"],
    "gqkv_near": ["gqkv_sent"],
    "gout": ["dh1_core0", "gqkv_sent"],
    "gqkv_kept": ["gup_z2", "gqkv_near"],
    "gqkv_z1": ["gup_z2", "gup_z1", "gout_near"],
    "gqkv_z2": ["gqkv_kept"],
    "gout_z1": ["dh1_y", "dx_1_y"],
    "gout_z2": ["gout_far"],
    "block_out": ["gqkv_z1"],
    "owners": ["up_xb", "gout_z1", "gqkv_z2", "gqkv_far"],
}
N_VEC = 8
VEC_ROWS = 8


def dot(left, right):
    return jnp.dot(left, right, preferred_element_type=F32)


def dot_nt(left, right):
    return lax.dot_general(left, right, (((1,), (1,)), ((), ())), preferred_element_type=F32)


def dot_tn(left, right):
    return lax.dot_general(left, right, (((0,), (0,)), ((), ())), preferred_element_type=F32)


def swap(values, axis, mask):
    size = lax.axis_size(axis)
    return lax.ppermute(values, axis, [(i, i ^ mask) for i in range(size)])


def shape(dims, kind):
    return jax.ShapeDtypeStruct(tuple(dims), kind)


def call(kernel, name, ins, outs, scratch=(), specs=None, limit=LIMIT):
    return pl.pallas_call(
        kernel,
        name=name,
        out_shape=tuple(outs),
        in_specs=specs or [VMEM] * len(ins),
        out_specs=tuple([VMEM] * len(outs)),
        scratch_shapes=list(scratch),
        compiler_params=pltpu.CompilerParams(vmem_limit_bytes=limit),
        cost_estimate=pl.CostEstimate(
            flops=0, bytes_accessed=0, transcendentals=0
        ),
    )(*ins)


def aligned(index, size):
    return pl.multiple_of(index * size, size)


def place_blocks(refs, masks, out):
    own = lax.axis_index("dp")
    for ref, group in zip(refs, masks):
        rows = ref.shape[1]
        for i, mask in enumerate(group):
            out[pl.ds(aligned(own ^ mask, rows), rows), :] = ref[i]


def start_copies(jobs, scratch, sems):
    copies = []
    for src, block, rows in jobs:
        copy = pltpu.make_async_copy(
            src, scratch.at[pl.ds(aligned(block, rows), rows)], sems.at[len(copies)]
        )
        copy.start()
        copies.append(copy)
    return copies


def out_jobs(refs, tile, blocks):
    own = lax.axis_index("seq")
    size = len(refs)
    rows = (refs[0].shape[0] - tile) // blocks
    return [
        (ref.at[pl.ds(tile + b * rows, rows)], b * size + (own ^ r), rows)
        for r, ref in enumerate(refs)
        for b in range(blocks)
    ]


def pack_kernel(cols, hpiece, wqkv, wup, *outs):
    own = lax.axis_index("seq")
    size = len(outs)
    hidden = wup.shape[1] // size
    width = wqkv.shape[1] // 3
    for r, out in enumerate(outs):
        dest = own ^ r
        for i in range(3):
            at = pl.multiple_of(dest * cols + i * width, LANES)
            out[:, i * cols : (i + 1) * cols] = wqkv[:, pl.ds(at, cols)]
        for i in range(hidden // hpiece):
            at = pl.multiple_of((i * size + dest) * hpiece, LANES)
            start = 3 * cols + i * hpiece
            out[:, start : start + hpiece] = wup[:, pl.ds(at, hpiece)]


def place_kernel(*refs):
    size = len(refs) - 2
    qkv, up = refs[size:]
    own = lax.axis_index("seq")
    cut = qkv.shape[2]
    for r in range(size):
        rows = refs[r].shape[0]
        at = pl.ds(aligned(own ^ r, rows), rows)
        qkv[0, at, :] = refs[r][:, :cut]
        up[0, at, :] = refs[r][:, cut:]


def owners_kernel(*refs):
    left, right, outs = refs[:3], refs[3:6], refs[6:]
    own = lax.axis_index("seq")
    rows = outs[0].shape[0]
    cut = left[0].shape[2]
    for r, out in enumerate(outs):
        at = pl.ds(aligned(own ^ r, rows), rows)
        for parts, cols in ((left, slice(0, cut)), (right, slice(cut, out.shape[1]))):
            total = parts[0][0, at, :].astype(F32) + parts[1][0, at, :].astype(F32)
            out[:, cols] = (total + parts[2][0, at, :].astype(F32)).astype(BF16)


def unplace_kernel(cols, hpiece, *refs):
    *parts, qkv, up = refs
    size = len(parts)
    own = lax.axis_index("seq")
    width = qkv.shape[1] // 3
    for r, part in enumerate(parts):
        src = own ^ r
        for i in range(3):
            at = pl.multiple_of(src * cols + i * width, LANES)
            qkv[:, pl.ds(at, cols)] = part[:, i * cols : (i + 1) * cols].astype(F32)
        for i in range((part.shape[1] - 3 * cols) // hpiece):
            at = pl.multiple_of((i * size + src) * hpiece, LANES)
            start = 3 * cols + i * hpiece
            up[:, pl.ds(at, hpiece)] = part[:, start : start + hpiece].astype(F32)


def out_pack_kernel(tile, wout, *refs):
    n = N_VEC + 1
    vecs, out, landed, scratch, sems = refs[:n], refs[n], refs[n + 1 : -2], refs[-2], refs[-1]
    copies = [pltpu.make_async_copy(v, l, sems.at[i]) for i, (v, l) in enumerate(zip(vecs, landed))]
    for copy in copies:
        copy.start()
    out[0, tile:, :] = wout[...]
    scratch[...] = jnp.zeros_like(scratch)
    for copy in copies:
        copy.wait()
    for i, vec in enumerate(landed):
        row, lane = (0, i * LANES) if i < N_VEC else (1, 0)
        scratch[row : row + 1, lane : lane + vec.shape[0]] = vec[...].astype(F32)[None, :]
    out[0, :tile, :] = scratch[...].astype(BF16)


def out_pieces_kernel(masks, tile, blocks, *refs):
    n = len(masks)
    outs, mixed = refs[n:-1], refs[-1]
    d = lax.axis_index("dp")
    s = lax.axis_index("seq")
    flat = [(i, j) for i, group in enumerate(masks) for j in range(len(group))]
    mask_of = [mask for group in masks for mask in group]
    total = None
    for n, (i, j) in enumerate(flat):
        part = refs[i][j, :tile, :].astype(F32)
        part = pltpu.roll(part, 2 * n, 0) if n else part
        total = part if total is None else total + part
    mixed[...] = total.astype(BF16)
    piece = refs[0].shape[1] - tile
    for r, out in enumerate(outs):
        out[:tile, :] = mixed[...]
        for b in range(blocks):
            want = d ^ ((s ^ r) * blocks + b)
            for (i, j), mask in zip(flat, mask_of):

                @pl.when(want == mask)
                def _(out=out, b=b, i=i, j=j):
                    start = tile + b * piece
                    out[start : start + piece, :] = refs[i][j, tile:, :]


def vector_unpack_kernel(masks, tile, n_seq, cols, hpiece, *refs):
    parts, (vectors, qkv_bias, ubias) = refs[:n_seq], refs[n_seq:]
    width = vectors.shape[1]
    hidden = ubias.shape[1]
    mask_of = [mask for group in masks for mask in group]
    piece = width // (n_seq * len(mask_of))
    s = lax.axis_index("seq")
    d = lax.axis_index("dp")
    row = lax.broadcasted_iota(jnp.int32, (tile, 1), 0)
    dist = jnp.zeros_like(row)
    for n, mask in enumerate(mask_of):
        dist = jnp.where(row // 2 == n, mask, dist)
    source = d ^ dist
    lane = lax.broadcasted_iota(jnp.int32, (LANES, width), 1)
    sub = lax.broadcasted_iota(jnp.int32, (LANES, width), 0)
    spread = jnp.where(lane % piece == sub, 1.0, 0.0).astype(BF16)
    target = lax.broadcasted_iota(jnp.int32, (1, width), 1) // piece
    even = row % 2 == 0
    for i in range(N_VEC):
        total = None
        for r, part in enumerate(parts):
            tiled = dot(part[:tile, i * LANES : (i + 1) * LANES], spread)
            here = even & (source * n_seq + (s ^ r) == target)
            tiled = jnp.sum(jnp.where(here, tiled, 0.0), axis=0, keepdims=True)
            total = tiled if total is None else total + tiled
        vectors[i : i + 1, :] = total
    lane = lax.broadcasted_iota(jnp.int32, (LANES, hidden), 1)
    sub = lax.broadcasted_iota(jnp.int32, (LANES, hidden), 0)
    spread = jnp.where(lane % hpiece == sub, 1.0, 0.0).astype(BF16)
    target = lax.broadcasted_iota(jnp.int32, (1, hidden), 1) // hpiece
    tiled = dot(parts[0][:tile, :LANES], spread)
    here = (row % 2 == 1) & (source == target)
    ubias[...] = jnp.sum(jnp.where(here, tiled, 0.0), axis=0, keepdims=True)
    at = pl.ds(pl.multiple_of(s * cols, LANES), cols)
    qkv_bias[...] = jnp.zeros_like(qkv_bias)
    qkv_bias[:, :cols] = vectors[0:1, at]
    qkv_bias[:, 2 * cols :] = vectors[1:2, at]


def positions(block, rows, n_seq, axis):
    half = n_seq // 2
    owner = lax.axis_index("seq") ^ (2 * (block % half) + block // half)
    dims = (rows, 1) if axis == 0 else (1, rows)
    return owner * rows + lax.broadcasted_iota(jnp.int32, dims, axis)


def attention_kernel(masks, tile, blocks, cols, n_seq, item, *refs):
    first = item == 0
    a1, bias, lens = refs[:3]
    n = len(masks) if first else 1
    pieces, outs = refs[3 : 3 + n], refs[3 + n : 3 + n + (n_seq if first else 1)]
    refs = refs[3 + n + len(outs) :]
    if first:
        qkv, att, probs, own, rest, high, wqkv, wout, ok, sems = refs
    else:
        qkv, att, probs, own, rest, high, ok = refs
        (wqkv,), (wout,) = pieces, outs
    rows = a1.shape[0]
    cut = rows // 2
    blk = own.shape[0]
    out_copies = []
    if first:
        out_copies = start_copies(out_jobs(outs, tile, blocks), wout, sems)
        place_blocks(pieces, masks, wqkv)
    for q in range(n_seq):
        good = positions(q, blk, n_seq, 1) < lens[item]
        ok[:, q * blk : (q + 1) * blk] = jnp.where(good, 0.0, -1e30)
    for i in range(3):
        part = slice(i * cols, (i + 1) * cols)
        qkv[:, part] = (dot(a1[...], wqkv[:, part]) + bias[:, part]).astype(BF16)
    step_rows = min(256, rows)
    lane = lax.broadcasted_iota(jnp.int32, (1, LANES), 1)
    sides = [(lane < HEAD_DIM), (lane >= HEAD_DIM)]
    for pair in range(cols // LANES):
        at = slice(pair * LANES, (pair + 1) * LANES)
        keys = qkv[:, cols + pair * LANES : cols + (pair + 1) * LANES]
        vals = qkv[:, 2 * cols + pair * LANES : 2 * cols + (pair + 1) * LANES]
        split = [jnp.where(side, vals, jnp.zeros_like(vals)) for side in sides]

        def step(block, carry, pair=pair, at=at, keys=keys, split=split):
            place = pl.ds(aligned(block, step_rows), step_rows)
            query = qkv[place, at]
            total = None
            for h in range(2):
                q = jnp.where(sides[h], query, jnp.zeros_like(query))
                scores = dot_nt(q, keys) + ok[...]
                peak = jnp.max(scores, axis=-1, keepdims=True)
                expo = jnp.exp2((scores - peak) * SOFTMAX_RATE)
                rate = 1.0 / jnp.sum(expo, axis=-1, keepdims=True)
                low = (expo * rate).astype(BF16)
                probs[2 * pair + h, place, :] = low
                out = dot(low, split[h])
                total = out if total is None else total + out
            att[place, at] = total.astype(BF16)
            return carry

        lax.fori_loop(0, rows // step_rows, step, 0)
    for copy in out_copies:
        copy.wait()
    high[...] = dot(att[cut:, :], wout[...]).astype(BF16)
    own[...] = dot(att[:blk, :], wout[...])
    rest[...] = dot(att[blk:cut, :], wout[...])


def attention_back_kernel(cols, n_seq, *refs):
    parts = refs[:n_seq]
    qkv, probs, hat, wqkv, wout = refs[n_seq : n_seq + 5]
    dqkv, own, rest, high, sums, sums_one, grad, datt, dkt, dvt = refs[n_seq + 5 :]
    rows = dqkv.shape[0]
    cut = rows // 2
    blk = own.shape[0]
    for i, part in enumerate(parts):
        grad[i * blk : (i + 1) * blk, :] = part[...]
    datt[...] = dot_nt(grad[...], wout[...]).astype(BF16)
    step_rows = min(256, rows)
    lane = lax.broadcasted_iota(jnp.int32, (1, LANES), 1)
    sides = [(lane < HEAD_DIM), (lane >= HEAD_DIM)]
    scale = HEAD_DIM**-0.5
    for pair in range(cols // LANES):
        at = slice(pair * LANES, (pair + 1) * LANES)
        at_k = slice(cols + pair * LANES, cols + (pair + 1) * LANES)
        at_v = slice(2 * cols + pair * LANES, 2 * cols + (pair + 1) * LANES)
        keys = qkv[:, at_k]
        vals = qkv[:, at_v]
        split = [jnp.where(side, keys, jnp.zeros_like(keys)) for side in sides]
        dkt[...] = jnp.zeros_like(dkt)
        dvt[...] = jnp.zeros_like(dvt)

        def step(block, carry, pair=pair, at=at, vals=vals, split=split):
            place = pl.ds(aligned(block, step_rows), step_rows)
            gatt = datt[place, at]
            query = qkv[place, at]
            gatt_t = gatt.T
            query_t = query.T
            total = None
            for h in range(2):
                g = jnp.where(sides[h], gatt, jnp.zeros_like(gatt))
                gp = dot_nt(g, vals)
                low = probs[2 * pair + h, place, :]
                p = low.astype(F32)
                mean = jnp.sum(gp * p, axis=-1, keepdims=True)
                gs = (p * (gp - mean)).astype(BF16)
                half = slice(h * HEAD_DIM, (h + 1) * HEAD_DIM)
                dvt[half, :] += dot(gatt_t[half, :], low)
                dkt[half, :] += dot(query_t[half, :], gs)
                out = dot(gs, split[h])
                total = out if total is None else total + out
            dqkv[place, at] = (total * scale).astype(BF16)
            return carry

        lax.fori_loop(0, rows // step_rows, step, 0)
        dqkv[:, at_k] = (dkt[...].T * scale).astype(BF16)
        dqkv[:, at_v] = dvt[...].T.astype(BF16)
    sums[...] = jnp.sum(dqkv[...].astype(F32), axis=0, keepdims=True)
    sums_one[...] = jnp.zeros_like(sums_one)

    def last(block, carry):
        at = pl.ds(aligned(block, 256), 256)
        value = dot_nt(dqkv[...], wqkv[at, :])
        own[:, at] = value[:blk]
        rest[:, at] = value[blk:cut]
        high[:, at] = value[cut:].astype(BF16)
        sums_one[0:1, at] = jnp.sum(value * hat[:, at].astype(F32), axis=0, keepdims=True)
        sums_one[1:2, at] = jnp.sum(value, axis=0, keepdims=True)
        return carry

    lax.fori_loop(0, wqkv.shape[0] // 256, last, 0, unroll=2)


def up_kernel(masks, n_seq, item, *refs):
    first = item == 0
    n = len(masks) if first else 1
    parts, bias = refs[:n_seq], refs[n_seq]
    pieces = refs[n_seq + 1 : n_seq + 1 + n]
    if first:
        a2, act, slope, wup = refs[n_seq + 1 + n :]
        place_blocks(pieces, masks, wup)
    else:
        a2, act, slope = refs[n_seq + 1 + n :]
        (wup,) = pieces
    blk = parts[0].shape[0]
    rows = a2.shape[0]
    width = min(256, act.shape[1])
    for i, part in enumerate(parts):
        a2[i * blk : (i + 1) * blk, :] = part[...]
    half = min(256, rows)
    for i in range(rows // half):
        place = slice(i * half, (i + 1) * half)

        def step(block, carry, place=place):
            at = pl.ds(aligned(block, width), width)
            u = dot(a2[place, :], wup[:, at]) + bias[:, at]
            cdf = 0.5 * (1.0 + lax.erf(u * 0.7071067811865476))
            bell = jnp.exp2(u * u * -0.7213475204444817) * 0.3989422804014327
            act[place, at] = (u * cdf).astype(BF16)
            slope[place, at] = cdf + u * bell
            return carry

        lax.fori_loop(0, act.shape[1] // width, step, 0)


def down_kernel(masks, item, *refs):
    n = len(masks) if item == 0 else 1
    dy, act, slope, wup = refs[:4]
    downs = refs[4 : 4 + n]
    if item == 0:
        du, own, rest, high, oown, orest, ohigh, sums, wdown = refs[4 + n :]
        place_blocks(downs, masks, wdown)
    else:
        du, own, rest, high, oown, orest, ohigh, sums = refs[4 + n :]
        (wdown,) = downs
    rows = dy.shape[0]
    cut = rows // 2
    blk = own.shape[0]
    hidden = act.shape[1]
    width = min(256, hidden)

    def first(block, carry):
        at = pl.ds(aligned(block, width), width)
        value = (slope[:, at] * dot_nt(dy[...], wdown[at, :])).astype(BF16)
        du[:, at] = value
        sums[:, at] = jnp.sum(value.astype(F32), axis=0, keepdims=True)
        return carry

    lax.fori_loop(0, hidden // width, first, 0)

    def second(block, carry):
        at = pl.ds(aligned(block, 256), 256)
        value = dot_nt(du[...], wup[at, :])
        own[:, at] = value[:blk]
        rest[:, at] = value[blk:cut]
        high[:, at] = value[cut:].astype(BF16)
        value = dot(act[...], wdown[:, at])
        oown[:, at] = value[:blk]
        orest[:, at] = value[blk:cut]
        ohigh[:, at] = value[cut:].astype(BF16)
        return carry

    lax.fori_loop(0, wup.shape[0] // 256, second, 0)


def grad_kernel(j, inner, slots, *refs):
    lefts, rights = refs[:slots], refs[slots : 2 * slots]
    *outs, turned = refs[2 * slots :]
    rows = lefts[0].shape[0]
    each, blk = outs[0].shape[:2]
    own = lax.axis_index("dp")
    for n, k in enumerate(ORDER):
        at = pl.ds(aligned(own ^ (k * inner + j), blk), blk)
        for i, left in enumerate(lefts):
            turned[n * blk : (n + 1) * blk, i * rows : (i + 1) * rows] = left[:, at].T
    width = min(256, outs[0].shape[2])

    def step(block, carry):
        at = pl.ds(aligned(block, width), width)
        total = None
        for i, right in enumerate(rights):
            out = dot(turned[:, i * rows : (i + 1) * rows], right[:, at])
            total = out if total is None else total + out
        for n in range(len(ORDER)):
            out = outs[n // each]
            out[n % each, :, at] = total[n * blk : (n + 1) * blk].astype(out.dtype)
        return carry

    lax.fori_loop(0, outs[0].shape[2] // width, step, 0, unroll=True)


def grad_out_kernel(masks, tile, cols, hpiece, slots, n_seq, *refs):
    take = lambda n: (refs[:n], refs[n:])
    lefts, refs = take(slots)
    rights, refs = take(slots * n_seq)
    sums1, refs = take(slots)
    sums2, refs = take(slots)
    sums_q, refs = take(slots)
    sums_u, refs = take(slots)
    outs, (scratch, wide) = take(n_seq)[0], refs[n_seq:]
    width = wide.shape[1]
    s = lax.axis_index("seq")
    d = lax.axis_index("dp")
    total = lambda refs: functools.reduce(lambda a, b: a + b, [ref[...] for ref in refs])
    q, u = total(sums_q), total(sums_u)
    one, two = total(sums1), total(sums2)
    wide[...] = jnp.zeros_like(wide)
    at = pl.ds(pl.multiple_of(s * cols, LANES), cols)
    wide[0:1, at] = q[:, :cols]
    wide[1:2, at] = q[:, 2 * cols :]
    wide[2:4, :] = two[:2]
    wide[4:6, :] = one[:2]
    wide[6:8, :] = two[2:4]
    piece = width // (n_seq * len(masks))
    row = lax.broadcasted_iota(jnp.int32, (n_seq * tile, 1), 0)
    near = row % tile
    dist = jnp.zeros_like(row)
    for n, mask in enumerate(masks):
        dist = jnp.where(near // 2 == n, mask, dist)
    dest = (d ^ dist) * n_seq + (s ^ (row // tile))
    dest = jnp.where(near % 2 == 0, dest, -1)
    spread = jnp.where(
        lax.broadcasted_iota(jnp.int32, (width, LANES), 0) % piece
        == lax.broadcasted_iota(jnp.int32, (width, LANES), 1),
        1.0,
        0.0,
    ).astype(BF16)
    here = lax.broadcasted_iota(jnp.int32, (1, width), 1) // piece == dest
    vecs = []
    for i in range(N_VEC):
        vecs.append(dot(jnp.where(here, wide[i : i + 1, :], 0.0).astype(BF16), spread))
    hidden = u.shape[1]
    spread = jnp.where(
        lax.broadcasted_iota(jnp.int32, (hidden, LANES), 0) % hpiece
        == lax.broadcasted_iota(jnp.int32, (hidden, LANES), 1),
        1.0,
        0.0,
    ).astype(BF16)
    dest = jnp.where(near % 2 == 1, d ^ dist, -1)[:tile]
    here = lax.broadcasted_iota(jnp.int32, (1, hidden), 1) // hpiece == dest
    long = dot(jnp.where(here, u, 0.0).astype(BF16), spread)
    for r, out in enumerate(outs):
        for i, vec in enumerate(vecs):
            value = vec[r * tile : (r + 1) * tile]
            if r == 0 and i == 0:
                value = value + long
            out[:tile, i * LANES : (i + 1) * LANES] = value.astype(BF16)
    rows = rights[0].shape[0]
    blocks = (outs[0].shape[0] - tile) // piece
    grad = None
    for i, left in enumerate(lefts):
        for q in range(n_seq):
            scratch[q * rows : (q + 1) * rows, :] = rights[i * n_seq + q][...]
        part = dot_tn(left[...], scratch[...])
        grad = part if grad is None else grad + part
    grad = grad.astype(BF16)
    for other in range(n_seq):
        for r in range(n_seq):

            @pl.when(s ^ r == other)
            def _(other=other, r=r):
                for b in range(blocks):
                    at = (b * n_seq + other) * piece
                    start = tile + b * piece
                    outs[r][start : start + piece, :] = grad[at : at + piece]


def grad_out_groups_kernel(masks, tile, *refs):
    n_out = len(masks) // 2
    pieces, outs = refs[:-n_out], refs[-n_out:]
    size = len(pieces)
    head = VEC_ROWS
    rows = outs[0].shape[1] - head
    blocks = (pieces[0].shape[0] - tile) // rows
    d = lax.axis_index("dp")
    s = lax.axis_index("seq")
    total = None
    for piece in pieces:
        part = piece[:tile, :].astype(F32)
        total = part if total is None else total + part
    row = lax.broadcasted_iota(jnp.int32, (tile, 1), 0)
    for n, mask in enumerate(masks):
        out, i = outs[n // 2], n % 2
        value = pltpu.roll(total, tile - 2 * n, 0) if n else total
        out[i, :head, :] = jnp.where(row < 2, value, 0.0)[:head].astype(out.dtype)
        for r in range(size):
            for b in range(blocks):

                @pl.when(d ^ mask == (s ^ r) * blocks + b)
                def _(out=out, i=i, r=r, b=b):
                    start = tile + b * rows
                    out[i, head:, :] = pieces[r][start : start + rows, :].astype(out.dtype)


def out_final_kernel(total, grad, *vecs):
    grad[...] = total[VEC_ROWS:, :]
    for i, vec in enumerate(vecs[:-1]):
        vec[...] = total[0:1, i * LANES : i * LANES + vec.shape[1]]
    vecs[-1][...] = total[1:2, : vecs[-1].shape[1]]


def items_kernel(*refs):
    slots, blk = refs[-1].shape[:2]
    rests, nears, outs = refs[:slots], refs[slots : 2 * slots], refs[2 * slots :]
    for i in range(slots):
        for j, out in enumerate(outs):
            near = nears[i][(j + 1) * blk : (j + 2) * blk, :].astype(F32)
            out[i] = (rests[i][j * blk : (j + 1) * blk, :] + near).astype(BF16)


def item_sum(item, own, near, far, blk):
    total = own[...] + near[:blk, :].astype(F32)
    for ref in far:
        total = total + ref[item].astype(F32)
    return total


def gathered_sum(own, near, far, blk):
    total = own[...] + near[:blk, :].astype(F32)
    for ref in far:
        total = total + ref[...].astype(F32)
    return total


def stats(values):
    center = values - jnp.mean(values, axis=-1, keepdims=True)
    rate = lax.rsqrt(jnp.mean(center * center, axis=-1, keepdims=True) + EPSILON)
    return center * rate, rate


def norm_kernel(n_seq, *refs):
    parts, vectors, outs = refs[:n_seq], refs[n_seq], refs[n_seq + 1 :]
    rows = parts[0].shape[1]
    outs, hats = outs[: len(outs) // 2], outs[len(outs) // 2 :]
    for i, (out, kept) in enumerate(zip(outs, hats)):
        for q, part in enumerate(parts):
            hat, _ = stats(part[i].astype(F32))
            kept[q * rows : (q + 1) * rows, :] = hat.astype(BF16)
            out[q * rows : (q + 1) * rows, :] = (
                hat * vectors[4:5, :] + vectors[5:6, :]
            ).astype(BF16)


def mask_kernel(n_seq, *refs):
    parts, limits, outs = refs[:n_seq], refs[n_seq], refs[n_seq + 1 :]
    rows = parts[0].shape[1]
    for i, out in enumerate(outs):
        for q, part in enumerate(parts):
            good = jnp.where(positions(q, rows, n_seq, 0) < limits[i], 1.0, 0.0)
            out[q * rows : (q + 1) * rows, :] = (part[i].astype(F32) * good).astype(BF16)


def norm_two_kernel(item, own, near, *refs):
    *far, x, vectors, x2, a2 = refs
    value = x[item].astype(F32) + (
        gathered_sum(own, near, far, x2.shape[0]) + vectors[2:3, :]
    )
    x2[...] = value
    hat, _ = stats(value)
    a2[...] = (hat * vectors[6:7, :] + vectors[7:8, :]).astype(BF16)


def norm_back(grad, gain, hat, rate):
    scaled = grad * gain
    return rate * (
        scaled
        - jnp.mean(scaled, axis=-1, keepdims=True)
        - hat * jnp.mean(scaled * hat, axis=-1, keepdims=True)
    )


def norm_two_back_kernel(own, near, *refs):
    *far, x2, dy, vectors, dx2, low, sums = refs
    grad = gathered_sum(own, near, far, x2.shape[0])
    hat, rate = stats(x2[...])
    rows = dy[: x2.shape[0], :].astype(F32)
    value = rows + norm_back(grad, vectors[6:7, :], hat, rate)
    dx2[...] = value
    rounded = value.astype(BF16)
    low[...] = rounded
    sums[0:1, :] = jnp.sum(rounded.astype(F32), axis=0, keepdims=True)
    sums[1:2, :] = jnp.sum(rows, axis=0, keepdims=True)
    sums[2:3, :] = jnp.sum(grad * hat, axis=0, keepdims=True)
    sums[3:4, :] = jnp.sum(grad, axis=0, keepdims=True)
    sums[4:8, :] = jnp.zeros_like(sums[4:8, :])


def norm_one_back_kernel(slots, *refs):
    owns, nears, refs = refs[:slots], refs[slots : 2 * slots], refs[2 * slots :]
    *far, x, vectors, out = refs
    far, dxs = far[:-slots], far[-slots:]
    for i in range(slots):
        grad = item_sum(i, owns[i], nears[i], far, x.shape[1])
        hat, rate = stats(x[i].astype(F32))
        out[i] = dxs[i][...] + norm_back(grad, vectors[4:5, :], hat, rate)


def block_out_kernel(slots, n_seq, *refs):
    owns, nears, refs = refs[:slots], refs[slots : 2 * slots], refs[2 * slots :]
    *far, limits, vectors, out = refs
    far, x2s = far[:-slots], far[-slots:]
    for i, x2 in enumerate(x2s):
        blk = x2.shape[0]
        value = x2[...] + item_sum(i, owns[i], nears[i], far, blk) + vectors[3:4, :]
        good = jnp.where(positions(0, blk, n_seq, 0) < limits[i], 1.0, 0.0)
        out[i] = value * good


def exchange_seq(pieces):
    return [swap(piece, "seq", r) if r else piece for r, piece in enumerate(pieces)]


def gather_masks():
    inner = lax.axis_size("dp") // OUTER
    return [
        tuple(k * inner ^ j for k in pair) for pair in (ORDER[:2], ORDER[2:]) for j in range(inner)
    ]


def total_of(parts):
    return functools.reduce(lambda a, b: a + b, [part[0].astype(F32) for part in parts])


class Steps:
    def __init__(self):
        self.known = {}

    def keep(self, name, value):
        self.known[name] = value
        return value

    def send(self, name, value, axis, mask):
        return self.keep(name, swap(value, axis, mask))

    def gate(self, name, value):
        others = [self.known[key] for key in WAITS.get(name, ()) if key in self.known]
        return lax.optimization_barrier((value, others))[0] if others else value


def inner_masks():
    inner = lax.axis_size("dp") // OUTER
    out, bit = [], 1
    while bit < inner:
        out.append(bit)
        bit *= 2
    return out


def gather_dp(steps, name, block):
    inner = lax.axis_size("dp") // OUTER
    far = steps.send(name + "_z2", steps.gate(name + "_z2", block), "dp", 2 * inner)
    pair = jnp.concatenate([block, far], 0)
    other = steps.send(name + "_z1", steps.gate(name + "_z1", pair), "dp", inner)
    out = []
    for part, key in ((pair, name + "_xa"), (other, name + "_xb")):
        group = [part]
        for bit in inner_masks():
            group += [swap(steps.gate(key, p), "dp", bit) for p in group]
        steps.keep(key, group[1:])
        out += group
    return out


def scatter_first(steps, name, made, part):
    pairs = [group[part] for group in made[1:2] if len(made) == 2]
    steps.keep(name, [swap(steps.gate(name, pair), "dp", 1) for pair in pairs])
    return steps.known[name]


def inner_sum(parts, early):
    parts = [parts[0].astype(F32)] + list(parts[1:])
    for bit in inner_masks():
        for j in range(0, len(parts), 2 * bit):
            if len(parts) == 2:
                got = early[0]
            else:
                got = swap(parts[j + bit].astype(BF16), "dp", bit)
            parts[j] = parts[j].astype(F32) + got.astype(F32)
    return parts[0]


class Scatter:
    def __init__(self, steps, name):
        self.steps, self.name = steps, name

    def send(self, made):
        self.far = scatter_first(self.steps, self.name + "_far", made, 1)
        self.near = scatter_first(self.steps, self.name + "_near", made, 0)

    def finish(self, groups):
        steps, name = self.steps, self.name
        inner = len(groups)
        far = inner_sum([group[1] for group in groups], self.far).astype(BF16)
        got = steps.send(name + "_z1", steps.gate(name + "_z1", far), "dp", inner)
        near = inner_sum([group[0] for group in groups], self.near)
        send = (near[1:] + got[1:].astype(F32)).astype(BF16)
        tail = steps.send(name + "_z2", steps.gate(name + "_z2", send), "dp", 2 * inner)
        return near, got, tail


def scatter_seq(steps, name, rest, high):
    half = lax.axis_size("seq") // 2
    near = steps.send(name + "_core", steps.gate(name + "_core", high), "seq", 1)
    blk = near.shape[0] // half
    send = (rest + near[blk:].astype(F32)).astype(BF16)
    send = steps.gate(name + "_y", steps.keep(name + "_send", send))
    far = [swap(send[(j - 1) * blk : j * blk], "seq", 2 * j) for j in range(1, half)]
    return [near] + steps.keep(name + "_y", far)


def scatter_items(steps, name, parts):
    half = lax.axis_size("seq") // 2
    slots = len(parts)
    nears = [
        steps.send(f"{name}_core{i}", steps.gate(f"{name}_core{i}", high), "seq", 1)
        for i, (_, high) in enumerate(parts)
    ]
    rests = [rest for rest, _ in parts]
    blk = nears[0].shape[0] // half
    width = nears[0].shape[1]
    sends = call(
        items_kernel,
        "items",
        rests + nears,
        [shape((slots, blk, width), BF16)] * (half - 1),
    )
    sends = steps.gate(name + "_y", steps.keep(name + "_send", list(sends)))
    far = [swap(send, "seq", 2 * (j + 1)) for j, send in enumerate(sends)]
    steps.keep(name + "_y", far)
    return nears, far


def gather_seq(steps, name, block):
    half = lax.axis_size("seq") // 2
    block = steps.gate(name + "_y", block)
    far = steps.keep(name + "_y", [swap(block, "seq", 2 * j) for j in range(1, half)])
    mine = [block] + far
    other = [swap(block, "seq", 1)]
    other += [swap(steps.gate(name + "_core", part), "seq", 1) for part in far]
    steps.keep(name + "_core", other)
    return mine + other


def grad_kernels(steps, name, lefts, rights):
    lefts, rights = list(lefts), list(rights)
    inner = lax.axis_size("dp") // OUTER
    slots = len(lefts)
    blk = lefts[0].shape[1] // (OUTER * inner)
    width = rights[0].shape[1]
    rows = lefts[0].shape[0]
    if blk % LANES:
        own = lax.axis_index("dp")
        whole = sum(dot_tn(a, b) for a, b in zip(lefts, rights)).reshape(-1, blk, width)
        take = lambda k: lax.dynamic_index_in_dim(whole, own ^ k, 0)
        made = []
        for j in range(inner):
            got = [take(k * inner + j) for k in ORDER]
            made.append([jnp.concatenate(got[:2], 0), jnp.concatenate(got[2:], 0)])
        return made, lambda: made
    made = [None] * inner

    def make(j):
        key = name + ("_sent" if j else "_kept")
        made[j] = steps.keep(
            key,
            list(
                call(
                    functools.partial(grad_kernel, j, inner, slots),
                    key,
                    [steps.gate(key, lefts[0])] + lefts[1:] + rights,
                    [shape((2, blk, width), BF16 if j else F32)] * 2,
                    [pltpu.VMEM((4 * blk, slots * rows), BF16)],
                )
            ),
        )

    def rest():
        make(0)
        return made

    for j in range(1, inner):
        make(j)
    return made, rest


def body(
    tokens,
    cotangent,
    item_count,
    valid_len,
    w_qkv,
    q_bias,
    v_bias,
    w_out,
    out_bias,
    w_up,
    up_bias,
    w_down,
    down_bias,
    gain_one,
    shift_one,
    gain_two,
    shift_two,
):
    slots, rows, width = tokens.shape
    n_seq = lax.axis_size("seq")
    n_dp = lax.axis_size("dp")
    inner = n_dp // OUTER
    count = n_seq * n_dp
    half = n_seq // 2
    cut = half * rows
    full = n_seq * rows
    cols = width // n_seq
    heads = cols // HEAD_DIM
    piece = width // count
    hidden_all = w_up.shape[1]
    hidden = hidden_all // n_seq
    hpiece = hidden_all // count
    blocks = n_dp // n_seq
    regular = hpiece % LANES == 0 and piece % 16 == 0

    limits = jnp.where(jnp.arange(slots) < item_count[0], valid_len, 0)
    dma = lambda n: pltpu.SemaphoreType.DMA((n,))

    rows_in = [
        q_bias,
        v_bias,
        out_bias,
        down_bias,
        gain_one,
        shift_one,
        gain_two,
        shift_two,
        up_bias,
    ]
    tile = max(16, 2 * n_dp)
    masks = gather_masks()
    n_parts = len(masks)
    flat_masks = [k * inner + j for j in range(inner) for k in ORDER]
    steps = Steps()
    out_block = call(
        functools.partial(out_pack_kernel, tile),
        "out_pack",
        [w_out] + rows_in,
        [shape((1, tile + piece, width), BF16)],
        [pltpu.VMEM(v.shape, BF16) for v in rows_in]
        + [pltpu.VMEM((tile, width), F32), dma(N_VEC + 1)],
        [VMEM] + [HBM] * (N_VEC + 1),
        WHOLE,
    )[0]
    if regular:
        packed = call(
            functools.partial(pack_kernel, cols, hpiece),
            "pack",
            [w_qkv, w_up],
            [shape((piece, 3 * cols + hidden), BF16)] * n_seq,
        )
        own_qkv, own_up = call(
            place_kernel,
            "place",
            exchange_seq(packed),
            [
                shape((1, n_seq * piece, 3 * cols), BF16),
                shape((1, n_seq * piece, hidden), BF16),
            ],
        )
    else:
        s = lax.axis_index("seq")
        split = jnp.concatenate(
            [
                w_qkv.reshape(piece, 3, n_seq, cols).transpose(2, 0, 1, 3).reshape(n_seq, piece, -1),
                w_up.reshape(piece, n_dp, n_seq, hpiece)
                .transpose(2, 0, 1, 3)
                .reshape(n_seq, piece, -1),
            ],
            -1,
        )
        packed = [lax.dynamic_index_in_dim(split, s ^ r, 0, False) for r in range(n_seq)]
        placed = jnp.zeros_like(split)
        for r, part in enumerate(exchange_seq(packed)):
            placed = lax.dynamic_update_index_in_dim(placed, part, s ^ r, 0)
        placed = placed.reshape(1, n_seq * piece, -1)
        own_qkv, own_up = placed[:, :, : 3 * cols], placed[:, :, 3 * cols :]

    steps.keep("place", [own_qkv, own_up])
    out_all = gather_dp(steps, "out", out_block)
    wqkv = gather_dp(steps, "qkv", own_qkv)
    wup = gather_dp(steps, "up", own_up)
    wdown = gather_dp(steps, "down", w_down[None])
    wout = exchange_seq(
        call(
            functools.partial(out_pieces_kernel, masks, tile, blocks),
            "out_pieces",
            [steps.gate("out_pieces", out_all[0])] + out_all[1:],
            [shape((tile + blocks * piece, width), BF16)] * n_seq,
            [pltpu.VMEM((tile, width), BF16)],
        )
    )
    steps.keep("out_seq", wout[1:])
    tok = gather_seq(steps, "tok", tokens)
    cot = gather_seq(steps, "cot", cotangent)
    vectors, qkv_bias, ubias = call(
        functools.partial(vector_unpack_kernel, masks, tile, n_seq, cols, hpiece),
        "vector_unpack",
        [steps.gate("vectors", wout[0])] + wout[1:],
        [shape((N_VEC, width), F32), shape((1, 3 * cols), F32), shape((1, hidden), F32)],
    )
    a1 = call(
        functools.partial(norm_kernel, n_seq),
        "norm_one",
        [steps.gate("norm_one", tok[0])] + tok[1:] + [vectors],
        [shape((full, width), BF16)] * (2 * slots),
    )
    a1, hats = list(a1[:slots]), list(a1[slots:])
    steps.keep("norm_one", a1)
    dys = call(
        functools.partial(mask_kernel, n_seq),
        "mask",
        [steps.gate("mask", cot[0])] + cot[1:] + [limits],
        [shape((full, width), BF16)] * slots,
        specs=[VMEM] * n_seq + [SMEM],
    )
    steps.keep("mask", dys)

    outs3 = [shape((rows, width), F32), shape((cut - rows, width), F32), shape((cut, width), BF16)]
    qkvs, atts, probss, x2s, a2s, acts, slopes, a2_of = [], [], [], [], [], [], [], []
    for i in range(slots):
        first = i == 0
        qkv, att, probs, own, rest, high, *kept = call(
            functools.partial(attention_kernel, masks, tile, blocks, cols, n_seq, i),
            "attention",
            [steps.gate(f"att{i}", a1[i]), qkv_bias, valid_len] + wqkv + wout,
            [
                shape((full, 3 * cols), BF16),
                shape((full, cols), BF16),
                shape((heads, full, full), BF16),
            ]
            + outs3
            + ([shape((width, 3 * cols), BF16), shape((cols, width), BF16)] if first else []),
            [pltpu.VMEM((1, full), F32)] + ([dma(n_dp)] if first else []),
            [VMEM] * 2 + [SMEM] + ([VMEM] * n_parts + [ANY] * n_seq if first else [VMEM] * 2),
        )
        if first:
            wqkv, wout = [kept[0]], [kept[1]]
        steps.keep(f"att{i}", att)
        for store, value in zip((qkvs, atts, probss, a2_of), (qkv, att, probs, (own, rest, high))):
            store.append(value)
        if i == 0:
            a2_of[0] = [own] + scatter_seq(steps, "x2_0", rest, high)
        if i == 1 or slots == 1:
            norm_two_of = lambda i: call(
                functools.partial(norm_two_kernel, i),
                "norm_two",
                [steps.gate(f"norm{i}", a2_of[i][0])] + a2_of[i][1:] + [tokens, vectors],
                [shape((rows, width), F32), shape((rows, width), BF16)],
            )
            x2, a2 = norm_two_of(0)
            x2s.append(x2)
            a2_of[0] = gather_seq(steps, "a2_0", steps.keep("norm0", a2))
        if i:
            own, rest, high = a2_of[i]
            a2_of[i] = [own] + scatter_seq(steps, f"x2_{i}", rest, high)

    for i in range(slots):
        first = i == 0
        if i:
            x2, a2 = norm_two_of(i)
            x2s.append(x2)
            a2_of[i] = gather_seq(steps, f"a2_{i}", steps.keep(f"norm{i}", a2))
        a2, act, slope, *kept = call(
            functools.partial(up_kernel, masks, n_seq, i),
            "up",
            [steps.gate(f"up{i}", a2_of[i][0])] + a2_of[i][1:] + [ubias] + wup,
            [
                shape((full, width), BF16),
                shape((full, hidden), BF16),
                shape((full, hidden), F32),
            ]
            + ([shape((width, hidden), BF16)] if first else []),
        )
        if first:
            wup = kept
        steps.keep(f"up{i}", act)
        for store, value in zip((a2s, acts, slopes), (a2, act, slope)):
            store.append(value)

    dus, dxs, dattns, sums2, sums_u, downs = [], [], [], [], [], []
    down_sum, up_sum = Scatter(steps, "gdown"), Scatter(steps, "gup")
    made, down_rest = grad_kernels(steps, "gdown", acts, dys)
    down_sum.send(made)
    down_made = down_rest()

    def norm_two_back(i):
        dx2, low, sums = call(
            norm_two_back_kernel,
            "norm_two_back",
            [steps.gate(f"back{i}", downs[i][0])] + downs[i][1:] + [x2s[i], dys[i], vectors],
            [shape((rows, width), F32), shape((rows, width), BF16), shape((8, width), F32)],
        )
        for store, value in zip((dxs, sums2), (dx2, sums)):
            store.append(value)
        return steps.keep(f"back{i}", low)

    out_parts = []
    for i in range(slots):
        first = i == 0
        du, own, rest, high, oown, orest, ohigh, usum, *kept = call(
            functools.partial(down_kernel, masks, i),
            "down",
            [steps.gate(f"down{i}", dys[i]), acts[i], slopes[i]] + wup + wdown,
            [shape((full, hidden), BF16)]
            + outs3
            + outs3
            + [shape((1, hidden), F32)]
            + ([shape((hidden, width), BF16)] if first else []),
        )
        if first:
            wdown = kept
        steps.keep(f"down{i}", du)
        for store, value in zip(
            (dus, sums_u, downs, out_parts), (du, usum, (own, rest, high), (oown, orest, ohigh))
        ):
            store.append(value)
        if i == 0:
            downs[0] = [own] + scatter_seq(steps, "dh2_0", rest, high)
        if i == slots - 1:
            made, up_rest = grad_kernels(steps, "gup", a2s, dus)
            up_sum.send(made)
        if i == 1 or slots == 1:
            dattns.append(gather_seq(steps, "dx_0", norm_two_back(0)))
        if i:
            downs[i] = [own] + scatter_seq(steps, f"dh2_{i}", rest, high)
    g_down = down_sum.finish(down_made)
    up_made = up_rest()
    nears, far = scatter_items(steps, "out", [(rest, high) for _, rest, high in out_parts])
    block_out_in = [own for own, _, _ in out_parts] + nears + far
    for i in range(1, slots):
        dattns.append(gather_seq(steps, f"dx_{i}", norm_two_back(i)))

    g_up = up_sum.finish(up_made)
    dqkvs, sums_q, sums1, back_parts = [], [], [], []
    for i in range(slots):
        dqkv, own, rest, high, qsum, sums = call(
            functools.partial(attention_back_kernel, cols, n_seq),
            "attention_back",
            [steps.gate(f"attb{i}", dattns[i][0])]
            + dattns[i][1:]
            + [qkvs[i], probss[i], hats[i]]
            + wqkv
            + wout,
            [shape((full, 3 * cols), BF16)]
            + outs3
            + [shape((1, 3 * cols), F32), shape((8, width), F32)],
            [
                pltpu.VMEM((full, width), BF16),
                pltpu.VMEM((full, cols), BF16),
                pltpu.VMEM((LANES, full), F32),
                pltpu.VMEM((LANES, full), F32),
            ],
        )
        back_parts.append((own, rest, high))
        steps.keep(f"attb{i}", dqkv)
        for store, value in zip((dqkvs, sums_q, sums1), (dqkv, qsum, sums)):
            store.append(value)
    nears, far = scatter_items(steps, "dh1", [(rest, high) for _, rest, high in back_parts])
    back_in = [own for own, _, _ in back_parts] + nears + far
    qkv_sum, out_sum = Scatter(steps, "gqkv"), Scatter(steps, "gout")
    made, qkv_rest = grad_kernels(steps, "gqkv", a1, dqkvs)
    qkv_sum.send(made)
    pieces = call(
        functools.partial(grad_out_kernel, flat_masks, tile, cols, hpiece, slots, n_seq),
        "grad_out",
        [steps.gate("gout", atts[0])]
        + atts[1:]
        + sum(dattns, [])
        + sums1
        + sums2
        + sums_q
        + sums_u,
        [shape((tile + blocks * piece, width), BF16)] * n_seq,
        [pltpu.VMEM((full, width), BF16), pltpu.VMEM((N_VEC, width), F32)],
    )
    pieces = exchange_seq(pieces)
    steps.keep("gout_seq", pieces[1:])
    made = call(
        functools.partial(grad_out_groups_kernel, flat_masks, tile),
        "grad_out_groups",
        [steps.gate("gout_groups", pieces[0])] + pieces[1:],
        [
            shape((2, VEC_ROWS + piece, width), BF16 if j else F32)
            for j in range(inner)
            for _ in range(2)
        ],
    )
    made = [[made[2 * j], made[2 * j + 1]] for j in range(inner)]
    out_sum.send(made)
    g_qkv = qkv_sum.finish(qkv_rest())
    g_out = out_sum.finish(made)
    g_wdown = total_of(g_down)
    block_out = call(
        functools.partial(block_out_kernel, slots, n_seq),
        "block_out",
        [steps.gate("block_out", block_out_in[0])] + block_out_in[1:] + x2s + [limits, vectors],
        [shape((slots, rows, width), F32)],
        specs=[VMEM] * (len(block_out_in) + slots) + [SMEM, VMEM],
    )[0]
    grad_tokens = call(
        functools.partial(norm_one_back_kernel, slots),
        "norm_one_back",
        [steps.gate("norm_one_back", back_in[0])] + back_in[1:] + dxs + [tokens, vectors],
        [shape((slots, rows, width), F32)],
    )[0]
    g_wout, *vecs = call(
        out_final_kernel,
        "out_final",
        [total_of(g_out)],
        [shape((piece, width), F32)]
        + [shape((1, piece), F32)] * N_VEC
        + [shape((1, hpiece), F32)],
    )

    if regular:
        steps.keep("block_out", block_out)
        steps.keep("norm_one_back", grad_tokens)
        g_qkv = [steps.gate("owners", g_qkv[0])] + list(g_qkv[1:])
        parts = exchange_seq(
            call(
                owners_kernel,
                "owners",
                list(g_qkv) + list(g_up),
                [shape((piece, 3 * cols + hidden), BF16)] * n_seq,
            )
        )
        g_wqkv, g_wup = call(
            functools.partial(unplace_kernel, cols, hpiece),
            "unplace",
            parts,
            [shape((piece, 3 * width), F32), shape((piece, hidden_all), F32)],
        )
    else:
        placed = []
        for parts in (g_qkv, g_up):
            parts = total_of(parts).astype(BF16).reshape(n_seq, piece, -1)
            parts = exchange_seq(
                [lax.dynamic_index_in_dim(parts, s ^ r, 0, False) for r in range(n_seq)]
            )
            out = jnp.zeros((n_seq,) + parts[0].shape, BF16)
            for r, part in enumerate(parts):
                out = lax.dynamic_update_index_in_dim(out, part, s ^ r, 0)
            placed.append(out.astype(F32))
        g_wqkv = placed[0].reshape(n_seq, piece, 3, cols).transpose(1, 2, 0, 3).reshape(piece, -1)
        g_wup = (
            placed[1].reshape(n_seq, piece, n_dp, hpiece).transpose(1, 2, 0, 3).reshape(piece, -1)
        )
    vecs = [v.reshape(-1) for v in vecs]
    return (
        block_out,
        grad_tokens,
        g_wqkv,
        vecs[0],
        vecs[1],
        g_wout,
        vecs[2],
        g_wup,
        vecs[8],
        g_wdown,
        vecs[3],
        vecs[4],
        vecs[5],
        vecs[6],
        vecs[7],
    )


def solution(mesh):
    both = ("dp", "seq")
    act = P("dp", "seq", None)
    mat = P(both, None)
    vec = P(both)
    return jax.shard_map(
        body,
        mesh=mesh,
        in_specs=(act, act, P("dp"), P("dp"), mat, vec, vec, mat, vec, mat, vec, mat)
        + (vec,) * 5,
        out_specs=(act, act, mat, vec, vec, mat, vec, mat, vec, mat) + (vec,) * 5,
        check_vma=False,
    )
```

```python
import functools

import jax
import jax.numpy as jnp
from jax import lax
from jax.experimental import pallas as pl
from jax.experimental.pallas import tpu as pltpu
from jax.sharding import PartitionSpec as P

HEAD_DIM = 64
LANES = 128
EPSILON = 1e-06
F32 = jnp.float32
BF16 = jnp.bfloat16
OUTER = 4
ORDER = (0, 2, 1, 3)
VMEM = pl.BlockSpec(memory_space=pltpu.VMEM)
ANY = pl.BlockSpec(memory_space=pl.ANY)
HBM = pl.BlockSpec(memory_space=pltpu.HBM)
SMEM = pl.BlockSpec(memory_space=pltpu.SMEM)
LIMIT = 14 * 1024 * 1024
WHOLE = 60 * 1024 * 1024
SOFTMAX_RATE = HEAD_DIM**-0.5 * 1.4426950408889634
WAITS = {
    "qkv_z1": ["out_z2"],
    "qkv_xb": ["out_xa"],
    "up_z2": ["out_xb"],
    "up_z1": ["place"],
    "up_xa": ["qkv_z1"],
    "down_z1": ["qkv_z2", "qkv_xa"],
    "down_xb": ["down_xa"],
    "tok_core": ["tok_y", "out_z1"],
    "cot_y": ["out_seq"],
    "att0": ["qkv_xb"],
    "x2_0_core": ["out_seq"],
    "x2_0_y": ["up_xa"],
    "norm0": ["up_z2", "up_z1"],
    "a2_0_y": ["out_seq"],
    "a2_0_core": ["x2_0_y", "norm0", "mask"],
    "x2_1_core": ["tok_core"],
    "x2_1_y": ["tok_core", "cot_core", "att0"],
    "up0": ["norm_one"],
    "up1": ["a2_1_y", "a2_0_y"],
    "gdown_near": ["up1"],
    "gdown_kept": ["norm1", "x2_1_core", "up0"],
    "down0": ["a2_0_core", "gdown_sent"],
    "dh2_0_core": ["down_z1", "mask"],
    "dh2_0_y": ["x2_1_y"],
    "down1": ["cot_y"],
    "gup_sent": ["a2_1_core"],
    "gup_near": ["x2_1_y", "dh2_0_core"],
    "back0": ["up1"],
    "gdown_z1": ["dh2_0_send", "gdown_kept"],
    "gdown_z2": ["back0"],
    "gup_kept": ["dx_0_core", "gup_sent"],
    "out_core1": ["down0"],
    "out_y": ["dh2_1_send", "dh2_1_core", "out_core1"],
    "back1": ["out_core0"],
    "gup_z1": ["dx_1_core", "out_send", "gup_far"],
    "gup_z2": ["dh2_0_y", "dx_1_y"],
    "attb1": ["attb0"],
    "dh1_core0": ["gdown_z1", "attb1"],
    "dh1_core1": ["dh2_1_send"],
    "dh1_y": ["dx_0_core"],
    "gqkv_near": ["gqkv_sent"],
    "gout": ["dh1_core0"],
    "gout_near": ["gout_far"],
    "gqkv_kept": ["gup_z2"],
    "gqkv_z1": ["gup_z2", "gup_z1"],
    "gqkv_z2": ["gqkv_kept"],
    "gout_z1": ["dh1_y"],
    "owners": ["up_xb", "gqkv_z1", "block_out", "gqkv_near", "gout_z1", "gout_near"],
}
N_VEC = 8
VEC_ROWS = 8


def dot(left, right):
    return jnp.dot(left, right, preferred_element_type=F32)


def dot_nt(left, right):
    return lax.dot_general(left, right, (((1,), (1,)), ((), ())), preferred_element_type=F32)


def dot_tn(left, right):
    return lax.dot_general(left, right, (((0,), (0,)), ((), ())), preferred_element_type=F32)


def swap(values, axis, mask):
    size = lax.axis_size(axis)
    return lax.ppermute(values, axis, [(i, i ^ mask) for i in range(size)])


def shape(dims, kind):
    return jax.ShapeDtypeStruct(tuple(dims), kind)


def call(kernel, name, ins, outs, scratch=(), specs=None, limit=LIMIT):
    return pl.pallas_call(
        kernel,
        name=name,
        out_shape=tuple(outs),
        in_specs=specs or [VMEM] * len(ins),
        out_specs=tuple([VMEM] * len(outs)),
        scratch_shapes=list(scratch),
        compiler_params=pltpu.CompilerParams(vmem_limit_bytes=limit),
        cost_estimate=pl.CostEstimate(
            flops=0, bytes_accessed=0, transcendentals=0
        ),
    )(*ins)


def aligned(index, size):
    return pl.multiple_of(index * size, size)


def place_blocks(refs, masks, out):
    own = lax.axis_index("dp")
    for ref, group in zip(refs, masks):
        rows = ref.shape[1]
        for i, mask in enumerate(group):
            out[pl.ds(aligned(own ^ mask, rows), rows), :] = ref[i]


def start_copies(jobs, scratch, sems):
    copies = []
    for src, block, rows in jobs:
        copy = pltpu.make_async_copy(
            src, scratch.at[pl.ds(aligned(block, rows), rows)], sems.at[len(copies)]
        )
        copy.start()
        copies.append(copy)
    return copies


def out_jobs(refs, tile, blocks):
    own = lax.axis_index("seq")
    size = len(refs)
    rows = (refs[0].shape[0] - tile) // blocks
    return [
        (ref.at[pl.ds(tile + b * rows, rows)], b * size + (own ^ r), rows)
        for r, ref in enumerate(refs)
        for b in range(blocks)
    ]


def pack_kernel(cols, hpiece, wqkv, wup, *outs):
    own = lax.axis_index("seq")
    size = len(outs)
    hidden = wup.shape[1] // size
    width = wqkv.shape[1] // 3
    for r, out in enumerate(outs):
        dest = own ^ r
        for i in range(3):
            at = pl.multiple_of(dest * cols + i * width, LANES)
            out[:, i * cols : (i + 1) * cols] = wqkv[:, pl.ds(at, cols)]
        for i in range(hidden // hpiece):
            at = pl.multiple_of((i * size + dest) * hpiece, LANES)
            start = 3 * cols + i * hpiece
            out[:, start : start + hpiece] = wup[:, pl.ds(at, hpiece)]


def place_kernel(*refs):
    size = len(refs) - 2
    qkv, up = refs[size:]
    own = lax.axis_index("seq")
    cut = qkv.shape[2]
    for r in range(size):
        rows = refs[r].shape[0]
        at = pl.ds(aligned(own ^ r, rows), rows)
        qkv[0, at, :] = refs[r][:, :cut]
        up[0, at, :] = refs[r][:, cut:]


def owners_kernel(*refs):
    left, right, outs = refs[:3], refs[3:6], refs[6:]
    own = lax.axis_index("seq")
    rows = outs[0].shape[0]
    cut = left[0].shape[2]
    for r, out in enumerate(outs):
        at = pl.ds(aligned(own ^ r, rows), rows)
        for parts, cols in ((left, slice(0, cut)), (right, slice(cut, out.shape[1]))):
            total = parts[0][0, at, :].astype(F32) + parts[1][0, at, :].astype(F32)
            out[:, cols] = (total + parts[2][0, at, :].astype(F32)).astype(BF16)


def unplace_kernel(cols, hpiece, *refs):
    *parts, qkv, up = refs
    size = len(parts)
    own = lax.axis_index("seq")
    width = qkv.shape[1] // 3
    for r, part in enumerate(parts):
        src = own ^ r
        for i in range(3):
            at = pl.multiple_of(src * cols + i * width, LANES)
            qkv[:, pl.ds(at, cols)] = part[:, i * cols : (i + 1) * cols].astype(F32)
        for i in range((part.shape[1] - 3 * cols) // hpiece):
            at = pl.multiple_of((i * size + src) * hpiece, LANES)
            start = 3 * cols + i * hpiece
            up[:, pl.ds(at, hpiece)] = part[:, start : start + hpiece].astype(F32)


def out_pack_kernel(tile, wout, *refs):
    n = N_VEC + 1
    vecs, out, landed, scratch, sems = refs[:n], refs[n], refs[n + 1 : -2], refs[-2], refs[-1]
    copies = [pltpu.make_async_copy(v, l, sems.at[i]) for i, (v, l) in enumerate(zip(vecs, landed))]
    for copy in copies:
        copy.start()
    out[0, tile:, :] = wout[...]
    scratch[...] = jnp.zeros_like(scratch)
    for copy in copies:
        copy.wait()
    for i, vec in enumerate(landed):
        row, lane = (0, i * LANES) if i < N_VEC else (1, 0)
        scratch[row : row + 1, lane : lane + vec.shape[0]] = vec[...].astype(F32)[None, :]
    out[0, :tile, :] = scratch[...].astype(BF16)


def out_pieces_kernel(masks, tile, blocks, *refs):
    n = len(masks)
    outs, mixed = refs[n:-1], refs[-1]
    d = lax.axis_index("dp")
    s = lax.axis_index("seq")
    flat = [(i, j) for i, group in enumerate(masks) for j in range(len(group))]
    mask_of = [mask for group in masks for mask in group]
    total = None
    for n, (i, j) in enumerate(flat):
        part = refs[i][j, :tile, :].astype(F32)
        part = pltpu.roll(part, 2 * n, 0) if n else part
        total = part if total is None else total + part
    mixed[...] = total.astype(BF16)
    piece = refs[0].shape[1] - tile
    for r, out in enumerate(outs):
        out[:tile, :] = mixed[...]
        for b in range(blocks):
            want = d ^ ((s ^ r) * blocks + b)
            for (i, j), mask in zip(flat, mask_of):

                @pl.when(want == mask)
                def _(out=out, b=b, i=i, j=j):
                    start = tile + b * piece
                    out[start : start + piece, :] = refs[i][j, tile:, :]


def vector_unpack_kernel(masks, tile, n_seq, cols, hpiece, *refs):
    parts, (vectors, qkv_bias, ubias) = refs[:n_seq], refs[n_seq:]
    width = vectors.shape[1]
    hidden = ubias.shape[1]
    mask_of = [mask for group in masks for mask in group]
    piece = width // (n_seq * len(mask_of))
    s = lax.axis_index("seq")
    d = lax.axis_index("dp")
    row = lax.broadcasted_iota(jnp.int32, (tile, 1), 0)
    dist = jnp.zeros_like(row)
    for n, mask in enumerate(mask_of):
        dist = jnp.where(row // 2 == n, mask, dist)
    source = d ^ dist
    lane = lax.broadcasted_iota(jnp.int32, (LANES, width), 1)
    sub = lax.broadcasted_iota(jnp.int32, (LANES, width), 0)
    spread = jnp.where(lane % piece == sub, 1.0, 0.0).astype(BF16)
    target = lax.broadcasted_iota(jnp.int32, (1, width), 1) // piece
    even = row % 2 == 0
    for i in range(N_VEC):
        total = None
        for r, part in enumerate(parts):
            tiled = dot(part[:tile, i * LANES : (i + 1) * LANES], spread)
            here = even & (source * n_seq + (s ^ r) == target)
            tiled = jnp.sum(jnp.where(here, tiled, 0.0), axis=0, keepdims=True)
            total = tiled if total is None else total + tiled
        vectors[i : i + 1, :] = total
    lane = lax.broadcasted_iota(jnp.int32, (LANES, hidden), 1)
    sub = lax.broadcasted_iota(jnp.int32, (LANES, hidden), 0)
    spread = jnp.where(lane % hpiece == sub, 1.0, 0.0).astype(BF16)
    target = lax.broadcasted_iota(jnp.int32, (1, hidden), 1) // hpiece
    tiled = dot(parts[0][:tile, :LANES], spread)
    here = (row % 2 == 1) & (source == target)
    ubias[...] = jnp.sum(jnp.where(here, tiled, 0.0), axis=0, keepdims=True)
    at = pl.ds(pl.multiple_of(s * cols, LANES), cols)
    qkv_bias[...] = jnp.zeros_like(qkv_bias)
    qkv_bias[:, :cols] = vectors[0:1, at]
    qkv_bias[:, 2 * cols :] = vectors[1:2, at]


def positions(block, rows, n_seq, axis):
    half = n_seq // 2
    owner = lax.axis_index("seq") ^ (2 * (block % half) + block // half)
    dims = (rows, 1) if axis == 0 else (1, rows)
    return owner * rows + lax.broadcasted_iota(jnp.int32, dims, axis)


def attention_kernel(masks, tile, blocks, cols, n_seq, item, *refs):
    first = item == 0
    a1, bias, lens = refs[:3]
    n = len(masks) if first else 1
    pieces, outs = refs[3 : 3 + n], refs[3 + n : 3 + n + (n_seq if first else 1)]
    refs = refs[3 + n + len(outs) :]
    if first:
        qkv, att, probs, own, rest, high, wqkv, wout, ok, sems = refs
    else:
        qkv, att, probs, own, rest, high, ok = refs
        (wqkv,), (wout,) = pieces, outs
    rows = a1.shape[0]
    cut = rows // 2
    blk = own.shape[0]
    out_copies = []
    if first:
        out_copies = start_copies(out_jobs(outs, tile, blocks), wout, sems)
        place_blocks(pieces, masks, wqkv)
    for q in range(n_seq):
        good = positions(q, blk, n_seq, 1) < lens[item]
        ok[:, q * blk : (q + 1) * blk] = jnp.where(good, 0.0, -1e30)
    for i in range(3):
        part = slice(i * cols, (i + 1) * cols)
        qkv[:, part] = (dot(a1[...], wqkv[:, part]) + bias[:, part]).astype(BF16)
    step_rows = min(256, rows)
    lane = lax.broadcasted_iota(jnp.int32, (1, LANES), 1)
    sides = [(lane < HEAD_DIM), (lane >= HEAD_DIM)]
    for pair in range(cols // LANES):
        at = slice(pair * LANES, (pair + 1) * LANES)
        keys = qkv[:, cols + pair * LANES : cols + (pair + 1) * LANES]
        vals = qkv[:, 2 * cols + pair * LANES : 2 * cols + (pair + 1) * LANES]
        split = [jnp.where(side, vals, jnp.zeros_like(vals)) for side in sides]

        def step(block, carry, pair=pair, at=at, keys=keys, split=split):
            place = pl.ds(aligned(block, step_rows), step_rows)
            query = qkv[place, at]
            total = None
            for h in range(2):
                q = jnp.where(sides[h], query, jnp.zeros_like(query))
                scores = dot_nt(q, keys) + ok[...]
                peak = jnp.max(scores, axis=-1, keepdims=True)
                expo = jnp.exp2((scores - peak) * SOFTMAX_RATE)
                rate = 1.0 / jnp.sum(expo, axis=-1, keepdims=True)
                low = (expo * rate).astype(BF16)
                probs[2 * pair + h, place, :] = low
                out = dot(low, split[h])
                total = out if total is None else total + out
            att[place, at] = total.astype(BF16)
            return carry

        lax.fori_loop(0, rows // step_rows, step, 0)
    for copy in out_copies:
        copy.wait()
    high[...] = dot(att[cut:, :], wout[...]).astype(BF16)
    own[...] = dot(att[:blk, :], wout[...])
    rest[...] = dot(att[blk:cut, :], wout[...])


def attention_back_kernel(cols, n_seq, *refs):
    parts = refs[:n_seq]
    qkv, probs, hat, wqkv, wout = refs[n_seq : n_seq + 5]
    dqkv, own, rest, high, sums, sums_one, grad, datt, dkt, dvt = refs[n_seq + 5 :]
    rows = dqkv.shape[0]
    cut = rows // 2
    blk = own.shape[0]
    for i, part in enumerate(parts):
        grad[i * blk : (i + 1) * blk, :] = part[...]
    datt[...] = dot_nt(grad[...], wout[...]).astype(BF16)
    step_rows = min(256, rows)
    lane = lax.broadcasted_iota(jnp.int32, (1, LANES), 1)
    sides = [(lane < HEAD_DIM), (lane >= HEAD_DIM)]
    scale = HEAD_DIM**-0.5
    for pair in range(cols // LANES):
        at = slice(pair * LANES, (pair + 1) * LANES)
        at_k = slice(cols + pair * LANES, cols + (pair + 1) * LANES)
        at_v = slice(2 * cols + pair * LANES, 2 * cols + (pair + 1) * LANES)
        keys = qkv[:, at_k]
        vals = qkv[:, at_v]
        split = [jnp.where(side, keys, jnp.zeros_like(keys)) for side in sides]
        dkt[...] = jnp.zeros_like(dkt)
        dvt[...] = jnp.zeros_like(dvt)

        def step(block, carry, pair=pair, at=at, vals=vals, split=split):
            place = pl.ds(aligned(block, step_rows), step_rows)
            gatt = datt[place, at]
            query = qkv[place, at]
            gatt_t = gatt.T
            query_t = query.T
            total = None
            for h in range(2):
                g = jnp.where(sides[h], gatt, jnp.zeros_like(gatt))
                gp = dot_nt(g, vals)
                low = probs[2 * pair + h, place, :]
                p = low.astype(F32)
                mean = jnp.sum(gp * p, axis=-1, keepdims=True)
                gs = (p * (gp - mean)).astype(BF16)
                half = slice(h * HEAD_DIM, (h + 1) * HEAD_DIM)
                dvt[half, :] += dot(gatt_t[half, :], low)
                dkt[half, :] += dot(query_t[half, :], gs)
                out = dot(gs, split[h])
                total = out if total is None else total + out
            dqkv[place, at] = (total * scale).astype(BF16)
            return carry

        lax.fori_loop(0, rows // step_rows, step, 0)
        dqkv[:, at_k] = (dkt[...].T * scale).astype(BF16)
        dqkv[:, at_v] = dvt[...].T.astype(BF16)
    sums[...] = jnp.sum(dqkv[...].astype(F32), axis=0, keepdims=True)
    sums_one[...] = jnp.zeros_like(sums_one)

    def last(block, carry):
        at = pl.ds(aligned(block, 256), 256)
        value = dot_nt(dqkv[...], wqkv[at, :])
        own[:, at] = value[:blk]
        rest[:, at] = value[blk:cut]
        high[:, at] = value[cut:].astype(BF16)
        sums_one[0:1, at] = jnp.sum(value * hat[:, at].astype(F32), axis=0, keepdims=True)
        sums_one[1:2, at] = jnp.sum(value, axis=0, keepdims=True)
        return carry

    lax.fori_loop(0, wqkv.shape[0] // 256, last, 0, unroll=4)


def up_kernel(masks, n_seq, item, *refs):
    first = item == 0
    n = len(masks) if first else 1
    parts, bias = refs[:n_seq], refs[n_seq]
    pieces = refs[n_seq + 1 : n_seq + 1 + n]
    if first:
        a2, act, slope, wup = refs[n_seq + 1 + n :]
        place_blocks(pieces, masks, wup)
    else:
        a2, act, slope = refs[n_seq + 1 + n :]
        (wup,) = pieces
    blk = parts[0].shape[0]
    rows = a2.shape[0]
    width = min(256, act.shape[1])
    for i, part in enumerate(parts):
        a2[i * blk : (i + 1) * blk, :] = part[...]
    half = min(256, rows)
    for i in range(rows // half):
        place = slice(i * half, (i + 1) * half)

        def step(block, carry, place=place):
            at = pl.ds(aligned(block, width), width)
            u = dot(a2[place, :], wup[:, at]) + bias[:, at]
            cdf = 0.5 * (1.0 + lax.erf(u * 0.7071067811865476))
            bell = jnp.exp2(u * u * -0.7213475204444817) * 0.3989422804014327
            act[place, at] = (u * cdf).astype(BF16)
            slope[place, at] = cdf + u * bell
            return carry

        lax.fori_loop(0, act.shape[1] // width, step, 0)


def down_kernel(masks, item, *refs):
    n = len(masks) if item == 0 else 1
    dy, act, slope, wup = refs[:4]
    downs = refs[4 : 4 + n]
    if item == 0:
        du, own, rest, high, oown, orest, ohigh, sums, wdown = refs[4 + n :]
        place_blocks(downs, masks, wdown)
    else:
        du, own, rest, high, oown, orest, ohigh, sums = refs[4 + n :]
        (wdown,) = downs
    rows = dy.shape[0]
    cut = rows // 2
    blk = own.shape[0]
    hidden = act.shape[1]
    width = min(256, hidden)

    def first(block, carry):
        at = pl.ds(aligned(block, width), width)
        value = (slope[:, at] * dot_nt(dy[...], wdown[at, :])).astype(BF16)
        du[:, at] = value
        sums[:, at] = jnp.sum(value.astype(F32), axis=0, keepdims=True)
        return carry

    lax.fori_loop(0, hidden // width, first, 0)

    def second(block, carry):
        at = pl.ds(aligned(block, 256), 256)
        value = dot_nt(du[...], wup[at, :])
        own[:, at] = value[:blk]
        rest[:, at] = value[blk:cut]
        high[:, at] = value[cut:].astype(BF16)
        value = dot(act[...], wdown[:, at])
        oown[:, at] = value[:blk]
        orest[:, at] = value[blk:cut]
        ohigh[:, at] = value[cut:].astype(BF16)
        return carry

    lax.fori_loop(0, wup.shape[0] // 256, second, 0)


def grad_kernel(j, inner, slots, *refs):
    lefts, rights = refs[:slots], refs[slots : 2 * slots]
    *outs, turned = refs[2 * slots :]
    rows = lefts[0].shape[0]
    each, blk = outs[0].shape[:2]
    own = lax.axis_index("dp")
    for n, k in enumerate(ORDER):
        at = pl.ds(aligned(own ^ (k * inner + j), blk), blk)
        for i, left in enumerate(lefts):
            turned[n * blk : (n + 1) * blk, i * rows : (i + 1) * rows] = left[:, at].T
    width = min(256, outs[0].shape[2])

    def step(block, carry):
        at = pl.ds(aligned(block, width), width)
        total = None
        for i, right in enumerate(rights):
            out = dot(turned[:, i * rows : (i + 1) * rows], right[:, at])
            total = out if total is None else total + out
        for n in range(len(ORDER)):
            out = outs[n // each]
            out[n % each, :, at] = total[n * blk : (n + 1) * blk].astype(out.dtype)
        return carry

    lax.fori_loop(0, outs[0].shape[2] // width, step, 0, unroll=True)


def grad_out_kernel(masks, tile, cols, hpiece, slots, n_seq, *refs):
    take = lambda n: (refs[:n], refs[n:])
    lefts, refs = take(slots)
    rights, refs = take(slots * n_seq)
    sums1, refs = take(slots)
    sums2, refs = take(slots)
    sums_q, refs = take(slots)
    sums_u, refs = take(slots)
    outs, (scratch, wide) = take(n_seq)[0], refs[n_seq:]
    width = wide.shape[1]
    s = lax.axis_index("seq")
    d = lax.axis_index("dp")
    total = lambda refs: functools.reduce(lambda a, b: a + b, [ref[...] for ref in refs])
    q, u = total(sums_q), total(sums_u)
    one, two = total(sums1), total(sums2)
    wide[...] = jnp.zeros_like(wide)
    at = pl.ds(pl.multiple_of(s * cols, LANES), cols)
    wide[0:1, at] = q[:, :cols]
    wide[1:2, at] = q[:, 2 * cols :]
    wide[2:4, :] = two[:2]
    wide[4:6, :] = one[:2]
    wide[6:8, :] = two[2:4]
    piece = width // (n_seq * len(masks))
    row = lax.broadcasted_iota(jnp.int32, (n_seq * tile, 1), 0)
    near = row % tile
    dist = jnp.zeros_like(row)
    for n, mask in enumerate(masks):
        dist = jnp.where(near // 2 == n, mask, dist)
    dest = (d ^ dist) * n_seq + (s ^ (row // tile))
    dest = jnp.where(near % 2 == 0, dest, -1)
    spread = jnp.where(
        lax.broadcasted_iota(jnp.int32, (width, LANES), 0) % piece
        == lax.broadcasted_iota(jnp.int32, (width, LANES), 1),
        1.0,
        0.0,
    ).astype(BF16)
    here = lax.broadcasted_iota(jnp.int32, (1, width), 1) // piece == dest
    vecs = []
    for i in range(N_VEC):
        vecs.append(dot(jnp.where(here, wide[i : i + 1, :], 0.0).astype(BF16), spread))
    hidden = u.shape[1]
    spread = jnp.where(
        lax.broadcasted_iota(jnp.int32, (hidden, LANES), 0) % hpiece
        == lax.broadcasted_iota(jnp.int32, (hidden, LANES), 1),
        1.0,
        0.0,
    ).astype(BF16)
    dest = jnp.where(near % 2 == 1, d ^ dist, -1)[:tile]
    here = lax.broadcasted_iota(jnp.int32, (1, hidden), 1) // hpiece == dest
    long = dot(jnp.where(here, u, 0.0).astype(BF16), spread)
    for r, out in enumerate(outs):
        for i, vec in enumerate(vecs):
            value = vec[r * tile : (r + 1) * tile]
            if r == 0 and i == 0:
                value = value + long
            out[:tile, i * LANES : (i + 1) * LANES] = value.astype(BF16)
    rows = rights[0].shape[0]
    blocks = (outs[0].shape[0] - tile) // piece
    grad = None
    for i, left in enumerate(lefts):
        for q in range(n_seq):
            scratch[q * rows : (q + 1) * rows, :] = rights[i * n_seq + q][...]
        part = dot_tn(left[...], scratch[...])
        grad = part if grad is None else grad + part
    grad = grad.astype(BF16)
    for other in range(n_seq):
        for r in range(n_seq):

            @pl.when(s ^ r == other)
            def _(other=other, r=r):
                for b in range(blocks):
                    at = (b * n_seq + other) * piece
                    start = tile + b * piece
                    outs[r][start : start + piece, :] = grad[at : at + piece]


def grad_out_groups_kernel(masks, tile, *refs):
    n_out = len(masks) // 2
    pieces, outs = refs[:-n_out], refs[-n_out:]
    size = len(pieces)
    head = VEC_ROWS
    rows = outs[0].shape[1] - head
    blocks = (pieces[0].shape[0] - tile) // rows
    d = lax.axis_index("dp")
    s = lax.axis_index("seq")
    total = None
    for piece in pieces:
        part = piece[:tile, :].astype(F32)
        total = part if total is None else total + part
    row = lax.broadcasted_iota(jnp.int32, (tile, 1), 0)
    for n, mask in enumerate(masks):
        out, i = outs[n // 2], n % 2
        value = pltpu.roll(total, tile - 2 * n, 0) if n else total
        out[i, :head, :] = jnp.where(row < 2, value, 0.0)[:head].astype(out.dtype)
        for r in range(size):
            for b in range(blocks):

                @pl.when(d ^ mask == (s ^ r) * blocks + b)
                def _(out=out, i=i, r=r, b=b):
                    start = tile + b * rows
                    out[i, head:, :] = pieces[r][start : start + rows, :].astype(out.dtype)


def out_final_kernel(total, grad, *vecs):
    grad[...] = total[VEC_ROWS:, :]
    for i, vec in enumerate(vecs[:-1]):
        vec[...] = total[0:1, i * LANES : i * LANES + vec.shape[1]]
    vecs[-1][...] = total[1:2, : vecs[-1].shape[1]]


def items_kernel(*refs):
    slots, blk = refs[-1].shape[:2]
    rests, nears, outs = refs[:slots], refs[slots : 2 * slots], refs[2 * slots :]
    for i in range(slots):
        for j, out in enumerate(outs):
            near = nears[i][(j + 1) * blk : (j + 2) * blk, :].astype(F32)
            out[i] = (rests[i][j * blk : (j + 1) * blk, :] + near).astype(BF16)


def item_sum(item, own, near, far, blk):
    total = own[...] + near[:blk, :].astype(F32)
    for ref in far:
        total = total + ref[item].astype(F32)
    return total


def gathered_sum(own, near, far, blk):
    total = own[...] + near[:blk, :].astype(F32)
    for ref in far:
        total = total + ref[...].astype(F32)
    return total


def stats(values):
    center = values - jnp.mean(values, axis=-1, keepdims=True)
    rate = lax.rsqrt(jnp.mean(center * center, axis=-1, keepdims=True) + EPSILON)
    return center * rate, rate


def norm_kernel(n_seq, *refs):
    parts, vectors, outs = refs[:n_seq], refs[n_seq], refs[n_seq + 1 :]
    rows = parts[0].shape[1]
    outs, hats = outs[: len(outs) // 2], outs[len(outs) // 2 :]
    for i, (out, kept) in enumerate(zip(outs, hats)):
        for q, part in enumerate(parts):
            hat, _ = stats(part[i].astype(F32))
            kept[q * rows : (q + 1) * rows, :] = hat.astype(BF16)
            out[q * rows : (q + 1) * rows, :] = (
                hat * vectors[4:5, :] + vectors[5:6, :]
            ).astype(BF16)


def mask_kernel(n_seq, *refs):
    parts, limits, outs = refs[:n_seq], refs[n_seq], refs[n_seq + 1 :]
    rows = parts[0].shape[1]
    for i, out in enumerate(outs):
        for q, part in enumerate(parts):
            good = jnp.where(positions(q, rows, n_seq, 0) < limits[i], 1.0, 0.0)
            out[q * rows : (q + 1) * rows, :] = (part[i].astype(F32) * good).astype(BF16)


def norm_two_kernel(item, own, near, *refs):
    *far, x, vectors, x2, a2 = refs
    value = x[item].astype(F32) + (
        gathered_sum(own, near, far, x2.shape[0]) + vectors[2:3, :]
    )
    x2[...] = value
    hat, _ = stats(value)
    a2[...] = (hat * vectors[6:7, :] + vectors[7:8, :]).astype(BF16)


def norm_back(grad, gain, hat, rate):
    scaled = grad * gain
    return rate * (
        scaled
        - jnp.mean(scaled, axis=-1, keepdims=True)
        - hat * jnp.mean(scaled * hat, axis=-1, keepdims=True)
    )


def norm_two_back_kernel(own, near, *refs):
    *far, x2, dy, vectors, dx2, low, sums = refs
    grad = gathered_sum(own, near, far, x2.shape[0])
    hat, rate = stats(x2[...])
    rows = dy[: x2.shape[0], :].astype(F32)
    value = rows + norm_back(grad, vectors[6:7, :], hat, rate)
    dx2[...] = value
    rounded = value.astype(BF16)
    low[...] = rounded
    sums[0:1, :] = jnp.sum(rounded.astype(F32), axis=0, keepdims=True)
    sums[1:2, :] = jnp.sum(rows, axis=0, keepdims=True)
    sums[2:3, :] = jnp.sum(grad * hat, axis=0, keepdims=True)
    sums[3:4, :] = jnp.sum(grad, axis=0, keepdims=True)
    sums[4:8, :] = jnp.zeros_like(sums[4:8, :])


def norm_one_back_kernel(slots, *refs):
    owns, nears, refs = refs[:slots], refs[slots : 2 * slots], refs[2 * slots :]
    *far, x, vectors, out = refs
    far, dxs = far[:-slots], far[-slots:]
    for i in range(slots):
        grad = item_sum(i, owns[i], nears[i], far, x.shape[1])
        hat, rate = stats(x[i].astype(F32))
        out[i] = dxs[i][...] + norm_back(grad, vectors[4:5, :], hat, rate)


def block_out_kernel(slots, n_seq, *refs):
    owns, nears, refs = refs[:slots], refs[slots : 2 * slots], refs[2 * slots :]
    *far, limits, vectors, out = refs
    far, x2s = far[:-slots], far[-slots:]
    for i, x2 in enumerate(x2s):
        blk = x2.shape[0]
        value = x2[...] + item_sum(i, owns[i], nears[i], far, blk) + vectors[3:4, :]
        good = jnp.where(positions(0, blk, n_seq, 0) < limits[i], 1.0, 0.0)
        out[i] = value * good


def exchange_seq(pieces):
    return [swap(piece, "seq", r) if r else piece for r, piece in enumerate(pieces)]


def gather_masks():
    inner = lax.axis_size("dp") // OUTER
    return [
        tuple(k * inner ^ j for k in pair) for pair in (ORDER[:2], ORDER[2:]) for j in range(inner)
    ]


def total_of(parts):
    return functools.reduce(lambda a, b: a + b, [part[0].astype(F32) for part in parts])


class Steps:
    def __init__(self):
        self.known = {}

    def keep(self, name, value):
        self.known[name] = value
        return value

    def send(self, name, value, axis, mask):
        return self.keep(name, swap(value, axis, mask))

    def gate(self, name, value):
        others = [self.known[key] for key in WAITS.get(name, ()) if key in self.known]
        return lax.optimization_barrier((value, others))[0] if others else value


def inner_masks():
    inner = lax.axis_size("dp") // OUTER
    out, bit = [], 1
    while bit < inner:
        out.append(bit)
        bit *= 2
    return out


def gather_dp(steps, name, block):
    inner = lax.axis_size("dp") // OUTER
    far = steps.send(name + "_z2", steps.gate(name + "_z2", block), "dp", 2 * inner)
    pair = jnp.concatenate([block, far], 0)
    other = steps.send(name + "_z1", steps.gate(name + "_z1", pair), "dp", inner)
    out = []
    for part, key in ((pair, name + "_xa"), (other, name + "_xb")):
        group = [part]
        for bit in inner_masks():
            group += [swap(steps.gate(key, p), "dp", bit) for p in group]
        steps.keep(key, group[1:])
        out += group
    return out


def scatter_first(steps, name, made, part):
    pairs = [group[part] for group in made[1:2] if len(made) == 2]
    steps.keep(name, [swap(steps.gate(name, pair), "dp", 1) for pair in pairs])
    return steps.known[name]


def inner_sum(parts, early):
    parts = [parts[0].astype(F32)] + list(parts[1:])
    for bit in inner_masks():
        for j in range(0, len(parts), 2 * bit):
            if len(parts) == 2:
                got = early[0]
            else:
                got = swap(parts[j + bit].astype(BF16), "dp", bit)
            parts[j] = parts[j].astype(F32) + got.astype(F32)
    return parts[0]


class Scatter:
    def __init__(self, steps, name):
        self.steps, self.name = steps, name

    def send(self, made):
        self.far = scatter_first(self.steps, self.name + "_far", made, 1)
        self.near = scatter_first(self.steps, self.name + "_near", made, 0)

    def finish(self, groups):
        steps, name = self.steps, self.name
        inner = len(groups)
        far = inner_sum([group[1] for group in groups], self.far).astype(BF16)
        got = steps.send(name + "_z1", steps.gate(name + "_z1", far), "dp", inner)
        near = inner_sum([group[0] for group in groups], self.near)
        send = (near[1:] + got[1:].astype(F32)).astype(BF16)
        tail = steps.send(name + "_z2", steps.gate(name + "_z2", send), "dp", 2 * inner)
        return near, got, tail


def scatter_seq(steps, name, rest, high):
    half = lax.axis_size("seq") // 2
    near = steps.send(name + "_core", steps.gate(name + "_core", high), "seq", 1)
    blk = near.shape[0] // half
    send = (rest + near[blk:].astype(F32)).astype(BF16)
    send = steps.gate(name + "_y", steps.keep(name + "_send", send))
    far = [swap(send[(j - 1) * blk : j * blk], "seq", 2 * j) for j in range(1, half)]
    return [near] + steps.keep(name + "_y", far)


def scatter_items(steps, name, parts):
    half = lax.axis_size("seq") // 2
    slots = len(parts)
    nears = [
        steps.send(f"{name}_core{i}", steps.gate(f"{name}_core{i}", high), "seq", 1)
        for i, (_, high) in enumerate(parts)
    ]
    rests = [rest for rest, _ in parts]
    blk = nears[0].shape[0] // half
    width = nears[0].shape[1]
    sends = call(
        items_kernel,
        "items",
        rests + nears,
        [shape((slots, blk, width), BF16)] * (half - 1),
    )
    sends = steps.gate(name + "_y", steps.keep(name + "_send", list(sends)))
    far = [swap(send, "seq", 2 * (j + 1)) for j, send in enumerate(sends)]
    steps.keep(name + "_y", far)
    return nears, far


def gather_seq(steps, name, block):
    half = lax.axis_size("seq") // 2
    block = steps.gate(name + "_y", block)
    far = steps.keep(name + "_y", [swap(block, "seq", 2 * j) for j in range(1, half)])
    mine = [block] + far
    other = [swap(block, "seq", 1)]
    other += [swap(steps.gate(name + "_core", part), "seq", 1) for part in far]
    steps.keep(name + "_core", other)
    return mine + other


def grad_kernels(steps, name, lefts, rights):
    lefts, rights = list(lefts), list(rights)
    inner = lax.axis_size("dp") // OUTER
    slots = len(lefts)
    blk = lefts[0].shape[1] // (OUTER * inner)
    width = rights[0].shape[1]
    rows = lefts[0].shape[0]
    if blk % LANES:
        own = lax.axis_index("dp")
        whole = sum(dot_tn(a, b) for a, b in zip(lefts, rights)).reshape(-1, blk, width)
        take = lambda k: lax.dynamic_index_in_dim(whole, own ^ k, 0)
        made = []
        for j in range(inner):
            got = [take(k * inner + j) for k in ORDER]
            made.append([jnp.concatenate(got[:2], 0), jnp.concatenate(got[2:], 0)])
        return made, lambda: made
    made = [None] * inner

    def make(j):
        key = name + ("_sent" if j else "_kept")
        made[j] = steps.keep(
            key,
            list(
                call(
                    functools.partial(grad_kernel, j, inner, slots),
                    key,
                    [steps.gate(key, lefts[0])] + lefts[1:] + rights,
                    [shape((2, blk, width), BF16 if j else F32)] * 2,
                    [pltpu.VMEM((4 * blk, slots * rows), BF16)],
                )
            ),
        )

    def rest():
        make(0)
        return made

    for j in range(1, inner):
        make(j)
    return made, rest


def body(
    tokens,
    cotangent,
    item_count,
    valid_len,
    w_qkv,
    q_bias,
    v_bias,
    w_out,
    out_bias,
    w_up,
    up_bias,
    w_down,
    down_bias,
    gain_one,
    shift_one,
    gain_two,
    shift_two,
):
    slots, rows, width = tokens.shape
    n_seq = lax.axis_size("seq")
    n_dp = lax.axis_size("dp")
    inner = n_dp // OUTER
    count = n_seq * n_dp
    half = n_seq // 2
    cut = half * rows
    full = n_seq * rows
    cols = width // n_seq
    heads = cols // HEAD_DIM
    piece = width // count
    hidden_all = w_up.shape[1]
    hidden = hidden_all // n_seq
    hpiece = hidden_all // count
    blocks = n_dp // n_seq
    regular = hpiece % LANES == 0 and piece % 16 == 0

    limits = jnp.where(jnp.arange(slots) < item_count[0], valid_len, 0)
    dma = lambda n: pltpu.SemaphoreType.DMA((n,))

    rows_in = [
        q_bias,
        v_bias,
        out_bias,
        down_bias,
        gain_one,
        shift_one,
        gain_two,
        shift_two,
        up_bias,
    ]
    tile = max(16, 2 * n_dp)
    masks = gather_masks()
    n_parts = len(masks)
    flat_masks = [k * inner + j for j in range(inner) for k in ORDER]
    steps = Steps()
    out_block = call(
        functools.partial(out_pack_kernel, tile),
        "out_pack",
        [w_out] + rows_in,
        [shape((1, tile + piece, width), BF16)],
        [pltpu.VMEM(v.shape, BF16) for v in rows_in]
        + [pltpu.VMEM((tile, width), F32), dma(N_VEC + 1)],
        [VMEM] + [HBM] * (N_VEC + 1),
        WHOLE,
    )[0]
    if regular:
        packed = call(
            functools.partial(pack_kernel, cols, hpiece),
            "pack",
            [w_qkv, w_up],
            [shape((piece, 3 * cols + hidden), BF16)] * n_seq,
        )
        own_qkv, own_up = call(
            place_kernel,
            "place",
            exchange_seq(packed),
            [
                shape((1, n_seq * piece, 3 * cols), BF16),
                shape((1, n_seq * piece, hidden), BF16),
            ],
        )
    else:
        s = lax.axis_index("seq")
        split = jnp.concatenate(
            [
                w_qkv.reshape(piece, 3, n_seq, cols).transpose(2, 0, 1, 3).reshape(n_seq, piece, -1),
                w_up.reshape(piece, n_dp, n_seq, hpiece)
                .transpose(2, 0, 1, 3)
                .reshape(n_seq, piece, -1),
            ],
            -1,
        )
        packed = [lax.dynamic_index_in_dim(split, s ^ r, 0, False) for r in range(n_seq)]
        placed = jnp.zeros_like(split)
        for r, part in enumerate(exchange_seq(packed)):
            placed = lax.dynamic_update_index_in_dim(placed, part, s ^ r, 0)
        placed = placed.reshape(1, n_seq * piece, -1)
        own_qkv, own_up = placed[:, :, : 3 * cols], placed[:, :, 3 * cols :]

    steps.keep("place", [own_qkv, own_up])
    out_all = gather_dp(steps, "out", out_block)
    wqkv = gather_dp(steps, "qkv", own_qkv)
    wup = gather_dp(steps, "up", own_up)
    wdown = gather_dp(steps, "down", w_down[None])
    wout = exchange_seq(
        call(
            functools.partial(out_pieces_kernel, masks, tile, blocks),
            "out_pieces",
            [steps.gate("out_pieces", out_all[0])] + out_all[1:],
            [shape((tile + blocks * piece, width), BF16)] * n_seq,
            [pltpu.VMEM((tile, width), BF16)],
        )
    )
    steps.keep("out_seq", wout[1:])
    tok = gather_seq(steps, "tok", tokens)
    cot = gather_seq(steps, "cot", cotangent)
    vectors, qkv_bias, ubias = call(
        functools.partial(vector_unpack_kernel, masks, tile, n_seq, cols, hpiece),
        "vector_unpack",
        [steps.gate("vectors", wout[0])] + wout[1:],
        [shape((N_VEC, width), F32), shape((1, 3 * cols), F32), shape((1, hidden), F32)],
    )
    a1 = call(
        functools.partial(norm_kernel, n_seq),
        "norm_one",
        [steps.gate("norm_one", tok[0])] + tok[1:] + [vectors],
        [shape((full, width), BF16)] * (2 * slots),
    )
    a1, hats = list(a1[:slots]), list(a1[slots:])
    steps.keep("norm_one", a1)
    dys = call(
        functools.partial(mask_kernel, n_seq),
        "mask",
        [steps.gate("mask", cot[0])] + cot[1:] + [limits],
        [shape((full, width), BF16)] * slots,
        specs=[VMEM] * n_seq + [SMEM],
    )
    steps.keep("mask", dys)

    outs3 = [shape((rows, width), F32), shape((cut - rows, width), F32), shape((cut, width), BF16)]
    qkvs, atts, probss, x2s, a2s, acts, slopes, a2_of = [], [], [], [], [], [], [], []
    for i in range(slots):
        first = i == 0
        qkv, att, probs, own, rest, high, *kept = call(
            functools.partial(attention_kernel, masks, tile, blocks, cols, n_seq, i),
            "attention",
            [steps.gate(f"att{i}", a1[i]), qkv_bias, valid_len] + wqkv + wout,
            [
                shape((full, 3 * cols), BF16),
                shape((full, cols), BF16),
                shape((heads, full, full), BF16),
            ]
            + outs3
            + ([shape((width, 3 * cols), BF16), shape((cols, width), BF16)] if first else []),
            [pltpu.VMEM((1, full), F32)] + ([dma(n_dp)] if first else []),
            [VMEM] * 2 + [SMEM] + ([VMEM] * n_parts + [ANY] * n_seq if first else [VMEM] * 2),
        )
        if first:
            wqkv, wout = [kept[0]], [kept[1]]
        steps.keep(f"att{i}", att)
        for store, value in zip((qkvs, atts, probss, a2_of), (qkv, att, probs, (own, rest, high))):
            store.append(value)
        if i == 0:
            a2_of[0] = [own] + scatter_seq(steps, "x2_0", rest, high)
        if i == 1 or slots == 1:
            norm_two_of = lambda i: call(
                functools.partial(norm_two_kernel, i),
                "norm_two",
                [steps.gate(f"norm{i}", a2_of[i][0])] + a2_of[i][1:] + [tokens, vectors],
                [shape((rows, width), F32), shape((rows, width), BF16)],
            )
            x2, a2 = norm_two_of(0)
            x2s.append(x2)
            a2_of[0] = gather_seq(steps, "a2_0", steps.keep("norm0", a2))
        if i:
            own, rest, high = a2_of[i]
            a2_of[i] = [own] + scatter_seq(steps, f"x2_{i}", rest, high)

    for i in range(slots):
        first = i == 0
        if i:
            x2, a2 = norm_two_of(i)
            x2s.append(x2)
            a2_of[i] = gather_seq(steps, f"a2_{i}", steps.keep(f"norm{i}", a2))
        a2, act, slope, *kept = call(
            functools.partial(up_kernel, masks, n_seq, i),
            "up",
            [steps.gate(f"up{i}", a2_of[i][0])] + a2_of[i][1:] + [ubias] + wup,
            [
                shape((full, width), BF16),
                shape((full, hidden), BF16),
                shape((full, hidden), F32),
            ]
            + ([shape((width, hidden), BF16)] if first else []),
        )
        if first:
            wup = kept
        steps.keep(f"up{i}", act)
        for store, value in zip((a2s, acts, slopes), (a2, act, slope)):
            store.append(value)

    dus, dxs, dattns, sums2, sums_u, downs = [], [], [], [], [], []
    down_sum, up_sum = Scatter(steps, "gdown"), Scatter(steps, "gup")
    made, down_rest = grad_kernels(steps, "gdown", acts, dys)
    down_sum.send(made)
    down_made = down_rest()

    def norm_two_back(i):
        dx2, low, sums = call(
            norm_two_back_kernel,
            "norm_two_back",
            [steps.gate(f"back{i}", downs[i][0])] + downs[i][1:] + [x2s[i], dys[i], vectors],
            [shape((rows, width), F32), shape((rows, width), BF16), shape((8, width), F32)],
        )
        for store, value in zip((dxs, sums2), (dx2, sums)):
            store.append(value)
        return steps.keep(f"back{i}", low)

    out_parts = []
    for i in range(slots):
        first = i == 0
        du, own, rest, high, oown, orest, ohigh, usum, *kept = call(
            functools.partial(down_kernel, masks, i),
            "down",
            [steps.gate(f"down{i}", dys[i]), acts[i], slopes[i]] + wup + wdown,
            [shape((full, hidden), BF16)]
            + outs3
            + outs3
            + [shape((1, hidden), F32)]
            + ([shape((hidden, width), BF16)] if first else []),
        )
        if first:
            wdown = kept
        steps.keep(f"down{i}", du)
        for store, value in zip(
            (dus, sums_u, downs, out_parts), (du, usum, (own, rest, high), (oown, orest, ohigh))
        ):
            store.append(value)
        if i == 0:
            downs[0] = [own] + scatter_seq(steps, "dh2_0", rest, high)
        if i == slots - 1:
            made, up_rest = grad_kernels(steps, "gup", a2s, dus)
            up_sum.send(made)
        if i == 1 or slots == 1:
            dattns.append(gather_seq(steps, "dx_0", norm_two_back(0)))
        if i:
            downs[i] = [own] + scatter_seq(steps, f"dh2_{i}", rest, high)
    g_down = down_sum.finish(down_made)
    up_made = up_rest()
    nears, far = scatter_items(steps, "out", [(rest, high) for _, rest, high in out_parts])
    block_out_in = [own for own, _, _ in out_parts] + nears + far
    for i in range(1, slots):
        dattns.append(gather_seq(steps, f"dx_{i}", norm_two_back(i)))

    g_up = up_sum.finish(up_made)
    dqkvs, sums_q, sums1, back_parts = [], [], [], []
    for i in range(slots):
        dqkv, own, rest, high, qsum, sums = call(
            functools.partial(attention_back_kernel, cols, n_seq),
            "attention_back",
            [steps.gate(f"attb{i}", dattns[i][0])]
            + dattns[i][1:]
            + [qkvs[i], probss[i], hats[i]]
            + wqkv
            + wout,
            [shape((full, 3 * cols), BF16)]
            + outs3
            + [shape((1, 3 * cols), F32), shape((8, width), F32)],
            [
                pltpu.VMEM((full, width), BF16),
                pltpu.VMEM((full, cols), BF16),
                pltpu.VMEM((LANES, full), F32),
                pltpu.VMEM((LANES, full), F32),
            ],
        )
        back_parts.append((own, rest, high))
        steps.keep(f"attb{i}", dqkv)
        for store, value in zip((dqkvs, sums_q, sums1), (dqkv, qsum, sums)):
            store.append(value)
    nears, far = scatter_items(steps, "dh1", [(rest, high) for _, rest, high in back_parts])
    back_in = [own for own, _, _ in back_parts] + nears + far
    qkv_sum, out_sum = Scatter(steps, "gqkv"), Scatter(steps, "gout")
    made, qkv_rest = grad_kernels(steps, "gqkv", a1, dqkvs)
    qkv_sum.send(made)
    pieces = call(
        functools.partial(grad_out_kernel, flat_masks, tile, cols, hpiece, slots, n_seq),
        "grad_out",
        [steps.gate("gout", atts[0])]
        + atts[1:]
        + sum(dattns, [])
        + sums1
        + sums2
        + sums_q
        + sums_u,
        [shape((tile + blocks * piece, width), BF16)] * n_seq,
        [pltpu.VMEM((full, width), BF16), pltpu.VMEM((N_VEC, width), F32)],
    )
    pieces = exchange_seq(pieces)
    steps.keep("gout_seq", pieces[1:])
    made = call(
        functools.partial(grad_out_groups_kernel, flat_masks, tile),
        "grad_out_groups",
        [steps.gate("gout_groups", pieces[0])] + pieces[1:],
        [
            shape((2, VEC_ROWS + piece, width), BF16 if j else F32)
            for j in range(inner)
            for _ in range(2)
        ],
    )
    made = [[made[2 * j], made[2 * j + 1]] for j in range(inner)]
    out_sum.send(made)
    g_qkv = qkv_sum.finish(qkv_rest())
    g_out = out_sum.finish(made)
    g_wdown = total_of(g_down)
    block_out = call(
        functools.partial(block_out_kernel, slots, n_seq),
        "block_out",
        [steps.gate("block_out", block_out_in[0])] + block_out_in[1:] + x2s + [limits, vectors],
        [shape((slots, rows, width), F32)],
        specs=[VMEM] * (len(block_out_in) + slots) + [SMEM, VMEM],
    )[0]
    grad_tokens = call(
        functools.partial(norm_one_back_kernel, slots),
        "norm_one_back",
        [steps.gate("norm_one_back", back_in[0])] + back_in[1:] + dxs + [tokens, vectors],
        [shape((slots, rows, width), F32)],
    )[0]
    g_wout, *vecs = call(
        out_final_kernel,
        "out_final",
        [total_of(g_out)],
        [shape((piece, width), F32)]
        + [shape((1, piece), F32)] * N_VEC
        + [shape((1, hpiece), F32)],
    )

    if regular:
        steps.keep("block_out", block_out)
        steps.keep("norm_one_back", grad_tokens)
        g_qkv = [steps.gate("owners", g_qkv[0])] + list(g_qkv[1:])
        parts = exchange_seq(
            call(
                owners_kernel,
                "owners",
                list(g_qkv) + list(g_up),
                [shape((piece, 3 * cols + hidden), BF16)] * n_seq,
            )
        )
        g_wqkv, g_wup = call(
            functools.partial(unplace_kernel, cols, hpiece),
            "unplace",
            parts,
            [shape((piece, 3 * width), F32), shape((piece, hidden_all), F32)],
        )
    else:
        placed = []
        for parts in (g_qkv, g_up):
            parts = total_of(parts).astype(BF16).reshape(n_seq, piece, -1)
            parts = exchange_seq(
                [lax.dynamic_index_in_dim(parts, s ^ r, 0, False) for r in range(n_seq)]
            )
            out = jnp.zeros((n_seq,) + parts[0].shape, BF16)
            for r, part in enumerate(parts):
                out = lax.dynamic_update_index_in_dim(out, part, s ^ r, 0)
            placed.append(out.astype(F32))
        g_wqkv = placed[0].reshape(n_seq, piece, 3, cols).transpose(1, 2, 0, 3).reshape(piece, -1)
        g_wup = (
            placed[1].reshape(n_seq, piece, n_dp, hpiece).transpose(1, 2, 0, 3).reshape(piece, -1)
        )
    vecs = [v.reshape(-1) for v in vecs]
    return (
        block_out,
        grad_tokens,
        g_wqkv,
        vecs[0],
        vecs[1],
        g_wout,
        vecs[2],
        g_wup,
        vecs[8],
        g_wdown,
        vecs[3],
        vecs[4],
        vecs[5],
        vecs[6],
        vecs[7],
    )


def solution(mesh):
    both = ("dp", "seq")
    act = P("dp", "seq", None)
    mat = P(both, None)
    vec = P(both)
    return jax.shard_map(
        body,
        mesh=mesh,
        in_specs=(act, act, P("dp"), P("dp"), mat, vec, vec, mat, vec, mat, vec, mat)
        + (vec,) * 5,
        out_specs=(act, act, mat, vec, vec, mat, vec, mat, vec, mat) + (vec,) * 5,
        check_vma=False,
    )
```

```python
import functools

import jax
import jax.numpy as jnp
from jax import lax
from jax.experimental import pallas as pl
from jax.experimental.pallas import tpu as pltpu
from jax.sharding import PartitionSpec as P

HEAD_DIM = 64
LANES = 128
EPSILON = 1e-06
F32 = jnp.float32
BF16 = jnp.bfloat16
OUTER = 4
ORDER = (0, 2, 1, 3)
VMEM = pl.BlockSpec(memory_space=pltpu.VMEM)
ANY = pl.BlockSpec(memory_space=pl.ANY)
HBM = pl.BlockSpec(memory_space=pltpu.HBM)
SMEM = pl.BlockSpec(memory_space=pltpu.SMEM)
LIMIT = 14 * 1024 * 1024
WHOLE = 60 * 1024 * 1024
SOFTMAX_RATE = HEAD_DIM**-0.5 * 1.4426950408889634
WAITS = {
    "qkv_z1": ["out_z2"],
    "qkv_xb": ["out_xa"],
    "up_z2": ["out_xb"],
    "up_z1": ["place"],
    "up_xa": ["qkv_z1"],
    "down_z1": ["qkv_z2", "qkv_xa"],
    "down_xb": ["down_xa"],
    "tok_core": ["tok_y", "out_z1"],
    "cot_y": ["out_seq"],
    "att0": ["qkv_xb"],
    "x2_0_core": ["out_seq"],
    "x2_0_y": ["up_xa"],
    "norm0": ["up_z2", "up_z1"],
    "a2_0_y": ["out_seq"],
    "a2_0_core": ["x2_0_y", "norm0", "mask"],
    "x2_1_core": ["tok_core"],
    "x2_1_y": ["tok_core", "cot_core", "att0"],
    "up0": ["norm_one"],
    "up1": ["a2_1_y", "a2_0_y"],
    "gdown_near": ["up1"],
    "gdown_kept": ["norm1", "x2_1_core", "up0"],
    "down0": ["a2_0_core", "gdown_sent"],
    "dh2_0_core": ["down_z1", "mask"],
    "dh2_0_y": ["x2_1_y"],
    "down1": ["cot_y"],
    "gup_sent": ["a2_1_core"],
    "gup_near": ["x2_1_y", "dh2_0_core"],
    "back0": ["up1"],
    "gdown_z1": ["dh2_0_send", "gdown_kept"],
    "gdown_z2": ["back0"],
    "gup_kept": ["dx_0_core", "gup_sent"],
    "out_core1": ["down0"],
    "out_y": ["dh2_1_send", "dh2_1_core", "out_core1"],
    "back1": ["out_core0"],
    "gup_z1": ["dx_1_core", "out_send", "gup_far"],
    "gup_z2": ["dh2_0_y", "dx_1_y"],
    "attb1": ["attb0"],
    "dh1_core0": ["gdown_z1", "attb1"],
    "dh1_core1": ["dh2_1_send"],
    "dh1_y": ["dx_0_core"],
    "gqkv_near": ["gqkv_sent"],
    "gout": ["dh1_core0"],
    "gout_near": ["gout_far"],
    "gqkv_kept": ["gup_z2"],
    "gqkv_z1": ["gup_z2", "gup_z1"],
    "gqkv_z2": ["gqkv_kept"],
    "gout_z1": ["dh1_y"],
    "owners": ["up_xb", "gqkv_z1", "block_out", "gqkv_near", "gout_z1", "gout_near"],
}
N_VEC = 8
VEC_ROWS = 8


def dot(left, right):
    return jnp.dot(left, right, preferred_element_type=F32)


def dot_nt(left, right):
    return lax.dot_general(left, right, (((1,), (1,)), ((), ())), preferred_element_type=F32)


def dot_tn(left, right):
    return lax.dot_general(left, right, (((0,), (0,)), ((), ())), preferred_element_type=F32)


def swap(values, axis, mask):
    size = lax.axis_size(axis)
    return lax.ppermute(values, axis, [(i, i ^ mask) for i in range(size)])


def shape(dims, kind):
    return jax.ShapeDtypeStruct(tuple(dims), kind)


def call(kernel, name, ins, outs, scratch=(), specs=None, limit=LIMIT):
    return pl.pallas_call(
        kernel,
        name=name,
        out_shape=tuple(outs),
        in_specs=specs or [VMEM] * len(ins),
        out_specs=tuple([VMEM] * len(outs)),
        scratch_shapes=list(scratch),
        compiler_params=pltpu.CompilerParams(vmem_limit_bytes=limit),
        cost_estimate=pl.CostEstimate(
            flops=0, bytes_accessed=0, transcendentals=0
        ),
    )(*ins)


def aligned(index, size):
    return pl.multiple_of(index * size, size)


def place_blocks(refs, masks, out):
    own = lax.axis_index("dp")
    for ref, group in zip(refs, masks):
        rows = ref.shape[1]
        for i, mask in enumerate(group):
            out[pl.ds(aligned(own ^ mask, rows), rows), :] = ref[i]


def start_copies(jobs, scratch, sems):
    copies = []
    for src, block, rows in jobs:
        copy = pltpu.make_async_copy(
            src, scratch.at[pl.ds(aligned(block, rows), rows)], sems.at[len(copies)]
        )
        copy.start()
        copies.append(copy)
    return copies


def out_jobs(refs, tile, blocks):
    own = lax.axis_index("seq")
    size = len(refs)
    rows = (refs[0].shape[0] - tile) // blocks
    return [
        (ref.at[pl.ds(tile + b * rows, rows)], b * size + (own ^ r), rows)
        for r, ref in enumerate(refs)
        for b in range(blocks)
    ]


def pack_kernel(cols, hpiece, wqkv, wup, *outs):
    own = lax.axis_index("seq")
    size = len(outs)
    hidden = wup.shape[1] // size
    width = wqkv.shape[1] // 3
    for r, out in enumerate(outs):
        dest = own ^ r
        for i in range(3):
            at = pl.multiple_of(dest * cols + i * width, LANES)
            out[:, i * cols : (i + 1) * cols] = wqkv[:, pl.ds(at, cols)]
        for i in range(hidden // hpiece):
            at = pl.multiple_of((i * size + dest) * hpiece, LANES)
            start = 3 * cols + i * hpiece
            out[:, start : start + hpiece] = wup[:, pl.ds(at, hpiece)]


def place_kernel(*refs):
    size = len(refs) - 2
    qkv, up = refs[size:]
    own = lax.axis_index("seq")
    cut = qkv.shape[2]
    for r in range(size):
        rows = refs[r].shape[0]
        at = pl.ds(aligned(own ^ r, rows), rows)
        qkv[0, at, :] = refs[r][:, :cut]
        up[0, at, :] = refs[r][:, cut:]


def owners_kernel(*refs):
    left, right, outs = refs[:3], refs[3:6], refs[6:]
    own = lax.axis_index("seq")
    rows = outs[0].shape[0]
    cut = left[0].shape[2]
    for r, out in enumerate(outs):
        at = pl.ds(aligned(own ^ r, rows), rows)
        for parts, cols in ((left, slice(0, cut)), (right, slice(cut, out.shape[1]))):
            total = parts[0][0, at, :].astype(F32) + parts[1][0, at, :].astype(F32)
            out[:, cols] = (total + parts[2][0, at, :].astype(F32)).astype(BF16)


def unplace_kernel(cols, hpiece, *refs):
    *parts, qkv, up = refs
    size = len(parts)
    own = lax.axis_index("seq")
    width = qkv.shape[1] // 3
    for r, part in enumerate(parts):
        src = own ^ r
        for i in range(3):
            at = pl.multiple_of(src * cols + i * width, LANES)
            qkv[:, pl.ds(at, cols)] = part[:, i * cols : (i + 1) * cols].astype(F32)
        for i in range((part.shape[1] - 3 * cols) // hpiece):
            at = pl.multiple_of((i * size + src) * hpiece, LANES)
            start = 3 * cols + i * hpiece
            up[:, pl.ds(at, hpiece)] = part[:, start : start + hpiece].astype(F32)


def out_pack_kernel(tile, wout, *refs):
    n = N_VEC + 1
    vecs, out, landed, scratch, sems = refs[:n], refs[n], refs[n + 1 : -2], refs[-2], refs[-1]
    copies = [pltpu.make_async_copy(v, l, sems.at[i]) for i, (v, l) in enumerate(zip(vecs, landed))]
    for copy in copies:
        copy.start()
    out[0, tile:, :] = wout[...]
    scratch[...] = jnp.zeros_like(scratch)
    for copy in copies:
        copy.wait()
    for i, vec in enumerate(landed):
        row, lane = (0, i * LANES) if i < N_VEC else (1, 0)
        scratch[row : row + 1, lane : lane + vec.shape[0]] = vec[...].astype(F32)[None, :]
    out[0, :tile, :] = scratch[...].astype(BF16)


def out_pieces_kernel(masks, tile, blocks, *refs):
    n = len(masks)
    outs, mixed = refs[n:-1], refs[-1]
    d = lax.axis_index("dp")
    s = lax.axis_index("seq")
    flat = [(i, j) for i, group in enumerate(masks) for j in range(len(group))]
    mask_of = [mask for group in masks for mask in group]
    total = None
    for n, (i, j) in enumerate(flat):
        part = refs[i][j, :tile, :].astype(F32)
        part = pltpu.roll(part, 2 * n, 0) if n else part
        total = part if total is None else total + part
    mixed[...] = total.astype(BF16)
    piece = refs[0].shape[1] - tile
    for r, out in enumerate(outs):
        out[:tile, :] = mixed[...]
        for b in range(blocks):
            want = d ^ ((s ^ r) * blocks + b)
            for (i, j), mask in zip(flat, mask_of):

                @pl.when(want == mask)
                def _(out=out, b=b, i=i, j=j):
                    start = tile + b * piece
                    out[start : start + piece, :] = refs[i][j, tile:, :]


def vector_unpack_kernel(masks, tile, n_seq, cols, hpiece, *refs):
    parts, (vectors, qkv_bias, ubias) = refs[:n_seq], refs[n_seq:]
    width = vectors.shape[1]
    hidden = ubias.shape[1]
    mask_of = [mask for group in masks for mask in group]
    piece = width // (n_seq * len(mask_of))
    s = lax.axis_index("seq")
    d = lax.axis_index("dp")
    row = lax.broadcasted_iota(jnp.int32, (tile, 1), 0)
    dist = jnp.zeros_like(row)
    for n, mask in enumerate(mask_of):
        dist = jnp.where(row // 2 == n, mask, dist)
    source = d ^ dist
    lane = lax.broadcasted_iota(jnp.int32, (LANES, width), 1)
    sub = lax.broadcasted_iota(jnp.int32, (LANES, width), 0)
    spread = jnp.where(lane % piece == sub, 1.0, 0.0).astype(BF16)
    target = lax.broadcasted_iota(jnp.int32, (1, width), 1) // piece
    even = row % 2 == 0
    for i in range(N_VEC):
        total = None
        for r, part in enumerate(parts):
            tiled = dot(part[:tile, i * LANES : (i + 1) * LANES], spread)
            here = even & (source * n_seq + (s ^ r) == target)
            tiled = jnp.sum(jnp.where(here, tiled, 0.0), axis=0, keepdims=True)
            total = tiled if total is None else total + tiled
        vectors[i : i + 1, :] = total
    lane = lax.broadcasted_iota(jnp.int32, (LANES, hidden), 1)
    sub = lax.broadcasted_iota(jnp.int32, (LANES, hidden), 0)
    spread = jnp.where(lane % hpiece == sub, 1.0, 0.0).astype(BF16)
    target = lax.broadcasted_iota(jnp.int32, (1, hidden), 1) // hpiece
    tiled = dot(parts[0][:tile, :LANES], spread)
    here = (row % 2 == 1) & (source == target)
    ubias[...] = jnp.sum(jnp.where(here, tiled, 0.0), axis=0, keepdims=True)
    at = pl.ds(pl.multiple_of(s * cols, LANES), cols)
    qkv_bias[...] = jnp.zeros_like(qkv_bias)
    qkv_bias[:, :cols] = vectors[0:1, at]
    qkv_bias[:, 2 * cols :] = vectors[1:2, at]


def positions(block, rows, n_seq, axis):
    half = n_seq // 2
    owner = lax.axis_index("seq") ^ (2 * (block % half) + block // half)
    dims = (rows, 1) if axis == 0 else (1, rows)
    return owner * rows + lax.broadcasted_iota(jnp.int32, dims, axis)


def attention_kernel(masks, tile, blocks, cols, n_seq, item, *refs):
    first = item == 0
    a1, bias, lens = refs[:3]
    n = len(masks) if first else 1
    pieces, outs = refs[3 : 3 + n], refs[3 + n : 3 + n + (n_seq if first else 1)]
    refs = refs[3 + n + len(outs) :]
    if first:
        qkv, att, probs, own, rest, high, wqkv, wout, ok, sems = refs
    else:
        qkv, att, probs, own, rest, high, ok = refs
        (wqkv,), (wout,) = pieces, outs
    rows = a1.shape[0]
    cut = rows // 2
    blk = own.shape[0]
    out_copies = []
    if first:
        out_copies = start_copies(out_jobs(outs, tile, blocks), wout, sems)
        place_blocks(pieces, masks, wqkv)
    for q in range(n_seq):
        good = positions(q, blk, n_seq, 1) < lens[item]
        ok[:, q * blk : (q + 1) * blk] = jnp.where(good, 0.0, -1e30)
    for i in range(3):
        part = slice(i * cols, (i + 1) * cols)
        qkv[:, part] = (dot(a1[...], wqkv[:, part]) + bias[:, part]).astype(BF16)
    step_rows = min(256, rows)
    lane = lax.broadcasted_iota(jnp.int32, (1, LANES), 1)
    sides = [(lane < HEAD_DIM), (lane >= HEAD_DIM)]
    for pair in range(cols // LANES):
        at = slice(pair * LANES, (pair + 1) * LANES)
        keys = qkv[:, cols + pair * LANES : cols + (pair + 1) * LANES]
        vals = qkv[:, 2 * cols + pair * LANES : 2 * cols + (pair + 1) * LANES]
        split = [jnp.where(side, vals, jnp.zeros_like(vals)) for side in sides]

        def step(block, carry, pair=pair, at=at, keys=keys, split=split):
            place = pl.ds(aligned(block, step_rows), step_rows)
            query = qkv[place, at]
            total = None
            for h in range(2):
                q = jnp.where(sides[h], query, jnp.zeros_like(query))
                scores = dot_nt(q, keys) + ok[...]
                peak = jnp.max(scores, axis=-1, keepdims=True)
                expo = jnp.exp2((scores - peak) * SOFTMAX_RATE)
                rate = 1.0 / jnp.sum(expo, axis=-1, keepdims=True)
                low = (expo * rate).astype(BF16)
                probs[2 * pair + h, place, :] = low
                out = dot(low, split[h])
                total = out if total is None else total + out
            att[place, at] = total.astype(BF16)
            return carry

        lax.fori_loop(0, rows // step_rows, step, 0)
    for copy in out_copies:
        copy.wait()
    high[...] = dot(att[cut:, :], wout[...]).astype(BF16)
    own[...] = dot(att[:blk, :], wout[...])
    rest[...] = dot(att[blk:cut, :], wout[...])


def attention_back_kernel(cols, n_seq, *refs):
    parts = refs[:n_seq]
    qkv, probs, hat, wqkv, wout = refs[n_seq : n_seq + 5]
    dqkv, own, rest, high, sums, sums_one, grad, datt, dkt, dvt = refs[n_seq + 5 :]
    rows = dqkv.shape[0]
    cut = rows // 2
    blk = own.shape[0]
    for i, part in enumerate(parts):
        grad[i * blk : (i + 1) * blk, :] = part[...]
    datt[...] = dot_nt(grad[...], wout[...]).astype(BF16)
    step_rows = min(256, rows)
    lane = lax.broadcasted_iota(jnp.int32, (1, LANES), 1)
    sides = [(lane < HEAD_DIM), (lane >= HEAD_DIM)]
    scale = HEAD_DIM**-0.5
    for pair in range(cols // LANES):
        at = slice(pair * LANES, (pair + 1) * LANES)
        at_k = slice(cols + pair * LANES, cols + (pair + 1) * LANES)
        at_v = slice(2 * cols + pair * LANES, 2 * cols + (pair + 1) * LANES)
        keys = qkv[:, at_k]
        vals = qkv[:, at_v]
        split = [jnp.where(side, keys, jnp.zeros_like(keys)) for side in sides]
        dkt[...] = jnp.zeros_like(dkt)
        dvt[...] = jnp.zeros_like(dvt)

        def step(block, carry, pair=pair, at=at, vals=vals, split=split):
            place = pl.ds(aligned(block, step_rows), step_rows)
            gatt = datt[place, at]
            query = qkv[place, at]
            gatt_t = gatt.T
            query_t = query.T
            total = None
            for h in range(2):
                g = jnp.where(sides[h], gatt, jnp.zeros_like(gatt))
                gp = dot_nt(g, vals)
                low = probs[2 * pair + h, place, :]
                p = low.astype(F32)
                mean = jnp.sum(gp * p, axis=-1, keepdims=True)
                gs = (p * (gp - mean)).astype(BF16)
                half = slice(h * HEAD_DIM, (h + 1) * HEAD_DIM)
                dvt[half, :] += dot(gatt_t[half, :], low)
                dkt[half, :] += dot(query_t[half, :], gs)
                out = dot(gs, split[h])
                total = out if total is None else total + out
            dqkv[place, at] = (total * scale).astype(BF16)
            return carry

        lax.fori_loop(0, rows // step_rows, step, 0)
        dqkv[:, at_k] = (dkt[...].T * scale).astype(BF16)
        dqkv[:, at_v] = dvt[...].T.astype(BF16)
    sums[...] = jnp.sum(dqkv[...].astype(F32), axis=0, keepdims=True)
    sums_one[...] = jnp.zeros_like(sums_one)

    def last(block, carry):
        at = pl.ds(aligned(block, 256), 256)
        value = dot_nt(dqkv[...], wqkv[at, :])
        own[:, at] = value[:blk]
        rest[:, at] = value[blk:cut]
        high[:, at] = value[cut:].astype(BF16)
        sums_one[0:1, at] = jnp.sum(value * hat[:, at].astype(F32), axis=0, keepdims=True)
        sums_one[1:2, at] = jnp.sum(value, axis=0, keepdims=True)
        return carry

    lax.fori_loop(0, wqkv.shape[0] // 256, last, 0, unroll=4)


def up_kernel(masks, n_seq, item, *refs):
    first = item == 0
    n = len(masks) if first else 1
    parts, bias = refs[:n_seq], refs[n_seq]
    pieces = refs[n_seq + 1 : n_seq + 1 + n]
    if first:
        a2, act, slope, wup = refs[n_seq + 1 + n :]
        place_blocks(pieces, masks, wup)
    else:
        a2, act, slope = refs[n_seq + 1 + n :]
        (wup,) = pieces
    blk = parts[0].shape[0]
    rows = a2.shape[0]
    width = min(256, act.shape[1])
    for i, part in enumerate(parts):
        a2[i * blk : (i + 1) * blk, :] = part[...]
    half = min(256, rows)
    for i in range(rows // half):
        place = slice(i * half, (i + 1) * half)

        def step(block, carry, place=place):
            at = pl.ds(aligned(block, width), width)
            u = dot(a2[place, :], wup[:, at]) + bias[:, at]
            cdf = 0.5 * (1.0 + lax.erf(u * 0.7071067811865476))
            bell = jnp.exp2(u * u * -0.7213475204444817) * 0.3989422804014327
            act[place, at] = (u * cdf).astype(BF16)
            slope[place, at] = cdf + u * bell
            return carry

        lax.fori_loop(0, act.shape[1] // width, step, 0)


def down_kernel(masks, item, *refs):
    n = len(masks) if item == 0 else 1
    dy, act, slope, wup = refs[:4]
    downs = refs[4 : 4 + n]
    if item == 0:
        du, own, rest, high, oown, orest, ohigh, sums, wdown = refs[4 + n :]
        place_blocks(downs, masks, wdown)
    else:
        du, own, rest, high, oown, orest, ohigh, sums = refs[4 + n :]
        (wdown,) = downs
    rows = dy.shape[0]
    cut = rows // 2
    blk = own.shape[0]
    hidden = act.shape[1]
    width = min(256, hidden)

    def first(block, carry):
        at = pl.ds(aligned(block, width), width)
        value = (slope[:, at] * dot_nt(dy[...], wdown[at, :])).astype(BF16)
        du[:, at] = value
        sums[:, at] = jnp.sum(value.astype(F32), axis=0, keepdims=True)
        return carry

    lax.fori_loop(0, hidden // width, first, 0)

    def second(block, carry):
        at = pl.ds(aligned(block, 256), 256)
        value = dot_nt(du[...], wup[at, :])
        own[:, at] = value[:blk]
        rest[:, at] = value[blk:cut]
        high[:, at] = value[cut:].astype(BF16)
        value = dot(act[...], wdown[:, at])
        oown[:, at] = value[:blk]
        orest[:, at] = value[blk:cut]
        ohigh[:, at] = value[cut:].astype(BF16)
        return carry

    lax.fori_loop(0, wup.shape[0] // 256, second, 0)


def grad_kernel(j, inner, slots, *refs):
    lefts, rights = refs[:slots], refs[slots : 2 * slots]
    *outs, turned = refs[2 * slots :]
    rows = lefts[0].shape[0]
    each, blk = outs[0].shape[:2]
    own = lax.axis_index("dp")
    for n, k in enumerate(ORDER):
        at = pl.ds(aligned(own ^ (k * inner + j), blk), blk)
        for i, left in enumerate(lefts):
            turned[n * blk : (n + 1) * blk, i * rows : (i + 1) * rows] = left[:, at].T
    width = min(256, outs[0].shape[2])

    def step(block, carry):
        at = pl.ds(aligned(block, width), width)
        total = None
        for i, right in enumerate(rights):
            out = dot(turned[:, i * rows : (i + 1) * rows], right[:, at])
            total = out if total is None else total + out
        for n in range(len(ORDER)):
            out = outs[n // each]
            out[n % each, :, at] = total[n * blk : (n + 1) * blk].astype(out.dtype)
        return carry

    lax.fori_loop(0, outs[0].shape[2] // width, step, 0, unroll=True)


def grad_out_kernel(masks, tile, cols, hpiece, slots, n_seq, *refs):
    take = lambda n: (refs[:n], refs[n:])
    lefts, refs = take(slots)
    rights, refs = take(slots * n_seq)
    sums1, refs = take(slots)
    sums2, refs = take(slots)
    sums_q, refs = take(slots)
    sums_u, refs = take(slots)
    outs, (scratch, wide) = take(n_seq)[0], refs[n_seq:]
    width = wide.shape[1]
    s = lax.axis_index("seq")
    d = lax.axis_index("dp")
    total = lambda refs: functools.reduce(lambda a, b: a + b, [ref[...] for ref in refs])
    q, u = total(sums_q), total(sums_u)
    one, two = total(sums1), total(sums2)
    wide[...] = jnp.zeros_like(wide)
    at = pl.ds(pl.multiple_of(s * cols, LANES), cols)
    wide[0:1, at] = q[:, :cols]
    wide[1:2, at] = q[:, 2 * cols :]
    wide[2:4, :] = two[:2]
    wide[4:6, :] = one[:2]
    wide[6:8, :] = two[2:4]
    piece = width // (n_seq * len(masks))
    row = lax.broadcasted_iota(jnp.int32, (n_seq * tile, 1), 0)
    near = row % tile
    dist = jnp.zeros_like(row)
    for n, mask in enumerate(masks):
        dist = jnp.where(near // 2 == n, mask, dist)
    dest = (d ^ dist) * n_seq + (s ^ (row // tile))
    dest = jnp.where(near % 2 == 0, dest, -1)
    spread = jnp.where(
        lax.broadcasted_iota(jnp.int32, (width, LANES), 0) % piece
        == lax.broadcasted_iota(jnp.int32, (width, LANES), 1),
        1.0,
        0.0,
    ).astype(BF16)
    here = lax.broadcasted_iota(jnp.int32, (1, width), 1) // piece == dest
    vecs = []
    for i in range(N_VEC):
        vecs.append(dot(jnp.where(here, wide[i : i + 1, :], 0.0).astype(BF16), spread))
    hidden = u.shape[1]
    spread = jnp.where(
        lax.broadcasted_iota(jnp.int32, (hidden, LANES), 0) % hpiece
        == lax.broadcasted_iota(jnp.int32, (hidden, LANES), 1),
        1.0,
        0.0,
    ).astype(BF16)
    dest = jnp.where(near % 2 == 1, d ^ dist, -1)[:tile]
    here = lax.broadcasted_iota(jnp.int32, (1, hidden), 1) // hpiece == dest
    long = dot(jnp.where(here, u, 0.0).astype(BF16), spread)
    for r, out in enumerate(outs):
        for i, vec in enumerate(vecs):
            value = vec[r * tile : (r + 1) * tile]
            if r == 0 and i == 0:
                value = value + long
            out[:tile, i * LANES : (i + 1) * LANES] = value.astype(BF16)
    rows = rights[0].shape[0]
    blocks = (outs[0].shape[0] - tile) // piece
    grad = None
    for i, left in enumerate(lefts):
        for q in range(n_seq):
            scratch[q * rows : (q + 1) * rows, :] = rights[i * n_seq + q][...]
        part = dot_tn(left[...], scratch[...])
        grad = part if grad is None else grad + part
    grad = grad.astype(BF16)
    for other in range(n_seq):
        for r in range(n_seq):

            @pl.when(s ^ r == other)
            def _(other=other, r=r):
                for b in range(blocks):
                    at = (b * n_seq + other) * piece
                    start = tile + b * piece
                    outs[r][start : start + piece, :] = grad[at : at + piece]


def grad_out_groups_kernel(masks, tile, *refs):
    n_out = len(masks) // 2
    pieces, outs = refs[:-n_out], refs[-n_out:]
    size = len(pieces)
    head = VEC_ROWS
    rows = outs[0].shape[1] - head
    blocks = (pieces[0].shape[0] - tile) // rows
    d = lax.axis_index("dp")
    s = lax.axis_index("seq")
    total = None
    for piece in pieces:
        part = piece[:tile, :].astype(F32)
        total = part if total is None else total + part
    row = lax.broadcasted_iota(jnp.int32, (tile, 1), 0)
    for n, mask in enumerate(masks):
        out, i = outs[n // 2], n % 2
        value = pltpu.roll(total, tile - 2 * n, 0) if n else total
        out[i, :head, :] = jnp.where(row < 2, value, 0.0)[:head].astype(out.dtype)
        for r in range(size):
            for b in range(blocks):

                @pl.when(d ^ mask == (s ^ r) * blocks + b)
                def _(out=out, i=i, r=r, b=b):
                    start = tile + b * rows
                    out[i, head:, :] = pieces[r][start : start + rows, :].astype(out.dtype)


def out_final_kernel(total, grad, *vecs):
    grad[...] = total[VEC_ROWS:, :]
    for i, vec in enumerate(vecs[:-1]):
        vec[...] = total[0:1, i * LANES : i * LANES + vec.shape[1]]
    vecs[-1][...] = total[1:2, : vecs[-1].shape[1]]


def items_kernel(*refs):
    slots, blk = refs[-1].shape[:2]
    rests, nears, outs = refs[:slots], refs[slots : 2 * slots], refs[2 * slots :]
    for i in range(slots):
        for j, out in enumerate(outs):
            near = nears[i][(j + 1) * blk : (j + 2) * blk, :].astype(F32)
            out[i] = (rests[i][j * blk : (j + 1) * blk, :] + near).astype(BF16)


def item_sum(item, own, near, far, blk):
    total = own[...] + near[:blk, :].astype(F32)
    for ref in far:
        total = total + ref[item].astype(F32)
    return total


def gathered_sum(own, near, far, blk):
    total = own[...] + near[:blk, :].astype(F32)
    for ref in far:
        total = total + ref[...].astype(F32)
    return total


def stats(values):
    center = values - jnp.mean(values, axis=-1, keepdims=True)
    rate = lax.rsqrt(jnp.mean(center * center, axis=-1, keepdims=True) + EPSILON)
    return center * rate, rate


def norm_kernel(n_seq, *refs):
    parts, vectors, outs = refs[:n_seq], refs[n_seq], refs[n_seq + 1 :]
    rows = parts[0].shape[1]
    outs, hats = outs[: len(outs) // 2], outs[len(outs) // 2 :]
    for i, (out, kept) in enumerate(zip(outs, hats)):
        for q, part in enumerate(parts):
            hat, _ = stats(part[i].astype(F32))
            kept[q * rows : (q + 1) * rows, :] = hat.astype(BF16)
            out[q * rows : (q + 1) * rows, :] = (
                hat * vectors[4:5, :] + vectors[5:6, :]
            ).astype(BF16)


def mask_kernel(n_seq, *refs):
    parts, limits, outs = refs[:n_seq], refs[n_seq], refs[n_seq + 1 :]
    rows = parts[0].shape[1]
    for i, out in enumerate(outs):
        for q, part in enumerate(parts):
            good = jnp.where(positions(q, rows, n_seq, 0) < limits[i], 1.0, 0.0)
            out[q * rows : (q + 1) * rows, :] = (part[i].astype(F32) * good).astype(BF16)


def norm_two_kernel(item, own, near, *refs):
    *far, x, vectors, x2, a2 = refs
    value = x[item].astype(F32) + (
        gathered_sum(own, near, far, x2.shape[0]) + vectors[2:3, :]
    )
    x2[...] = value
    hat, _ = stats(value)
    a2[...] = (hat * vectors[6:7, :] + vectors[7:8, :]).astype(BF16)


def norm_back(grad, gain, hat, rate):
    scaled = grad * gain
    return rate * (
        scaled
        - jnp.mean(scaled, axis=-1, keepdims=True)
        - hat * jnp.mean(scaled * hat, axis=-1, keepdims=True)
    )


def norm_two_back_kernel(own, near, *refs):
    *far, x2, dy, vectors, dx2, low, sums = refs
    grad = gathered_sum(own, near, far, x2.shape[0])
    hat, rate = stats(x2[...])
    rows = dy[: x2.shape[0], :].astype(F32)
    value = rows + norm_back(grad, vectors[6:7, :], hat, rate)
    dx2[...] = value
    rounded = value.astype(BF16)
    low[...] = rounded
    sums[0:1, :] = jnp.sum(rounded.astype(F32), axis=0, keepdims=True)
    sums[1:2, :] = jnp.sum(rows, axis=0, keepdims=True)
    sums[2:3, :] = jnp.sum(grad * hat, axis=0, keepdims=True)
    sums[3:4, :] = jnp.sum(grad, axis=0, keepdims=True)
    sums[4:8, :] = jnp.zeros_like(sums[4:8, :])


def norm_one_back_kernel(slots, *refs):
    owns, nears, refs = refs[:slots], refs[slots : 2 * slots], refs[2 * slots :]
    *far, x, vectors, out = refs
    far, dxs = far[:-slots], far[-slots:]
    for i in range(slots):
        grad = item_sum(i, owns[i], nears[i], far, x.shape[1])
        hat, rate = stats(x[i].astype(F32))
        out[i] = dxs[i][...] + norm_back(grad, vectors[4:5, :], hat, rate)


def block_out_kernel(slots, n_seq, *refs):
    owns, nears, refs = refs[:slots], refs[slots : 2 * slots], refs[2 * slots :]
    *far, limits, vectors, out = refs
    far, x2s = far[:-slots], far[-slots:]
    for i, x2 in enumerate(x2s):
        blk = x2.shape[0]
        value = x2[...] + item_sum(i, owns[i], nears[i], far, blk) + vectors[3:4, :]
        good = jnp.where(positions(0, blk, n_seq, 0) < limits[i], 1.0, 0.0)
        out[i] = value * good


def exchange_seq(pieces):
    return [swap(piece, "seq", r) if r else piece for r, piece in enumerate(pieces)]


def gather_masks():
    inner = lax.axis_size("dp") // OUTER
    return [
        tuple(k * inner ^ j for k in pair) for pair in (ORDER[:2], ORDER[2:]) for j in range(inner)
    ]


def total_of(parts):
    return functools.reduce(lambda a, b: a + b, [part[0].astype(F32) for part in parts])


class Steps:
    def __init__(self):
        self.known = {}

    def keep(self, name, value):
        self.known[name] = value
        return value

    def send(self, name, value, axis, mask):
        return self.keep(name, swap(value, axis, mask))

    def gate(self, name, value):
        others = [self.known[key] for key in WAITS.get(name, ()) if key in self.known]
        return lax.optimization_barrier((value, others))[0] if others else value


def inner_masks():
    inner = lax.axis_size("dp") // OUTER
    out, bit = [], 1
    while bit < inner:
        out.append(bit)
        bit *= 2
    return out


def gather_dp(steps, name, block):
    inner = lax.axis_size("dp") // OUTER
    far = steps.send(name + "_z2", steps.gate(name + "_z2", block), "dp", 2 * inner)
    pair = jnp.concatenate([block, far], 0)
    other = steps.send(name + "_z1", steps.gate(name + "_z1", pair), "dp", inner)
    out = []
    for part, key in ((pair, name + "_xa"), (other, name + "_xb")):
        group = [part]
        for bit in inner_masks():
            group += [swap(steps.gate(key, p), "dp", bit) for p in group]
        steps.keep(key, group[1:])
        out += group
    return out


def scatter_first(steps, name, made, part):
    pairs = [group[part] for group in made[1:2] if len(made) == 2]
    steps.keep(name, [swap(steps.gate(name, pair), "dp", 1) for pair in pairs])
    return steps.known[name]


def inner_sum(parts, early):
    parts = [parts[0].astype(F32)] + list(parts[1:])
    for bit in inner_masks():
        for j in range(0, len(parts), 2 * bit):
            if len(parts) == 2:
                got = early[0]
            else:
                got = swap(parts[j + bit].astype(BF16), "dp", bit)
            parts[j] = parts[j].astype(F32) + got.astype(F32)
    return parts[0]


class Scatter:
    def __init__(self, steps, name):
        self.steps, self.name = steps, name

    def send(self, made):
        self.far = scatter_first(self.steps, self.name + "_far", made, 1)
        self.near = scatter_first(self.steps, self.name + "_near", made, 0)

    def finish(self, groups):
        steps, name = self.steps, self.name
        inner = len(groups)
        far = inner_sum([group[1] for group in groups], self.far).astype(BF16)
        got = steps.send(name + "_z1", steps.gate(name + "_z1", far), "dp", inner)
        near = inner_sum([group[0] for group in groups], self.near)
        send = (near[1:] + got[1:].astype(F32)).astype(BF16)
        tail = steps.send(name + "_z2", steps.gate(name + "_z2", send), "dp", 2 * inner)
        return near, got, tail


def scatter_seq(steps, name, rest, high):
    half = lax.axis_size("seq") // 2
    near = steps.send(name + "_core", steps.gate(name + "_core", high), "seq", 1)
    blk = near.shape[0] // half
    send = (rest + near[blk:].astype(F32)).astype(BF16)
    send = steps.gate(name + "_y", steps.keep(name + "_send", send))
    far = [swap(send[(j - 1) * blk : j * blk], "seq", 2 * j) for j in range(1, half)]
    return [near] + steps.keep(name + "_y", far)


def scatter_items(steps, name, parts):
    half = lax.axis_size("seq") // 2
    slots = len(parts)
    nears = [
        steps.send(f"{name}_core{i}", steps.gate(f"{name}_core{i}", high), "seq", 1)
        for i, (_, high) in enumerate(parts)
    ]
    rests = [rest for rest, _ in parts]
    blk = nears[0].shape[0] // half
    width = nears[0].shape[1]
    sends = call(
        items_kernel,
        "items",
        rests + nears,
        [shape((slots, blk, width), BF16)] * (half - 1),
    )
    sends = steps.gate(name + "_y", steps.keep(name + "_send", list(sends)))
    far = [swap(send, "seq", 2 * (j + 1)) for j, send in enumerate(sends)]
    steps.keep(name + "_y", far)
    return nears, far


def gather_seq(steps, name, block):
    half = lax.axis_size("seq") // 2
    block = steps.gate(name + "_y", block)
    far = steps.keep(name + "_y", [swap(block, "seq", 2 * j) for j in range(1, half)])
    mine = [block] + far
    other = [swap(block, "seq", 1)]
    other += [swap(steps.gate(name + "_core", part), "seq", 1) for part in far]
    steps.keep(name + "_core", other)
    return mine + other


def grad_kernels(steps, name, lefts, rights):
    lefts, rights = list(lefts), list(rights)
    inner = lax.axis_size("dp") // OUTER
    slots = len(lefts)
    blk = lefts[0].shape[1] // (OUTER * inner)
    width = rights[0].shape[1]
    rows = lefts[0].shape[0]
    if blk % LANES:
        own = lax.axis_index("dp")
        whole = sum(dot_tn(a, b) for a, b in zip(lefts, rights)).reshape(-1, blk, width)
        take = lambda k: lax.dynamic_index_in_dim(whole, own ^ k, 0)
        made = []
        for j in range(inner):
            got = [take(k * inner + j) for k in ORDER]
            made.append([jnp.concatenate(got[:2], 0), jnp.concatenate(got[2:], 0)])
        return made, lambda: made
    made = [None] * inner

    def make(j):
        key = name + ("_sent" if j else "_kept")
        made[j] = steps.keep(
            key,
            list(
                call(
                    functools.partial(grad_kernel, j, inner, slots),
                    key,
                    [steps.gate(key, lefts[0])] + lefts[1:] + rights,
                    [shape((2, blk, width), BF16 if j else F32)] * 2,
                    [pltpu.VMEM((4 * blk, slots * rows), BF16)],
                )
            ),
        )

    def rest():
        make(0)
        return made

    for j in range(1, inner):
        make(j)
    return made, rest


def body(
    tokens,
    cotangent,
    item_count,
    valid_len,
    w_qkv,
    q_bias,
    v_bias,
    w_out,
    out_bias,
    w_up,
    up_bias,
    w_down,
    down_bias,
    gain_one,
    shift_one,
    gain_two,
    shift_two,
):
    slots, rows, width = tokens.shape
    n_seq = lax.axis_size("seq")
    n_dp = lax.axis_size("dp")
    inner = n_dp // OUTER
    count = n_seq * n_dp
    half = n_seq // 2
    cut = half * rows
    full = n_seq * rows
    cols = width // n_seq
    heads = cols // HEAD_DIM
    piece = width // count
    hidden_all = w_up.shape[1]
    hidden = hidden_all // n_seq
    hpiece = hidden_all // count
    blocks = n_dp // n_seq
    regular = hpiece % LANES == 0 and piece % 16 == 0

    limits = jnp.where(jnp.arange(slots) < item_count[0], valid_len, 0)
    dma = lambda n: pltpu.SemaphoreType.DMA((n,))

    rows_in = [
        q_bias,
        v_bias,
        out_bias,
        down_bias,
        gain_one,
        shift_one,
        gain_two,
        shift_two,
        up_bias,
    ]
    tile = max(16, 2 * n_dp)
    masks = gather_masks()
    n_parts = len(masks)
    flat_masks = [k * inner + j for j in range(inner) for k in ORDER]
    steps = Steps()
    out_block = call(
        functools.partial(out_pack_kernel, tile),
        "out_pack",
        [w_out] + rows_in,
        [shape((1, tile + piece, width), BF16)],
        [pltpu.VMEM(v.shape, BF16) for v in rows_in]
        + [pltpu.VMEM((tile, width), F32), dma(N_VEC + 1)],
        [VMEM] + [HBM] * (N_VEC + 1),
        WHOLE,
    )[0]
    if regular:
        packed = call(
            functools.partial(pack_kernel, cols, hpiece),
            "pack",
            [w_qkv, w_up],
            [shape((piece, 3 * cols + hidden), BF16)] * n_seq,
            limit=WHOLE,
        )
        own_qkv, own_up = call(
            place_kernel,
            "place",
            exchange_seq(packed),
            [
                shape((1, n_seq * piece, 3 * cols), BF16),
                shape((1, n_seq * piece, hidden), BF16),
            ],
        )
    else:
        s = lax.axis_index("seq")
        split = jnp.concatenate(
            [
                w_qkv.reshape(piece, 3, n_seq, cols).transpose(2, 0, 1, 3).reshape(n_seq, piece, -1),
                w_up.reshape(piece, n_dp, n_seq, hpiece)
                .transpose(2, 0, 1, 3)
                .reshape(n_seq, piece, -1),
            ],
            -1,
        )
        packed = [lax.dynamic_index_in_dim(split, s ^ r, 0, False) for r in range(n_seq)]
        placed = jnp.zeros_like(split)
        for r, part in enumerate(exchange_seq(packed)):
            placed = lax.dynamic_update_index_in_dim(placed, part, s ^ r, 0)
        placed = placed.reshape(1, n_seq * piece, -1)
        own_qkv, own_up = placed[:, :, : 3 * cols], placed[:, :, 3 * cols :]

    steps.keep("place", [own_qkv, own_up])
    out_all = gather_dp(steps, "out", out_block)
    wqkv = gather_dp(steps, "qkv", own_qkv)
    wup = gather_dp(steps, "up", own_up)
    wdown = gather_dp(steps, "down", w_down[None])
    wout = exchange_seq(
        call(
            functools.partial(out_pieces_kernel, masks, tile, blocks),
            "out_pieces",
            [steps.gate("out_pieces", out_all[0])] + out_all[1:],
            [shape((tile + blocks * piece, width), BF16)] * n_seq,
            [pltpu.VMEM((tile, width), BF16)],
        )
    )
    steps.keep("out_seq", wout[1:])
    tok = gather_seq(steps, "tok", tokens)
    cot = gather_seq(steps, "cot", cotangent)
    vectors, qkv_bias, ubias = call(
        functools.partial(vector_unpack_kernel, masks, tile, n_seq, cols, hpiece),
        "vector_unpack",
        [steps.gate("vectors", wout[0])] + wout[1:],
        [shape((N_VEC, width), F32), shape((1, 3 * cols), F32), shape((1, hidden), F32)],
    )
    a1 = call(
        functools.partial(norm_kernel, n_seq),
        "norm_one",
        [steps.gate("norm_one", tok[0])] + tok[1:] + [vectors],
        [shape((full, width), BF16)] * (2 * slots),
    )
    a1, hats = list(a1[:slots]), list(a1[slots:])
    steps.keep("norm_one", a1)
    dys = call(
        functools.partial(mask_kernel, n_seq),
        "mask",
        [steps.gate("mask", cot[0])] + cot[1:] + [limits],
        [shape((full, width), BF16)] * slots,
        specs=[VMEM] * n_seq + [SMEM],
    )
    steps.keep("mask", dys)

    outs3 = [shape((rows, width), F32), shape((cut - rows, width), F32), shape((cut, width), BF16)]
    qkvs, atts, probss, x2s, a2s, acts, slopes, a2_of = [], [], [], [], [], [], [], []
    for i in range(slots):
        first = i == 0
        qkv, att, probs, own, rest, high, *kept = call(
            functools.partial(attention_kernel, masks, tile, blocks, cols, n_seq, i),
            "attention",
            [steps.gate(f"att{i}", a1[i]), qkv_bias, valid_len] + wqkv + wout,
            [
                shape((full, 3 * cols), BF16),
                shape((full, cols), BF16),
                shape((heads, full, full), BF16),
            ]
            + outs3
            + ([shape((width, 3 * cols), BF16), shape((cols, width), BF16)] if first else []),
            [pltpu.VMEM((1, full), F32)] + ([dma(n_dp)] if first else []),
            [VMEM] * 2 + [SMEM] + ([VMEM] * n_parts + [ANY] * n_seq if first else [VMEM] * 2),
        )
        if first:
            wqkv, wout = [kept[0]], [kept[1]]
        steps.keep(f"att{i}", att)
        for store, value in zip((qkvs, atts, probss, a2_of), (qkv, att, probs, (own, rest, high))):
            store.append(value)
        if i == 0:
            a2_of[0] = [own] + scatter_seq(steps, "x2_0", rest, high)
        if i == 1 or slots == 1:
            norm_two_of = lambda i: call(
                functools.partial(norm_two_kernel, i),
                "norm_two",
                [steps.gate(f"norm{i}", a2_of[i][0])] + a2_of[i][1:] + [tokens, vectors],
                [shape((rows, width), F32), shape((rows, width), BF16)],
            )
            x2, a2 = norm_two_of(0)
            x2s.append(x2)
            a2_of[0] = gather_seq(steps, "a2_0", steps.keep("norm0", a2))
        if i:
            own, rest, high = a2_of[i]
            a2_of[i] = [own] + scatter_seq(steps, f"x2_{i}", rest, high)

    for i in range(slots):
        first = i == 0
        if i:
            x2, a2 = norm_two_of(i)
            x2s.append(x2)
            a2_of[i] = gather_seq(steps, f"a2_{i}", steps.keep(f"norm{i}", a2))
        a2, act, slope, *kept = call(
            functools.partial(up_kernel, masks, n_seq, i),
            "up",
            [steps.gate(f"up{i}", a2_of[i][0])] + a2_of[i][1:] + [ubias] + wup,
            [
                shape((full, width), BF16),
                shape((full, hidden), BF16),
                shape((full, hidden), F32),
            ]
            + ([shape((width, hidden), BF16)] if first else []),
        )
        if first:
            wup = kept
        steps.keep(f"up{i}", act)
        for store, value in zip((a2s, acts, slopes), (a2, act, slope)):
            store.append(value)

    dus, dxs, dattns, sums2, sums_u, downs = [], [], [], [], [], []
    down_sum, up_sum = Scatter(steps, "gdown"), Scatter(steps, "gup")
    made, down_rest = grad_kernels(steps, "gdown", acts, dys)
    down_sum.send(made)
    down_made = down_rest()

    def norm_two_back(i):
        dx2, low, sums = call(
            norm_two_back_kernel,
            "norm_two_back",
            [steps.gate(f"back{i}", downs[i][0])] + downs[i][1:] + [x2s[i], dys[i], vectors],
            [shape((rows, width), F32), shape((rows, width), BF16), shape((8, width), F32)],
        )
        for store, value in zip((dxs, sums2), (dx2, sums)):
            store.append(value)
        return steps.keep(f"back{i}", low)

    out_parts = []
    for i in range(slots):
        first = i == 0
        du, own, rest, high, oown, orest, ohigh, usum, *kept = call(
            functools.partial(down_kernel, masks, i),
            "down",
            [steps.gate(f"down{i}", dys[i]), acts[i], slopes[i]] + wup + wdown,
            [shape((full, hidden), BF16)]
            + outs3
            + outs3
            + [shape((1, hidden), F32)]
            + ([shape((hidden, width), BF16)] if first else []),
        )
        if first:
            wdown = kept
        steps.keep(f"down{i}", du)
        for store, value in zip(
            (dus, sums_u, downs, out_parts), (du, usum, (own, rest, high), (oown, orest, ohigh))
        ):
            store.append(value)
        if i == 0:
            downs[0] = [own] + scatter_seq(steps, "dh2_0", rest, high)
        if i == slots - 1:
            made, up_rest = grad_kernels(steps, "gup", a2s, dus)
            up_sum.send(made)
        if i == 1 or slots == 1:
            dattns.append(gather_seq(steps, "dx_0", norm_two_back(0)))
        if i:
            downs[i] = [own] + scatter_seq(steps, f"dh2_{i}", rest, high)
    g_down = down_sum.finish(down_made)
    up_made = up_rest()
    nears, far = scatter_items(steps, "out", [(rest, high) for _, rest, high in out_parts])
    block_out_in = [own for own, _, _ in out_parts] + nears + far
    for i in range(1, slots):
        dattns.append(gather_seq(steps, f"dx_{i}", norm_two_back(i)))

    g_up = up_sum.finish(up_made)
    dqkvs, sums_q, sums1, back_parts = [], [], [], []
    for i in range(slots):
        dqkv, own, rest, high, qsum, sums = call(
            functools.partial(attention_back_kernel, cols, n_seq),
            "attention_back",
            [steps.gate(f"attb{i}", dattns[i][0])]
            + dattns[i][1:]
            + [qkvs[i], probss[i], hats[i]]
            + wqkv
            + wout,
            [shape((full, 3 * cols), BF16)]
            + outs3
            + [shape((1, 3 * cols), F32), shape((8, width), F32)],
            [
                pltpu.VMEM((full, width), BF16),
                pltpu.VMEM((full, cols), BF16),
                pltpu.VMEM((LANES, full), F32),
                pltpu.VMEM((LANES, full), F32),
            ],
        )
        back_parts.append((own, rest, high))
        steps.keep(f"attb{i}", dqkv)
        for store, value in zip((dqkvs, sums_q, sums1), (dqkv, qsum, sums)):
            store.append(value)
    nears, far = scatter_items(steps, "dh1", [(rest, high) for _, rest, high in back_parts])
    back_in = [own for own, _, _ in back_parts] + nears + far
    qkv_sum, out_sum = Scatter(steps, "gqkv"), Scatter(steps, "gout")
    made, qkv_rest = grad_kernels(steps, "gqkv", a1, dqkvs)
    qkv_sum.send(made)
    pieces = call(
        functools.partial(grad_out_kernel, flat_masks, tile, cols, hpiece, slots, n_seq),
        "grad_out",
        [steps.gate("gout", atts[0])]
        + atts[1:]
        + sum(dattns, [])
        + sums1
        + sums2
        + sums_q
        + sums_u,
        [shape((tile + blocks * piece, width), BF16)] * n_seq,
        [pltpu.VMEM((full, width), BF16), pltpu.VMEM((N_VEC, width), F32)],
    )
    pieces = exchange_seq(pieces)
    steps.keep("gout_seq", pieces[1:])
    made = call(
        functools.partial(grad_out_groups_kernel, flat_masks, tile),
        "grad_out_groups",
        [steps.gate("gout_groups", pieces[0])] + pieces[1:],
        [
            shape((2, VEC_ROWS + piece, width), BF16 if j else F32)
            for j in range(inner)
            for _ in range(2)
        ],
    )
    made = [[made[2 * j], made[2 * j + 1]] for j in range(inner)]
    out_sum.send(made)
    g_qkv = qkv_sum.finish(qkv_rest())
    g_out = out_sum.finish(made)
    g_wdown = total_of(g_down)
    block_out = call(
        functools.partial(block_out_kernel, slots, n_seq),
        "block_out",
        [steps.gate("block_out", block_out_in[0])] + block_out_in[1:] + x2s + [limits, vectors],
        [shape((slots, rows, width), F32)],
        specs=[VMEM] * (len(block_out_in) + slots) + [SMEM, VMEM],
    )[0]
    grad_tokens = call(
        functools.partial(norm_one_back_kernel, slots),
        "norm_one_back",
        [steps.gate("norm_one_back", back_in[0])] + back_in[1:] + dxs + [tokens, vectors],
        [shape((slots, rows, width), F32)],
    )[0]
    g_wout, *vecs = call(
        out_final_kernel,
        "out_final",
        [total_of(g_out)],
        [shape((piece, width), F32)]
        + [shape((1, piece), F32)] * N_VEC
        + [shape((1, hpiece), F32)],
    )

    if regular:
        steps.keep("block_out", block_out)
        steps.keep("norm_one_back", grad_tokens)
        g_qkv = [steps.gate("owners", g_qkv[0])] + list(g_qkv[1:])
        parts = exchange_seq(
            call(
                owners_kernel,
                "owners",
                list(g_qkv) + list(g_up),
                [shape((piece, 3 * cols + hidden), BF16)] * n_seq,
            )
        )
        g_wqkv, g_wup = call(
            functools.partial(unplace_kernel, cols, hpiece),
            "unplace",
            parts,
            [shape((piece, 3 * width), F32), shape((piece, hidden_all), F32)],
        )
    else:
        placed = []
        for parts in (g_qkv, g_up):
            parts = total_of(parts).astype(BF16).reshape(n_seq, piece, -1)
            parts = exchange_seq(
                [lax.dynamic_index_in_dim(parts, s ^ r, 0, False) for r in range(n_seq)]
            )
            out = jnp.zeros((n_seq,) + parts[0].shape, BF16)
            for r, part in enumerate(parts):
                out = lax.dynamic_update_index_in_dim(out, part, s ^ r, 0)
            placed.append(out.astype(F32))
        g_wqkv = placed[0].reshape(n_seq, piece, 3, cols).transpose(1, 2, 0, 3).reshape(piece, -1)
        g_wup = (
            placed[1].reshape(n_seq, piece, n_dp, hpiece).transpose(1, 2, 0, 3).reshape(piece, -1)
        )
    vecs = [v.reshape(-1) for v in vecs]
    return (
        block_out,
        grad_tokens,
        g_wqkv,
        vecs[0],
        vecs[1],
        g_wout,
        vecs[2],
        g_wup,
        vecs[8],
        g_wdown,
        vecs[3],
        vecs[4],
        vecs[5],
        vecs[6],
        vecs[7],
    )


def solution(mesh):
    both = ("dp", "seq")
    act = P("dp", "seq", None)
    mat = P(both, None)
    vec = P(both)
    return jax.shard_map(
        body,
        mesh=mesh,
        in_specs=(act, act, P("dp"), P("dp"), mat, vec, vec, mat, vec, mat, vec, mat)
        + (vec,) * 5,
        out_specs=(act, act, mat, vec, vec, mat, vec, mat, vec, mat) + (vec,) * 5,
        check_vma=False,
    )
```
